32 devices in a mesh: grp: 2 (over y), tm: 4 (over z), tmpl: 4 (over x, core).
Axes of the slice: x: 2, y: 2, z: 4, core: 2. Of those that a mesh axis runs over, the one named last changes fastest.
Arguments:
- records: bfloat16 [160, 3072], P(None, ('grp', 'tm')), parts along dimension 1, may hold values from -600 to 600
- templates: bfloat16 [160, 4, 4, 200], P(None, 'tm', 'tmpl'), may hold values from -60 to 60
- channel_mask: int32 [160, 4, 4], P(None, 'tm', 'tmpl'), may hold values 0 or 1
- lag_table: int32 [160, 4, 4], P(None, 'tm', 'tmpl'), may hold values from 0 to 63
Outputs:
- stacked: float32 [4, 4, 3072], P(None, 'tmpl', ('grp', 'tm')), parts along dimension 2
The draws below stay inside these ranges and needn't reach their ends.
There are 2 independent parts, one for each index of `grp`. The reference program is written for one: setup_inputs(seed, part) draws one part's arguments, and reference() takes and returns one part's arrays. A program takes and returns all parts, laid end to end along the dimension named above; an argument that names none is the same for every part. Nothing has to cross between parts.
All inputs are finite; a program needn't handle non-finite values. No bound on the sum of `channel_mask` on one device may be relied on, other than what follows from the above.
Results may differ from the reference program's by a relative error of at most 0.0003.
Values may be sent and summed in bfloat16 or wider, within the bound.
A program may use at most 192 MiB of HBM per device.

```python
import math
import jax
import jax.numpy as jnp
from jax import lax

C = 160
L = 200
LAGS = 64
NT = 1536
KA = 4
KB = 4


def draw_records(key, part):
    key_base, key_chan, key_seg = jax.random.split(key, 3)
    base_noise = jnp.clip(jax.random.normal(key_base, (C, NT), jnp.float32), -6.0, 6.0)
    log_reach = math.log(10.0)
    channel_gain = jnp.exp(jax.random.uniform(key_chan, (C, 1), jnp.float32, 0.0, log_reach))
    segment_gain = jnp.exp(jax.random.uniform(key_seg, (C, NT // 32, 1), jnp.float32, 0.0, log_reach))
    values = (base_noise.reshape(C, NT // 32, 32) * segment_gain).reshape(C, NT) * channel_gain
    return values.astype(jnp.bfloat16)


def draw_templates(key, part):
    key_base, key_gain = jax.random.split(jax.random.fold_in(key, 7), 2)
    base_noise = jnp.clip(jax.random.normal(key_base, (C, KA, KB, L), jnp.float32), -6.0, 6.0)
    log_reach = math.log(10.0)
    channel_gain = jnp.exp(jax.random.uniform(key_gain, (C, KA, KB, 1), jnp.float32, 0.0, log_reach))
    return (base_noise * channel_gain).astype(jnp.bfloat16)


def place_ends(values, rng, low, largest):
    dims = values.shape
    spot = [jax.random.randint(jax.random.fold_in(rng, axis), (), 0, dims[axis]) for axis in range(len(dims))]
    values = values.at[tuple(spot)].set(low)
    longest = dims.index(max(dims))
    spot[longest] = (spot[longest] + 1) % dims[longest]
    return values.at[tuple(spot)].set(largest)


def setup_inputs(seed: int = 0, part: int = 0) -> dict:
    streams_of = jax.random.split(jax.random.key(seed), 5)
    part_keys = jax.random.split(jax.random.fold_in(streams_of[4], part), 5)
    return {
        "records": draw_records(jax.random.fold_in(jax.random.fold_in(streams_of[4], part), 71), part),
        "templates": draw_templates(jax.random.fold_in(streams_of[4], 71), part),
        "channel_mask": place_ends((jax.random.randint(streams_of[2], (C, KA, KB), 0, 4) < 3).astype(jnp.int32), jax.random.fold_in(streams_of[2], 1), 0, 1),
        "lag_table": place_ends(jax.random.randint(streams_of[3], (C, KA, KB), 0, LAGS), jax.random.fold_in(streams_of[3], 1), 0, LAGS - 1).astype(jnp.int32),
    }


def energy_scale(extended):
    squares = jnp.square(extended.astype(jnp.float32))
    window = lax.reduce_window(squares, jnp.zeros((), squares.dtype), lax.add, (1, L), (1, 1), 'VALID')
    return lax.rsqrt(window / L + 1e-05)

def stack_part(extended, inverse_rms, kernels, in_use, lag_rows, out_len):
    channels, template_count, tmpl_len = kernels.shape
    kernel_flat = kernels.reshape(channels * template_count, 1, tmpl_len)
    products = lax.conv_general_dilated(extended[None], kernel_flat, (1,), 'VALID', dimension_numbers=('NCH', 'OIH', 'NCH'), feature_group_count=channels, preferred_element_type=jnp.float32)[0]
    products = products.reshape(channels, template_count, -1)
    normalized = products * inverse_rms[:, None, :]
    positions = lag_rows.astype(jnp.int32)[:, :, None] + jnp.arange(out_len, dtype=jnp.int32)[None, None, :]
    aligned = jnp.take_along_axis(normalized, positions, axis=2)
    as_float = kernels.astype(jnp.float32)
    kernel_rms = jnp.sqrt(lax.optimization_barrier(jnp.mean(as_float * as_float, axis=2)) + 1e-05)
    weight = in_use.astype(jnp.float32) / (kernel_rms * tmpl_len)
    return jnp.einsum('cnt,cn->nt', aligned, weight, precision=lax.Precision.HIGHEST)

def reference(records, templates, channel_mask, lag_table):
    channels, record_len = records.shape
    extended = jnp.concatenate([records, jnp.zeros((channels, L + LAGS - 1), records.dtype)], axis=1)
    inverse_rms = energy_scale(extended)
    kernel_rows = jnp.moveaxis(templates, 1, 0)
    mask_rows = jnp.moveaxis(channel_mask, 1, 0)
    lag_rows = jnp.moveaxis(lag_table, 1, 0)

    def one_template_row(members):
        kernels, in_use, lags_here = members
        return stack_part(extended, inverse_rms, kernels, in_use, lags_here, record_len)
    return lax.map(one_template_row, (kernel_rows, mask_rows, lag_rows))
```

```python
import jax
import jax.numpy as jnp
from jax import lax
from jax.experimental import pallas as pl
from jax.experimental.pallas import tpu as pltpu
from jax.sharding import PartitionSpec as P

LAGS = 64
LANES = 128
STEP = 32
ROWS = 16
GROUP = 8
BAND = 256
BATCH = 4


def up(value, unit):
    return -(-value // unit) * unit


def shifted_left(values, count):
    width = values.shape[1]
    if count % width == 0:
        return values
    return pltpu.roll(values, width - count % width, 1)


def unroll_of(count):
    return max(k for k in range(1, 5) if count % k == 0)


def exchange(rec_ref, tmpl_ref, code_ref, tail_ref, slots_ref, codes_ref, sems):
    channels = rec_ref.shape[0]
    size = lax.axis_size("tm")
    last = size - 1
    me, col = lax.axis_index("tm"), lax.axis_index("tmpl")
    mate = col + 1 - 2 * (col % 2)
    half = channels // 2

    def there(axis, index):
        return {"device_id": {axis: index}, "device_id_type": pl.DeviceIdType.MESH}

    def copy(src, dst, name, out, into, where):
        send, recv = sems[name]
        return pltpu.make_async_remote_copy(
            src_ref=src, dst_ref=dst, send_sem=send.at[out], recv_sem=recv.at[into], **where
        )

    piece = pl.ds(pl.multiple_of((col % 2) * half, ROWS), half)
    barrier = pltpu.get_barrier_semaphore()
    rim = copy(rec_ref.at[piece], tail_ref.at[piece], "rim", 0, 0, there("tm", jnp.maximum(me - 1, 0)))
    rim_on = copy(tail_ref.at[piece], tail_ref.at[piece], "rim", 1, 1, there("tmpl", mate))

    def row_to(device):
        return copy(tmpl_ref, slots_ref.at[me], "tmpl", device, me, there("tm", device))

    def code_to(device):
        return copy(code_ref, codes_ref.at[me], "code", device, me, there("tm", device))

    def greet():
        @pl.when(me < last)
        def _():
            for d in range(1, last):
                pl.semaphore_signal(barrier, inc=1, **there("tm", (me + d) % last))
            pl.semaphore_signal(barrier, inc=1, **there("tmpl", mate))

    def open_early():
        @pl.when(me < last)
        def _():
            pl.semaphore_wait(barrier, last)
            pl.semaphore_signal(barrier, inc=1, **there("tm", last))
            for d in range(1, last):
                row_to((me + d) % last).start()
                code_to((me + d) % last).start()

            @pl.when(me > 0)
            def _():
                rim.start()

    def open_last_rows():
        @pl.when(me == last)
        def _():
            pl.semaphore_wait(barrier, last)
            for t in range(last):
                row_to(t).start()
            rim.start()
            for t in range(last):
                pl.semaphore_signal(barrier, inc=1, **there("tm", t))

    def open_last_codes():
        @pl.when(me == last)
        def _():
            for t in range(last):
                code_to(t).start()

    def serve_last():
        @pl.when(me < last)
        def _():
            pl.semaphore_wait(barrier, 1)
            row_to(last).start()
            code_to(last).start()

    def land_rim():
        @pl.when(me < last)
        def _():
            rim.wait_recv()
            rim_on.start()
            rim_on.wait_recv()

        @pl.when(me == last)
        def _():
            tail_ref[...] = jnp.zeros_like(tail_ref)

    def land_row(row):
        @pl.when(me != row)
        def _():
            other = (me + 1) % size
            copy(tmpl_ref, slots_ref.at[row], "tmpl", other, row, there("tm", other)).wait_recv()
            copy(code_ref, codes_ref.at[row], "code", other, row, there("tm", other)).wait_recv()

    def drain():
        for d in range(1, size):
            target = (me + d) % size
            row_to(target).wait_send()
            code_to(target).wait_send()

        @pl.when(me > 0)
        def _():
            rim.wait_send()

        @pl.when(me < last)
        def _():
            rim_on.wait_send()

    return greet, open_early, open_last_rows, open_last_codes, serve_last, land_rim, land_row, drain


def correlate(
    rec_ref,
    tmpl_ref,
    mask_ref,
    lag_ref,
    out_ref,
    own_ref,
    tail_ref,
    slots_ref,
    code_ref,
    codes_ref,
    wide_ref,
    trace_ref,
    weight_ref,
    spread_ref,
    moved_ref,
    inverse_ref,
    own_sems,
    *sem_refs,
):
    size, channels, tmpl_len = slots_ref.shape
    slab_len = rec_ref.shape[1]
    span = trace_ref.shape[2]
    blocks = -(-tmpl_len // STEP)
    wide = blocks * STEP * GROUP
    deep = STEP * GROUP
    reach = moved_ref.shape[2]
    per_tile = LANES // STEP
    me = lax.axis_index("tm")
    last = size - 1
    names = ("rim", "tmpl", "code")
    sems = {name: sem_refs[2 * i : 2 * i + 2] for i, name in enumerate(names)}
    greet, open_early, open_last_rows, open_last_codes, serve_last, land_rim, land_row, drain = exchange(
        rec_ref, tmpl_ref, code_ref, tail_ref, slots_ref, codes_ref, sems
    )
    greet()
    fetch_row = pltpu.make_async_copy(tmpl_ref, slots_ref.at[me], own_sems.at[0])
    fetch_rec = pltpu.make_async_copy(rec_ref, own_ref, own_sems.at[1])
    fetch_row.start()
    fetch_rec.start()
    open_last_rows()
    code_ref[...] = jnp.where(mask_ref[...] != 0, lag_ref[...], -1)
    codes_ref[me] = code_ref[...]
    open_last_codes()

    lane = lax.broadcasted_iota(jnp.int32, (tmpl_len, wide), 1)
    sample = lax.broadcasted_iota(jnp.int32, (tmpl_len, wide), 0)
    spread_ref[...] = jnp.where(lane // GROUP == sample, 1.0, 0.0).astype(jnp.bfloat16)
    own = lax.broadcasted_iota(jnp.int32, (channels, wide), 1) % GROUP == (
        lax.broadcasted_iota(jnp.int32, (channels, wide), 0) % GROUP
    )
    lag = LAGS - 1 - lax.broadcasted_iota(jnp.int32, (LAGS, channels), 0)
    fetch_row.wait()
    fetch_rec.wait()

    def expand(n):
        kernel = slots_ref[n]
        widened = jnp.dot(kernel, spread_ref[...], preferred_element_type=jnp.float32)
        as_float = kernel.astype(jnp.float32)
        mean = jnp.sum(as_float * as_float, axis=1, keepdims=True) / tmpl_len
        weight = 1.0 / (jnp.sqrt(mean + 1e-05) * tmpl_len)
        wide_ref[n] = jnp.where(own, widened, 0.0)
        weight_ref[n] = jnp.broadcast_to(weight, (channels, LANES))

    def scale():
        series = jnp.concatenate([own_ref[...], tail_ref[...]], axis=1).astype(jnp.float32)
        squares = series * series
        high = squares.astype(jnp.bfloat16)
        low = (squares - high.astype(jnp.float32)).astype(jnp.bfloat16)
        both = jnp.concatenate([high, low], axis=0)
        row = lax.broadcasted_iota(jnp.int32, (BAND, BAND), 0)
        column = lax.broadcasted_iota(jnp.int32, (BAND, BAND), 1)
        bands = []
        for d in range((tmpl_len + BAND - 2) // BAND + 1):
            off = d * BAND + row - column
            bands.append(jnp.where((off >= 0) & (off < tmpl_len), 1.0, 0.0).astype(jnp.bfloat16))
        for n in range(-(-span // BAND)):
            total = None
            for d, band in enumerate(bands):
                part = both[:, (n + d) * BAND : (n + d + 1) * BAND]
                if part.shape[1] == 0:
                    continue
                part = jnp.dot(part, band[: part.shape[1]], preferred_element_type=jnp.float32)
                total = part if total is None else total + part
            energy = total[:channels] + total[channels:]
            here = slice(n * BAND, min((n + 1) * BAND, span))
            inverse_ref[:, here] = lax.rsqrt(energy / tmpl_len + 1e-05)[:, : here.stop - here.start]

    def spread_out():
        @pl.loop(0, channels // ROWS)
        def _(pair):
            rows = pl.ds(pl.multiple_of(pair * ROWS, ROWS), ROWS)
            series = jnp.concatenate([own_ref[rows, :], tail_ref[rows, :]], axis=1).astype(jnp.float32)
            for side in range(ROWS // GROUP):
                part = series[side * GROUP : (side + 1) * GROUP]
                moved_ref[pair * (ROWS // GROUP) + side] = jnp.concatenate(
                    [shifted_left(part, b)[:, :reach] for b in range(STEP)], axis=0
                ).astype(jnp.bfloat16)

    def traces(first, batch):
        @pl.loop(0, channels // GROUP, unroll=unroll_of(channels // GROUP))
        def _(group):
            rows = pl.ds(pl.multiple_of(group * GROUP, GROUP), GROUP)
            left = jnp.concatenate(
                [
                    wide_ref[first + n, rows, a * deep : (a + 1) * deep]
                    for n in range(batch)
                    for a in range(blocks)
                ],
                axis=0,
            ).astype(jnp.bfloat16)
            partial = jnp.dot(left, moved_ref[group], preferred_element_type=jnp.float32)
            inverse_rms = inverse_ref[rows, :]
            for n in range(batch):
                total = None
                for phase in range(min(per_tile, blocks)):
                    lined = None
                    for a in range(phase, blocks, per_tile):
                        begin = (a - phase) * STEP
                        line = (n * blocks + a) * GROUP
                        piece = partial[line : line + GROUP, begin : begin + span + LANES]
                        if piece.shape[1] < span + LANES:
                            missing = span + LANES - piece.shape[1]
                            piece = jnp.concatenate(
                                [piece, jnp.zeros((GROUP, missing), jnp.float32)], axis=1
                            )
                        lined = piece if lined is None else lined + piece
                    lined = shifted_left(lined, phase * STEP)[:, :span]
                    total = lined if total is None else total + lined
                weight = jnp.concatenate([weight_ref[first + n, rows, :]] * (span // LANES), axis=1)
                trace_ref[first + n, rows, :] = total * inverse_rms * weight

    def stack(n):
        pick = jnp.where(codes_ref[n] == lag, 1.0, 0.0).astype(jnp.bfloat16)
        trace = trace_ref[n]
        high = trace.astype(jnp.bfloat16)
        low = (trace - high.astype(jnp.float32)).astype(jnp.bfloat16)
        by_lag = jnp.dot(pick, high, preferred_element_type=jnp.float32)
        by_lag += jnp.dot(pick, low, preferred_element_type=jnp.float32)
        lined = pltpu.roll(by_lag, span - LAGS + 1, 1, stride=1, stride_axis=0)
        out_ref[pl.ds(n, 1), :] = jnp.sum(lined, axis=0, keepdims=True)[:, :slab_len]

    def rows_of(first, batch):
        for n in range(batch):
            expand(first + n)
        traces(first, batch)
        for n in range(batch):
            stack(first + n)

    open_early()
    land_rim()
    scale()
    spread_out()
    serve_last()
    for row in range(last):
        land_row(row)
    batch = max(1, min(BATCH, last))
    if last // batch > 1:

        @pl.loop(0, last // batch)
        def _(turn):
            rows_of(turn * batch, batch)

    elif last:
        rows_of(0, batch)
    if last % batch:
        rows_of(last - last % batch, last % batch)
    land_row(last)
    rows_of(last, 1)
    drain()


def local(records, templates, channel_mask, lag_table):
    channels, slab_len = records.shape
    first, second, tmpl_len = templates.shape[1:]
    assert first == 1 and second == 1
    size = lax.axis_size("tm")
    span = up(slab_len + LAGS - 1, LANES)
    blocks = -(-tmpl_len // STEP)
    wide = blocks * STEP * GROUP
    reach = up(slab_len + LAGS - 1 + (blocks - 1) * STEP, LANES)
    dma = pltpu.SemaphoreType.DMA
    hbm, vmem = pl.BlockSpec(memory_space=pl.ANY), pl.BlockSpec(memory_space=pltpu.VMEM)
    out = pl.pallas_call(
        correlate,
        out_shape=jax.ShapeDtypeStruct((size, slab_len), jnp.float32),
        in_specs=[hbm, hbm, vmem, vmem],
        out_specs=vmem,
        scratch_shapes=[
            pltpu.VMEM((channels, slab_len), jnp.bfloat16),
            pltpu.VMEM((channels, slab_len), jnp.bfloat16),
            pltpu.VMEM((size, channels, tmpl_len), jnp.bfloat16),
            pltpu.VMEM((1, channels), jnp.int32),
            pltpu.VMEM((size, 1, channels), jnp.int32),
            pltpu.VMEM((size, channels, wide), jnp.float32),
            pltpu.VMEM((size, channels, span), jnp.float32),
            pltpu.VMEM((size, channels, LANES), jnp.float32),
            pltpu.VMEM((tmpl_len, wide), jnp.bfloat16),
            pltpu.VMEM((channels // GROUP, STEP * GROUP, reach), jnp.bfloat16),
            pltpu.VMEM((channels, span), jnp.float32),
            dma((2,)),
            dma((2,)),
            dma((2,)),
            dma((size,)),
            dma((size,)),
            dma((size,)),
            dma((size,)),
        ],
        compiler_params=pltpu.CompilerParams(
            vmem_limit_bytes=62 << 20, collective_id=0, has_side_effects=True
        ),
    )(
        records,
        templates.reshape(channels, tmpl_len),
        channel_mask.reshape(1, channels),
        lag_table.reshape(1, channels),
    )
    return out.reshape(size, 1, slab_len)


def solution(mesh):
    return jax.shard_map(
        local,
        mesh=mesh,
        in_specs=(
            P(None, ("grp", "tm")),
            P(None, "tm", "tmpl", None),
            P(None, "tm", "tmpl"),
            P(None, "tm", "tmpl"),
        ),
        out_specs=P(None, "tmpl", ("grp", "tm")),
        check_vma=False,
    )
```

```python
import jax
import jax.numpy as jnp
from jax import lax
from jax.experimental import pallas as pl
from jax.experimental.pallas import tpu as pltpu
from jax.sharding import PartitionSpec as P

LAGS = 64
LANES = 128
STEP = 32
ROWS = 16
GROUP = 8
BAND = 256
BATCH = 4


def up(value, unit):
    return -(-value // unit) * unit


def shifted_left(values, count):
    width = values.shape[1]
    if count % width == 0:
        return values
    return pltpu.roll(values, width - count % width, 1)


def unroll_of(count):
    return max(k for k in range(1, 5) if count % k == 0)


def exchange(rec_ref, tmpl_ref, code_ref, tail_ref, slots_ref, codes_ref, sems):
    channels = rec_ref.shape[0]
    size = lax.axis_size("tm")
    me, col = lax.axis_index("tm"), lax.axis_index("tmpl")
    mate = col + 1 - 2 * (col % 2)
    half = channels // 2

    def there(axis, index):
        return {"device_id": {axis: index}, "device_id_type": pl.DeviceIdType.MESH}

    def copy(src, dst, name, index, where):
        send, recv = sems[name]
        return pltpu.make_async_remote_copy(
            src_ref=src, dst_ref=dst, send_sem=send.at[index], recv_sem=recv.at[index], **where
        )

    piece = pl.ds(pl.multiple_of((col % 2) * half, ROWS), half)
    barrier = pltpu.get_barrier_semaphore()
    peer = [(me + d) % size for d in range(size)]
    rim = copy(rec_ref.at[piece], tail_ref.at[piece], "rim", 0, there("tm", jnp.maximum(me - 1, 0)))
    rim_on = copy(tail_ref.at[piece], tail_ref.at[piece], "rim", 1, there("tmpl", mate))
    row = [None] + [copy(tmpl_ref, slots_ref.at[d], "tmpl", d, there("tm", peer[d])) for d in range(1, size)]
    code = [None] + [copy(code_ref, codes_ref.at[d], "code", d, there("tm", peer[d])) for d in range(1, size)]

    def greet():
        for d in range(1, size):
            pl.semaphore_signal(barrier, inc=1, **there("tm", peer[d]))
        pl.semaphore_signal(barrier, inc=1, **there("tmpl", mate))

    def start():
        pl.semaphore_wait(barrier, size)

        @pl.when(me > 0)
        def _():
            rim.start()

        for move in row[1:] + code[1:]:
            move.start()

    def land_rim():
        @pl.when(me < size - 1)
        def _():
            rim.wait_recv()
            rim_on.start()
            rim_on.wait_recv()

        @pl.when(me == size - 1)
        def _():
            tail_ref[...] = jnp.zeros_like(tail_ref)

    def land_rows():
        for move in row[1:] + code[1:]:
            move.wait_recv()

    def drain():
        for move in row[1:] + code[1:]:
            move.wait_send()

        @pl.when(me > 0)
        def _():
            rim.wait_send()

        @pl.when(me < size - 1)
        def _():
            rim_on.wait_send()

    return greet, start, land_rim, land_rows, drain


def correlate(
    rec_ref,
    tmpl_ref,
    mask_ref,
    lag_ref,
    out_ref,
    own_ref,
    tail_ref,
    slots_ref,
    code_ref,
    codes_ref,
    wide_ref,
    trace_ref,
    weight_ref,
    spread_ref,
    moved_ref,
    inverse_ref,
    own_sems,
    *sem_refs,
):
    size, channels, tmpl_len = slots_ref.shape
    slab_len = rec_ref.shape[1]
    span = trace_ref.shape[2]
    blocks = -(-tmpl_len // STEP)
    wide = blocks * STEP * GROUP
    deep = STEP * GROUP
    reach = moved_ref.shape[2]
    per_tile = LANES // STEP
    me = lax.axis_index("tm")
    names = ("rim", "tmpl", "code")
    sems = {name: sem_refs[2 * i : 2 * i + 2] for i, name in enumerate(names)}
    greet, start, land_rim, land_rows, drain = exchange(
        rec_ref, tmpl_ref, code_ref, tail_ref, slots_ref, codes_ref, sems
    )
    greet()
    fetch_row = pltpu.make_async_copy(tmpl_ref, slots_ref.at[0], own_sems.at[0])
    fetch_rec = pltpu.make_async_copy(rec_ref, own_ref, own_sems.at[1])
    fetch_row.start()
    fetch_rec.start()
    code_ref[...] = jnp.where(mask_ref[...] != 0, lag_ref[...], -1)
    codes_ref[0] = code_ref[...]
    start()

    lane = lax.broadcasted_iota(jnp.int32, (tmpl_len, wide), 1)
    sample = lax.broadcasted_iota(jnp.int32, (tmpl_len, wide), 0)
    spread_ref[...] = jnp.where(lane // GROUP == sample, 1.0, 0.0).astype(jnp.bfloat16)
    own = lax.broadcasted_iota(jnp.int32, (channels, wide), 1) % GROUP == (
        lax.broadcasted_iota(jnp.int32, (channels, wide), 0) % GROUP
    )
    lag = LAGS - 1 - lax.broadcasted_iota(jnp.int32, (LAGS, channels), 0)
    fetch_row.wait()
    fetch_rec.wait()

    def expand(n):
        kernel = slots_ref[n]
        widened = jnp.dot(kernel, spread_ref[...], preferred_element_type=jnp.float32)
        as_float = kernel.astype(jnp.float32)
        mean = jnp.sum(as_float * as_float, axis=1, keepdims=True) / tmpl_len
        weight = 1.0 / (jnp.sqrt(mean + 1e-05) * tmpl_len)
        wide_ref[n] = jnp.where(own, widened, 0.0)
        weight_ref[n] = jnp.broadcast_to(weight, (channels, LANES))

    def scale():
        series = jnp.concatenate([own_ref[...], tail_ref[...]], axis=1).astype(jnp.float32)
        squares = series * series
        high = squares.astype(jnp.bfloat16)
        low = (squares - high.astype(jnp.float32)).astype(jnp.bfloat16)
        both = jnp.concatenate([high, low], axis=0)
        row = lax.broadcasted_iota(jnp.int32, (BAND, BAND), 0)
        column = lax.broadcasted_iota(jnp.int32, (BAND, BAND), 1)
        bands = []
        for d in range((tmpl_len + BAND - 2) // BAND + 1):
            off = d * BAND + row - column
            bands.append(jnp.where((off >= 0) & (off < tmpl_len), 1.0, 0.0).astype(jnp.bfloat16))
        for n in range(-(-span // BAND)):
            total = None
            for d, band in enumerate(bands):
                part = both[:, (n + d) * BAND : (n + d + 1) * BAND]
                if part.shape[1] == 0:
                    continue
                part = jnp.dot(part, band[: part.shape[1]], preferred_element_type=jnp.float32)
                total = part if total is None else total + part
            energy = total[:channels] + total[channels:]
            here = slice(n * BAND, min((n + 1) * BAND, span))
            inverse_ref[:, here] = lax.rsqrt(energy / tmpl_len + 1e-05)[:, : here.stop - here.start]

    def spread_out():
        @pl.loop(0, channels // ROWS)
        def _(pair):
            rows = pl.ds(pl.multiple_of(pair * ROWS, ROWS), ROWS)
            series = jnp.concatenate([own_ref[rows, :], tail_ref[rows, :]], axis=1).astype(jnp.float32)
            for side in range(ROWS // GROUP):
                part = series[side * GROUP : (side + 1) * GROUP]
                moved_ref[pair * (ROWS // GROUP) + side] = jnp.concatenate(
                    [shifted_left(part, b)[:, :reach] for b in range(STEP)], axis=0
                ).astype(jnp.bfloat16)

    def traces(first, batch):
        @pl.loop(0, channels // GROUP, unroll=unroll_of(channels // GROUP))
        def _(group):
            rows = pl.ds(pl.multiple_of(group * GROUP, GROUP), GROUP)
            left = jnp.concatenate(
                [
                    wide_ref[first + n, rows, a * deep : (a + 1) * deep]
                    for n in range(batch)
                    for a in range(blocks)
                ],
                axis=0,
            ).astype(jnp.bfloat16)
            partial = jnp.dot(left, moved_ref[group], preferred_element_type=jnp.float32)
            inverse_rms = inverse_ref[rows, :]
            for n in range(batch):
                total = None
                for phase in range(min(per_tile, blocks)):
                    lined = None
                    for a in range(phase, blocks, per_tile):
                        begin = (a - phase) * STEP
                        line = (n * blocks + a) * GROUP
                        piece = partial[line : line + GROUP, begin : begin + span + LANES]
                        if piece.shape[1] < span + LANES:
                            missing = span + LANES - piece.shape[1]
                            piece = jnp.concatenate(
                                [piece, jnp.zeros((GROUP, missing), jnp.float32)], axis=1
                            )
                        lined = piece if lined is None else lined + piece
                    lined = shifted_left(lined, phase * STEP)[:, :span]
                    total = lined if total is None else total + lined
                weight = jnp.concatenate([weight_ref[first + n, rows, :]] * (span // LANES), axis=1)
                trace_ref[first + n, rows, :] = total * inverse_rms * weight

    def stack(n):
        pick = jnp.where(codes_ref[n] == lag, 1.0, 0.0).astype(jnp.bfloat16)
        trace = trace_ref[n]
        high = trace.astype(jnp.bfloat16)
        low = (trace - high.astype(jnp.float32)).astype(jnp.bfloat16)
        by_lag = jnp.dot(pick, high, preferred_element_type=jnp.float32)
        by_lag += jnp.dot(pick, low, preferred_element_type=jnp.float32)
        lined = pltpu.roll(by_lag, span - LAGS + 1, 1, stride=1, stride_axis=0)
        out_ref[pl.ds((me + size - n) % size, 1), :] = jnp.sum(lined, axis=0, keepdims=True)[:, :slab_len]

    def rows_of(first, batch):
        for n in range(batch):
            expand(first + n)
        traces(first, batch)
        for n in range(batch):
            stack(first + n)

    expand(0)
    land_rim()
    scale()
    spread_out()
    traces(0, 1)
    stack(0)
    land_rows()
    others = size - 1
    batch = max(1, min(BATCH, others))
    if others // batch > 1:

        @pl.loop(0, others // batch)
        def _(turn):
            rows_of(1 + turn * batch, batch)

    elif others:
        rows_of(1, batch)
    if others % batch:
        rows_of(size - others % batch, others % batch)
    drain()


def local(records, templates, channel_mask, lag_table):
    channels, slab_len = records.shape
    first, second, tmpl_len = templates.shape[1:]
    assert first == 1 and second == 1
    size = lax.axis_size("tm")
    span = up(slab_len + LAGS - 1, LANES)
    blocks = -(-tmpl_len // STEP)
    wide = blocks * STEP * GROUP
    reach = up(slab_len + LAGS - 1 + (blocks - 1) * STEP, LANES)
    dma = pltpu.SemaphoreType.DMA
    hbm, vmem = pl.BlockSpec(memory_space=pl.ANY), pl.BlockSpec(memory_space=pltpu.VMEM)
    out = pl.pallas_call(
        correlate,
        out_shape=jax.ShapeDtypeStruct((size, slab_len), jnp.float32),
        in_specs=[hbm, hbm, vmem, vmem],
        out_specs=vmem,
        scratch_shapes=[
            pltpu.VMEM((channels, slab_len), jnp.bfloat16),
            pltpu.VMEM((channels, slab_len), jnp.bfloat16),
            pltpu.VMEM((size, channels, tmpl_len), jnp.bfloat16),
            pltpu.VMEM((1, channels), jnp.int32),
            pltpu.VMEM((size, 1, channels), jnp.int32),
            pltpu.VMEM((size, channels, wide), jnp.float32),
            pltpu.VMEM((size, channels, span), jnp.float32),
            pltpu.VMEM((size, channels, LANES), jnp.float32),
            pltpu.VMEM((tmpl_len, wide), jnp.bfloat16),
            pltpu.VMEM((channels // GROUP, STEP * GROUP, reach), jnp.bfloat16),
            pltpu.VMEM((channels, span), jnp.float32),
            dma((2,)),
            dma((2,)),
            dma((2,)),
            dma((size,)),
            dma((size,)),
            dma((size,)),
            dma((size,)),
        ],
        compiler_params=pltpu.CompilerParams(
            vmem_limit_bytes=62 << 20, collective_id=0, has_side_effects=True
        ),
    )(
        records,
        templates.reshape(channels, tmpl_len),
        channel_mask.reshape(1, channels),
        lag_table.reshape(1, channels),
    )
    return out.reshape(size, 1, slab_len)


def solution(mesh):
    return jax.shard_map(
        local,
        mesh=mesh,
        in_specs=(
            P(None, ("grp", "tm")),
            P(None, "tm", "tmpl", None),
            P(None, "tm", "tmpl"),
            P(None, "tm", "tmpl"),
        ),
        out_specs=P(None, "tmpl", ("grp", "tm")),
        check_vma=False,
    )
```

```python
import jax
import jax.numpy as jnp
from jax import lax
from jax.experimental import pallas as pl
from jax.experimental.pallas import tpu as pltpu
from jax.sharding import PartitionSpec as P

LAGS = 64
LANES = 128
STEP = 32
ROWS = 16
GROUP = 8
BAND = 256
BATCH = 4


def up(value, unit):
    return -(-value // unit) * unit


def shifted_left(values, count):
    width = values.shape[1]
    if count % width == 0:
        return values
    return pltpu.roll(values, width - count % width, 1)


def unroll_of(count):
    return max(k for k in range(1, 5) if count % k == 0)


def remainders(columns):
    parts, begin, left = [], 0, columns % LANES
    width = LANES // 2
    while left:
        if left >= width:
            parts.append((begin, width))
            begin, left = begin + width, left - width
        width //= 2
    return parts


def packed_rows(channels, columns, shares):
    blocks = channels // ROWS
    rows = columns // LANES * channels
    for _, width in remainders(columns):
        rows += -(-blocks // (LANES // width)) * ROWS
    return up(rows, ROWS * shares)


def pack(values, rows):
    channels, columns = values.shape
    whole = columns // LANES
    blocks = channels // ROWS
    out = [values[:, i * LANES : (i + 1) * LANES] for i in range(whole)]
    if columns % LANES:
        rest = values[:, whole * LANES :].astype(jnp.float32)
        rest = jnp.concatenate([rest, jnp.zeros((channels, LANES - rest.shape[1]), jnp.float32)], axis=1)
        lane = lax.broadcasted_iota(jnp.int32, (ROWS, LANES), 1)
        for begin, width in remainders(columns):
            side = LANES // width
            for first in range(0, blocks, side):
                line = jnp.zeros((ROWS, LANES), jnp.float32)
                for i in range(min(side, blocks - first)):
                    part = rest[(first + i) * ROWS : (first + i + 1) * ROWS]
                    part = shifted_left(part, (begin - i * width) % LANES)
                    line = jnp.where((lane >= i * width) & (lane < (i + 1) * width), part, line)
                out.append(line.astype(values.dtype))
    missing = rows - sum(part.shape[0] for part in out)
    if missing:
        out.append(jnp.zeros((missing, LANES), values.dtype))
    return jnp.concatenate(out, axis=0)


def unpack(values, channels, columns):
    whole = columns // LANES
    blocks = channels // ROWS
    out = [values[i * channels : (i + 1) * channels] for i in range(whole)]
    if columns % LANES:
        lane = lax.broadcasted_iota(jnp.int32, (ROWS, LANES), 1)
        lines = [jnp.zeros((ROWS, LANES), jnp.float32)] * blocks
        row = whole * channels
        for begin, width in remainders(columns):
            side = LANES // width
            for first in range(0, blocks, side):
                line = values[row : row + ROWS].astype(jnp.float32)
                row += ROWS
                for i in range(min(side, blocks - first)):
                    part = shifted_left(line, (i * width - begin) % LANES)
                    here = (lane >= begin) & (lane < begin + width)
                    lines[first + i] = jnp.where(here, part, lines[first + i])
        out.append(jnp.concatenate(lines, axis=0).astype(values.dtype))
    return jnp.concatenate(out, axis=1)


def exchange(rec_ref, code_ref, tail_ref, slots_ref, codes_ref, sems):
    channels = rec_ref.shape[0]
    size, grp_size = lax.axis_size("tm"), lax.axis_size("grp")
    me, part, col = lax.axis_index("tm"), lax.axis_index("grp"), lax.axis_index("tmpl")
    mate = col + 1 - 2 * (col % 2)
    half, share = channels // 2, slots_ref.shape[1] // grp_size

    def there(axis, index):
        return {"device_id": {axis: index}, "device_id_type": pl.DeviceIdType.MESH}

    def copy(src, dst, name, index, where):
        send, recv = sems[name]
        return pltpu.make_async_remote_copy(
            src_ref=src, dst_ref=dst, send_sem=send.at[index], recv_sem=recv.at[index], **where
        )

    piece = pl.ds(pl.multiple_of((col % 2) * half, ROWS), half)
    barrier = pltpu.get_barrier_semaphore()
    peer = [(me + d) % size for d in range(size)]
    rim = copy(rec_ref.at[piece], tail_ref.at[piece], "rim", 0, there("tm", jnp.maximum(me - 1, 0)))
    rim_on = copy(tail_ref.at[piece], tail_ref.at[piece], "rim", 1, there("tmpl", mate))
    mine = pl.ds(pl.multiple_of(part * share, ROWS), share)
    row = [None] + [
        copy(slots_ref.at[0, mine], slots_ref.at[d, mine], "tmpl", d, there("tm", peer[d])) for d in range(1, size)
    ]
    onward = [None] + [
        [
            copy(
                slots_ref.at[d, mine],
                slots_ref.at[d, mine],
                "pass",
                d * grp_size + e,
                there("grp", (part + e) % grp_size),
            )
            for e in range(1, grp_size)
        ]
        for d in range(1, size)
    ]
    code = [None] + [copy(code_ref, codes_ref.at[d], "code", d, there("tm", peer[d])) for d in range(1, size)]

    def greet():
        for d in range(1, size):
            pl.semaphore_signal(barrier, inc=1, **there("tm", peer[d]))
        for e in range(1, grp_size):
            pl.semaphore_signal(barrier, inc=1, **there("grp", (part + e) % grp_size))
        pl.semaphore_signal(barrier, inc=1, **there("tmpl", mate))

    def start():
        pl.semaphore_wait(barrier, size + grp_size - 1)

        @pl.when(me > 0)
        def _():
            rim.start()

        for move in row[1:] + code[1:]:
            move.start()

    def land_rim():
        @pl.when(me < size - 1)
        def _():
            rim.wait_recv()
            rim_on.start()
            rim_on.wait_recv()

        @pl.when(me == size - 1)
        def _():
            tail_ref[...] = jnp.zeros_like(tail_ref)

    def pass_on(d):
        if d < size:
            row[d].wait_recv()
            for step in onward[d]:
                step.start()

    def land_row(d):
        for step in onward[d]:
            step.wait_recv()
        code[d].wait_recv()

    def drain():
        for move in row[1:] + code[1:] + [step for steps in onward[1:] for step in steps]:
            move.wait_send()

        @pl.when(me > 0)
        def _():
            rim.wait_send()

        @pl.when(me < size - 1)
        def _():
            rim_on.wait_send()

    return greet, start, land_rim, pass_on, land_row, drain


def correlate(
    rec_ref,
    tmpl_ref,
    mask_ref,
    lag_ref,
    out_ref,
    own_ref,
    kernel_ref,
    tail_ref,
    slots_ref,
    code_ref,
    codes_ref,
    wide_ref,
    trace_ref,
    weight_ref,
    spread_ref,
    moved_ref,
    inverse_ref,
    own_sems,
    *sem_refs,
):
    channels, tmpl_len = tmpl_ref.shape
    size = slots_ref.shape[0]
    filled = spread_ref.shape[0]
    slab_len = rec_ref.shape[1]
    span = trace_ref.shape[2]
    blocks = -(-tmpl_len // STEP)
    wide = blocks * STEP * GROUP
    deep = STEP * GROUP
    reach = moved_ref.shape[2]
    per_tile = LANES // STEP
    me = lax.axis_index("tm")
    names = ("rim", "tmpl", "code", "pass")
    sems = {name: sem_refs[2 * i : 2 * i + 2] for i, name in enumerate(names)}
    greet, start, land_rim, pass_on, land_row, drain = exchange(
        rec_ref, code_ref, tail_ref, slots_ref, codes_ref, sems
    )
    greet()
    fetch_row = pltpu.make_async_copy(tmpl_ref, kernel_ref, own_sems.at[0])
    fetch_rec = pltpu.make_async_copy(rec_ref, own_ref, own_sems.at[1])
    fetch_row.start()
    fetch_rec.start()
    code_ref[...] = jnp.where(mask_ref[...] != 0, lag_ref[...], -1)
    codes_ref[0] = code_ref[...]
    fetch_row.wait()
    slots_ref[0] = pack(kernel_ref[...], slots_ref.shape[1])
    start()

    lane = lax.broadcasted_iota(jnp.int32, (filled, wide), 1)
    sample = lax.broadcasted_iota(jnp.int32, (filled, wide), 0)
    spread_ref[...] = jnp.where(lane // GROUP == sample, 1.0, 0.0).astype(jnp.bfloat16)
    own = lax.broadcasted_iota(jnp.int32, (channels, wide), 1) % GROUP == (
        lax.broadcasted_iota(jnp.int32, (channels, wide), 0) % GROUP
    )
    lag = LAGS - 1 - lax.broadcasted_iota(jnp.int32, (LAGS, channels), 0)
    fetch_rec.wait()

    def expand(n):
        kernel = unpack(slots_ref[n], channels, tmpl_len)
        widened = jnp.dot(kernel, spread_ref[...], preferred_element_type=jnp.float32)
        as_float = kernel.astype(jnp.float32)
        mean = jnp.sum(as_float * as_float, axis=1, keepdims=True) / tmpl_len
        weight = 1.0 / (jnp.sqrt(mean + 1e-05) * tmpl_len)
        wide_ref[n] = jnp.where(own, widened, 0.0)
        weight_ref[n] = jnp.broadcast_to(weight, (channels, LANES))

    def scale():
        series = jnp.concatenate([own_ref[...], tail_ref[...]], axis=1).astype(jnp.float32)
        squares = series * series
        high = squares.astype(jnp.bfloat16)
        low = (squares - high.astype(jnp.float32)).astype(jnp.bfloat16)
        both = jnp.concatenate([high, low], axis=0)
        row = lax.broadcasted_iota(jnp.int32, (BAND, BAND), 0)
        column = lax.broadcasted_iota(jnp.int32, (BAND, BAND), 1)
        bands = []
        for d in range((tmpl_len + BAND - 2) // BAND + 1):
            off = d * BAND + row - column
            bands.append(jnp.where((off >= 0) & (off < tmpl_len), 1.0, 0.0).astype(jnp.bfloat16))
        for n in range(-(-span // BAND)):
            total = None
            for d, band in enumerate(bands):
                part = both[:, (n + d) * BAND : (n + d + 1) * BAND]
                if part.shape[1] == 0:
                    continue
                part = jnp.dot(part, band[: part.shape[1]], preferred_element_type=jnp.float32)
                total = part if total is None else total + part
            energy = total[:channels] + total[channels:]
            here = slice(n * BAND, min((n + 1) * BAND, span))
            inverse_ref[:, here] = lax.rsqrt(energy / tmpl_len + 1e-05)[:, : here.stop - here.start]

    def spread_out(first, count):
        @pl.loop(first, first + count)
        def _(pair):
            rows = pl.ds(pl.multiple_of(pair * ROWS, ROWS), ROWS)
            series = jnp.concatenate([own_ref[rows, :], tail_ref[rows, :]], axis=1).astype(jnp.float32)
            for side in range(ROWS // GROUP):
                part = series[side * GROUP : (side + 1) * GROUP]
                moved_ref[pair * (ROWS // GROUP) + side] = jnp.concatenate(
                    [shifted_left(part, b)[:, :reach] for b in range(STEP)], axis=0
                ).astype(jnp.bfloat16)

    def traces(first, batch):
        @pl.loop(0, channels // GROUP, unroll=unroll_of(channels // GROUP))
        def _(group):
            rows = pl.ds(pl.multiple_of(group * GROUP, GROUP), GROUP)
            left = jnp.concatenate(
                [
                    wide_ref[first + n, rows, a * deep : (a + 1) * deep]
                    for n in range(batch)
                    for a in range(blocks)
                ],
                axis=0,
            ).astype(jnp.bfloat16)
            partial = jnp.dot(left, moved_ref[group], preferred_element_type=jnp.float32)
            inverse_rms = inverse_ref[rows, :]
            for n in range(batch):
                total = None
                for phase in range(min(per_tile, blocks)):
                    lined = None
                    for a in range(phase, blocks, per_tile):
                        begin = (a - phase) * STEP
                        line = (n * blocks + a) * GROUP
                        piece = partial[line : line + GROUP, begin : begin + span + LANES]
                        if piece.shape[1] < span + LANES:
                            missing = span + LANES - piece.shape[1]
                            piece = jnp.concatenate(
                                [piece, jnp.zeros((GROUP, missing), jnp.float32)], axis=1
                            )
                        lined = piece if lined is None else lined + piece
                    lined = shifted_left(lined, phase * STEP)[:, :span]
                    total = lined if total is None else total + lined
                weight = jnp.concatenate([weight_ref[first + n, rows, :]] * (span // LANES), axis=1)
                trace_ref[first + n, rows, :] = total * inverse_rms * weight

    def stack(n):
        pick = jnp.where(codes_ref[n] == lag, 1.0, 0.0).astype(jnp.bfloat16)
        trace = trace_ref[n]
        high = trace.astype(jnp.bfloat16)
        low = (trace - high.astype(jnp.float32)).astype(jnp.bfloat16)
        by_lag = jnp.dot(pick, high, preferred_element_type=jnp.float32)
        by_lag += jnp.dot(pick, low, preferred_element_type=jnp.float32)
        lined = pltpu.roll(by_lag, span - LAGS + 1, 1, stride=1, stride_axis=0)
        out_ref[pl.ds((me + size - n) % size, 1), :] = jnp.sum(lined, axis=0, keepdims=True)[:, :slab_len]

    def rows_of(first, batch):
        for n in range(batch):
            expand(first + n)
        traces(first, batch)
        for n in range(batch):
            stack(first + n)

    expand(0)
    land_rim()
    scale()
    pass_on(1)
    pairs = channels // ROWS
    spread_out(0, pairs // 2)
    pass_on(2)
    spread_out(pairs // 2, pairs - pairs // 2)
    pass_on(3)
    traces(0, 1)
    stack(0)
    for d in range(4, size):
        pass_on(d)
    ahead = size - 2
    for d in range(1, size - 1):
        land_row(d)
    batch = max(1, min(BATCH, ahead))
    if ahead // batch > 1:

        @pl.loop(0, ahead // batch)
        def _(turn):
            rows_of(1 + turn * batch, batch)

    elif ahead > 0:
        rows_of(1, batch)
    if ahead > 0 and ahead % batch:
        rows_of(size - 1 - ahead % batch, ahead % batch)
    if size > 1:
        land_row(size - 1)
        rows_of(size - 1, 1)
    drain()


def local(records, templates, channel_mask, lag_table):
    channels, slab_len = records.shape
    first, second, tmpl_len = templates.shape[1:]
    assert first == 1 and second == 1
    size = lax.axis_size("tm")
    span = up(slab_len + LAGS - 1, LANES)
    blocks = -(-tmpl_len // STEP)
    wide = blocks * STEP * GROUP
    reach = up(slab_len + LAGS - 1 + (blocks - 1) * STEP, LANES)
    grp_size = lax.axis_size("grp")
    dma = pltpu.SemaphoreType.DMA
    hbm, vmem = pl.BlockSpec(memory_space=pl.ANY), pl.BlockSpec(memory_space=pltpu.VMEM)
    out = pl.pallas_call(
        correlate,
        out_shape=jax.ShapeDtypeStruct((size, slab_len), jnp.float32),
        in_specs=[hbm, hbm, vmem, vmem],
        out_specs=vmem,
        scratch_shapes=[
            pltpu.VMEM((channels, slab_len), jnp.bfloat16),
            pltpu.VMEM((channels, tmpl_len), jnp.bfloat16),
            pltpu.VMEM((channels, slab_len), jnp.bfloat16),
            pltpu.VMEM((size, packed_rows(channels, tmpl_len, grp_size), LANES), jnp.bfloat16),
            pltpu.VMEM((1, channels), jnp.int32),
            pltpu.VMEM((size, 1, channels), jnp.int32),
            pltpu.VMEM((size, channels, wide), jnp.float32),
            pltpu.VMEM((size, channels, span), jnp.float32),
            pltpu.VMEM((size, channels, LANES), jnp.float32),
            pltpu.VMEM((up(tmpl_len, LANES), wide), jnp.bfloat16),
            pltpu.VMEM((channels // GROUP, STEP * GROUP, reach), jnp.bfloat16),
            pltpu.VMEM((channels, span), jnp.float32),
            dma((2,)),
            dma((2,)),
            dma((2,)),
            dma((size,)),
            dma((size,)),
            dma((size,)),
            dma((size,)),
            dma((size * grp_size,)),
            dma((size * grp_size,)),
        ],
        compiler_params=pltpu.CompilerParams(
            vmem_limit_bytes=62 << 20, collective_id=0, has_side_effects=True
        ),
    )(
        records,
        templates.reshape(channels, tmpl_len),
        channel_mask.reshape(1, channels),
        lag_table.reshape(1, channels),
    )
    return out.reshape(size, 1, slab_len)


def solution(mesh):
    return jax.shard_map(
        local,
        mesh=mesh,
        in_specs=(
            P(None, ("grp", "tm")),
            P(None, "tm", "tmpl", None),
            P(None, "tm", "tmpl"),
            P(None, "tm", "tmpl"),
        ),
        out_specs=P(None, "tmpl", ("grp", "tm")),
        check_vma=False,
    )
```

```python
import jax
import jax.numpy as jnp
from jax import lax
from jax.experimental import pallas as pl
from jax.experimental.pallas import tpu as pltpu
from jax.sharding import PartitionSpec as P

LAGS = 64
LANES = 128
STEP = 16
ROWS = 16
GROUP = 16
BAND = 256
BATCH = 4


def up(value, unit):
    return -(-value // unit) * unit


def shifted_left(values, count):
    width = values.shape[1]
    if count % width == 0:
        return values
    return pltpu.roll(values, width - count % width, 1)


def unroll_of(count):
    return max(k for k in range(1, 11) if count % k == 0)


def rim_columns(tmpl_len):
    return up(tmpl_len + LAGS - 2, 8)


def remainders(columns):
    parts, begin, left = [], 0, columns % LANES
    width = LANES // 2
    while left:
        if left >= width:
            parts.append((begin, width))
            begin, left = begin + width, left - width
        width //= 2
    return parts


def packed_rows(channels, columns, shares):
    blocks = channels // ROWS
    rows = columns // LANES * channels
    for _, width in remainders(columns):
        rows += -(-blocks // (LANES // width)) * ROWS
    return up(rows, ROWS * shares)


def pack(values, rows):
    channels, columns = values.shape
    whole = columns // LANES
    blocks = channels // ROWS
    out = [values[:, i * LANES : (i + 1) * LANES] for i in range(whole)]
    if columns % LANES:
        rest = values[:, whole * LANES :].astype(jnp.float32)
        rest = jnp.concatenate([rest, jnp.zeros((channels, LANES - rest.shape[1]), jnp.float32)], axis=1)
        lane = lax.broadcasted_iota(jnp.int32, (ROWS, LANES), 1)
        for begin, width in remainders(columns):
            side = LANES // width
            for first in range(0, blocks, side):
                line = jnp.zeros((ROWS, LANES), jnp.float32)
                for i in range(min(side, blocks - first)):
                    part = rest[(first + i) * ROWS : (first + i + 1) * ROWS]
                    part = shifted_left(part, (begin - i * width) % LANES)
                    line = jnp.where((lane >= i * width) & (lane < (i + 1) * width), part, line)
                out.append(line.astype(values.dtype))
    missing = rows - sum(part.shape[0] for part in out)
    if missing:
        out.append(jnp.zeros((missing, LANES), values.dtype))
    return jnp.concatenate(out, axis=0)


def unpack(values, channels, columns):
    whole = columns // LANES
    blocks = channels // ROWS
    out = [values[i * channels : (i + 1) * channels] for i in range(whole)]
    if columns % LANES:
        lane = lax.broadcasted_iota(jnp.int32, (ROWS, LANES), 1)
        lines = [jnp.zeros((ROWS, LANES), jnp.float32)] * blocks
        row = whole * channels
        for begin, width in remainders(columns):
            side = LANES // width
            for first in range(0, blocks, side):
                line = values[row : row + ROWS].astype(jnp.float32)
                row += ROWS
                for i in range(min(side, blocks - first)):
                    part = shifted_left(line, (i * width - begin) % LANES)
                    here = (lane >= begin) & (lane < begin + width)
                    lines[first + i] = jnp.where(here, part, lines[first + i])
        out.append(jnp.concatenate(lines, axis=0).astype(values.dtype))
    return jnp.concatenate(out, axis=1)


def exchange(code_ref, rims_ref, slots_ref, codes_ref, sems):
    size = lax.axis_size("tm")
    me, col = lax.axis_index("tm"), lax.axis_index("tmpl")
    mate = col + 1 - 2 * (col % 2)
    half = rims_ref.shape[1] // 2

    def there(axis, index):
        return {"device_id": {axis: index}, "device_id_type": pl.DeviceIdType.MESH}

    def copy(src, dst, name, index, where):
        send, recv = sems[name]
        return pltpu.make_async_remote_copy(
            src_ref=src, dst_ref=dst, send_sem=send.at[index], recv_sem=recv.at[index], **where
        )

    piece = pl.ds(pl.multiple_of((col % 2) * half, ROWS), half)
    barrier = pltpu.get_barrier_semaphore()
    peer = [(me + d) % size for d in range(size)]
    rim = copy(rims_ref.at[0, piece], rims_ref.at[1, piece], "rim", 0, there("tm", jnp.maximum(me - 1, 0)))
    rim_on = copy(rims_ref.at[1, piece], rims_ref.at[1, piece], "rim", 1, there("tmpl", mate))
    row = [None] + [
        copy(slots_ref.at[0], slots_ref.at[d], "tmpl", d, there("tm", peer[d])) for d in range(1, size)
    ]
    code = [None] + [copy(code_ref, codes_ref.at[d], "code", d, there("tm", peer[d])) for d in range(1, size)]

    def greet():
        for d in range(1, size):
            pl.semaphore_signal(barrier, inc=1, **there("tm", peer[d]))
        pl.semaphore_signal(barrier, inc=1, **there("tmpl", mate))

    def start():
        pl.semaphore_wait(barrier, size)

        @pl.when(me > 0)
        def _():
            rim.start()

        for move in row[1:] + code[1:]:
            move.start()

    def land_rim():
        @pl.when(me < size - 1)
        def _():
            rim.wait_recv()
            rim_on.start()
            rim_on.wait_recv()

        @pl.when(me == size - 1)
        def _():
            rims_ref[1] = jnp.zeros(rims_ref.shape[1:], rims_ref.dtype)

    def land_row(d):
        row[d].wait_recv()
        code[d].wait_recv()

    def drain():
        for move in row[1:] + code[1:]:
            move.wait_send()

        @pl.when(me > 0)
        def _():
            rim.wait_send()

        @pl.when(me < size - 1)
        def _():
            rim_on.wait_send()

    return greet, start, land_rim, land_row, drain


def correlate(
    rec_ref,
    tmpl_ref,
    mask_ref,
    lag_ref,
    out_ref,
    own_ref,
    kernel_ref,
    series_ref,
    rims_ref,
    slots_ref,
    code_ref,
    codes_ref,
    wide_ref,
    trace_ref,
    weight_ref,
    spread_ref,
    moved_ref,
    inverse_ref,
    own_sems,
    *sem_refs,
):
    channels, tmpl_len = tmpl_ref.shape
    size = slots_ref.shape[0]
    filled = spread_ref.shape[0]
    rim_len = rim_columns(tmpl_len)
    slab_len = rec_ref.shape[1]
    span = trace_ref.shape[2]
    blocks = -(-tmpl_len // STEP)
    wide = blocks * STEP * GROUP
    deep = STEP * GROUP
    reach = moved_ref.shape[2]
    per_tile = LANES // STEP
    me = lax.axis_index("tm")
    names = ("rim", "tmpl", "code")
    sems = {name: sem_refs[2 * i : 2 * i + 2] for i, name in enumerate(names)}
    greet, start, land_rim, land_row, drain = exchange(
        code_ref, rims_ref, slots_ref, codes_ref, sems
    )
    greet()
    fetch_row = pltpu.make_async_copy(tmpl_ref, kernel_ref, own_sems.at[0])
    fetch_rec = pltpu.make_async_copy(rec_ref, own_ref, own_sems.at[1])
    fetch_row.start()
    fetch_rec.start()
    code_ref[...] = jnp.where(mask_ref[...] != 0, lag_ref[...], -1)
    codes_ref[0] = code_ref[...]
    fetch_row.wait()
    slots_ref[0] = pack(kernel_ref[...], slots_ref.shape[1])
    fetch_rec.wait()
    rims_ref[0] = pack(own_ref[:, :rim_len], rims_ref.shape[1])
    start()

    lane = lax.broadcasted_iota(jnp.int32, (filled, wide), 1)
    sample = lax.broadcasted_iota(jnp.int32, (filled, wide), 0)
    spread_ref[...] = jnp.where(lane // GROUP == sample, 1.0, 0.0).astype(jnp.bfloat16)
    own = lax.broadcasted_iota(jnp.int32, (channels, wide), 1) % GROUP == (
        lax.broadcasted_iota(jnp.int32, (channels, wide), 0) % GROUP
    )
    lag = LAGS - 1 - lax.broadcasted_iota(jnp.int32, (LAGS, channels), 0)

    def expand(n, slot):
        kernel = unpack(slots_ref[n], channels, tmpl_len)
        widened = jnp.dot(kernel, spread_ref[...], preferred_element_type=jnp.float32)
        as_float = kernel.astype(jnp.float32)
        mean = jnp.sum(as_float * as_float, axis=1, keepdims=True) / tmpl_len
        weight = 1.0 / (jnp.sqrt(mean + 1e-05) * tmpl_len)
        wide_ref[slot] = jnp.where(own, widened, 0.0).astype(jnp.bfloat16)
        weight_ref[slot] = jnp.broadcast_to(weight, (channels, LANES))

    def scale():
        tail = unpack(rims_ref[1], channels, rim_len)
        beyond = series_ref.shape[1] - slab_len - tail.shape[1]
        parts = [own_ref[...], tail] + [jnp.zeros((channels, beyond), tail.dtype)] * (beyond > 0)
        series_ref[...] = jnp.concatenate(parts, axis=1)
        series = series_ref[...].astype(jnp.float32)
        squares = series * series
        high = squares.astype(jnp.bfloat16)
        low = (squares - high.astype(jnp.float32)).astype(jnp.bfloat16)
        both = jnp.concatenate([high, low], axis=0)
        row = lax.broadcasted_iota(jnp.int32, (BAND, BAND), 0)
        column = lax.broadcasted_iota(jnp.int32, (BAND, BAND), 1)
        bands = []
        for d in range((tmpl_len + BAND - 2) // BAND + 1):
            off = d * BAND + row - column
            bands.append(jnp.where((off >= 0) & (off < tmpl_len), 1.0, 0.0).astype(jnp.bfloat16))
        for n in range(-(-span // BAND)):
            total = None
            for d, band in enumerate(bands):
                part = both[:, (n + d) * BAND : (n + d + 1) * BAND]
                if part.shape[1] == 0:
                    continue
                part = jnp.dot(part, band[: part.shape[1]], preferred_element_type=jnp.float32)
                total = part if total is None else total + part
            energy = total[:channels] + total[channels:]
            here = slice(n * BAND, min((n + 1) * BAND, span))
            inverse_ref[:, here] = lax.rsqrt(energy / tmpl_len + 1e-05)[:, : here.stop - here.start]

    def spread_out():
        @pl.loop(0, channels // GROUP)
        def _(group):
            rows = pl.ds(pl.multiple_of(group * GROUP, GROUP), GROUP)
            series = series_ref[rows, :].astype(jnp.float32)
            moved_ref[group] = jnp.concatenate(
                [shifted_left(series, b)[:, :reach] for b in range(STEP)], axis=0
            ).astype(jnp.bfloat16)

    def traces(batch):
        @pl.loop(0, channels // GROUP, unroll=unroll_of(channels // GROUP))
        def _(group):
            rows = pl.ds(pl.multiple_of(group * GROUP, GROUP), GROUP)
            left = jnp.concatenate(
                [wide_ref[n, rows, a * deep : (a + 1) * deep] for n in range(batch) for a in range(blocks)],
                axis=0,
            )
            partial = jnp.dot(left, moved_ref[group], preferred_element_type=jnp.float32)
            inverse_rms = inverse_ref[rows, :]
            for n in range(batch):
                total = None
                for phase in range(min(per_tile, blocks)):
                    lined = None
                    for a in range(phase, blocks, per_tile):
                        begin = (a - phase) * STEP
                        line = (n * blocks + a) * GROUP
                        piece = partial[line : line + GROUP, begin : begin + span + LANES]
                        if piece.shape[1] < span + LANES:
                            missing = span + LANES - piece.shape[1]
                            piece = jnp.concatenate(
                                [piece, jnp.zeros((GROUP, missing), jnp.float32)], axis=1
                            )
                        lined = piece if lined is None else lined + piece
                    lined = shifted_left(lined, phase * STEP)[:, :span]
                    total = lined if total is None else total + lined
                weight = jnp.concatenate([weight_ref[n, rows, :]] * (span // LANES), axis=1)
                trace_ref[n, rows, :] = total * inverse_rms * weight

    def stack(n, slot):
        pick = jnp.where(codes_ref[n] == lag, 1.0, 0.0).astype(jnp.bfloat16)
        trace = trace_ref[slot]
        high = trace.astype(jnp.bfloat16)
        low = (trace - high.astype(jnp.float32)).astype(jnp.bfloat16)
        by_lag = jnp.dot(pick, high, preferred_element_type=jnp.float32)
        by_lag += jnp.dot(pick, low, preferred_element_type=jnp.float32)
        lined = pltpu.roll(by_lag, span - LAGS + 1, 1, stride=1, stride_axis=0)
        out_ref[pl.ds((me + size - n) % size, 1), :] = jnp.sum(lined, axis=0, keepdims=True)[:, :slab_len]

    def rows_of(first, batch):
        for n in range(batch):
            expand(first + n, n)
        traces(batch)
        for n in range(batch):
            stack(first + n, n)

    expand(0, 0)
    land_rim()
    scale()
    spread_out()
    traces(1)
    stack(0, 0)
    ahead = size - 2
    for d in range(1, size - 1):
        land_row(d)
    batch = max(1, min(BATCH, ahead))
    if ahead // batch > 1:

        @pl.loop(0, ahead // batch)
        def _(turn):
            rows_of(1 + turn * batch, batch)

    elif ahead > 0:
        rows_of(1, batch)
    if ahead > 0 and ahead % batch:
        rows_of(size - 1 - ahead % batch, ahead % batch)
    if size > 1:
        land_row(size - 1)
        rows_of(size - 1, 1)
    drain()


def local(records, templates, channel_mask, lag_table):
    channels, slab_len = records.shape
    first, second, tmpl_len = templates.shape[1:]
    assert first == 1 and second == 1
    size = lax.axis_size("tm")
    span = up(slab_len + LAGS - 1, LANES)
    blocks = -(-tmpl_len // STEP)
    wide = blocks * STEP * GROUP
    reach = up(slab_len + LAGS - 1 + (blocks - 1) * STEP, LANES)
    dma = pltpu.SemaphoreType.DMA
    hbm, vmem = pl.BlockSpec(memory_space=pl.ANY), pl.BlockSpec(memory_space=pltpu.VMEM)
    out = pl.pallas_call(
        correlate,
        out_shape=jax.ShapeDtypeStruct((size, slab_len), jnp.float32),
        in_specs=[hbm, hbm, vmem, vmem],
        out_specs=vmem,
        scratch_shapes=[
            pltpu.VMEM((channels, slab_len), jnp.bfloat16),
            pltpu.VMEM((channels, tmpl_len), jnp.bfloat16),
            pltpu.VMEM((channels, slab_len + up(rim_columns(tmpl_len), LANES)), jnp.bfloat16),
            pltpu.VMEM((2, packed_rows(channels, rim_columns(tmpl_len), 2), LANES), jnp.bfloat16),
            pltpu.VMEM((size, packed_rows(channels, tmpl_len, 1), LANES), jnp.bfloat16),
            pltpu.VMEM((1, channels), jnp.int32),
            pltpu.VMEM((size, 1, channels), jnp.int32),
            pltpu.VMEM((BATCH, channels, wide), jnp.bfloat16),
            pltpu.VMEM((BATCH, channels, span), jnp.float32),
            pltpu.VMEM((BATCH, channels, LANES), jnp.float32),
            pltpu.VMEM((up(tmpl_len, LANES), wide), jnp.bfloat16),
            pltpu.VMEM((channels // GROUP, STEP * GROUP, reach), jnp.bfloat16),
            pltpu.VMEM((channels, span), jnp.float32),
            dma((2,)),
            dma((2,)),
            dma((2,)),
            dma((size,)),
            dma((size,)),
            dma((size,)),
            dma((size,)),
        ],
        compiler_params=pltpu.CompilerParams(
            vmem_limit_bytes=62 << 20, collective_id=0, has_side_effects=True
        ),
    )(
        records,
        templates.reshape(channels, tmpl_len),
        channel_mask.reshape(1, channels),
        lag_table.reshape(1, channels),
    )
    return out.reshape(size, 1, slab_len)


def solution(mesh):
    return jax.shard_map(
        local,
        mesh=mesh,
        in_specs=(
            P(None, ("grp", "tm")),
            P(None, "tm", "tmpl", None),
            P(None, "tm", "tmpl"),
            P(None, "tm", "tmpl"),
        ),
        out_specs=P(None, "tmpl", ("grp", "tm")),
        check_vma=False,
    )
```

```python
import jax
import jax.numpy as jnp
from jax import lax
from jax.experimental import pallas as pl
from jax.experimental.pallas import tpu as pltpu
from jax.sharding import PartitionSpec as P

LAGS = 64
LANES = 128
STEP = 32
ROWS = 16
GROUP = 8
BAND = 256
BATCH = 4


def up(value, unit):
    return -(-value // unit) * unit


def shifted_left(values, count):
    width = values.shape[1]
    if count % width == 0:
        return values
    return pltpu.roll(values, width - count % width, 1)


def unroll_of(count):
    return max(k for k in range(1, 21) if count % k == 0)


def rim_columns(tmpl_len):
    return up(tmpl_len + LAGS - 2, 8)


def remainders(columns):
    parts, begin, left = [], 0, columns % LANES
    width = LANES // 2
    while left:
        if left >= width:
            parts.append((begin, width))
            begin, left = begin + width, left - width
        width //= 2
    return parts


def packed_rows(channels, columns, shares):
    blocks = channels // ROWS
    rows = columns // LANES * channels
    for _, width in remainders(columns):
        rows += -(-blocks // (LANES // width)) * ROWS
    return up(rows, ROWS * shares)


def code_place(channels, columns):
    blocks = channels // ROWS
    rows = packed_rows(channels, columns, 1)
    parts = remainders(columns)
    if parts:
        side = LANES // parts[-1][1]
        used = (blocks % side or side) * parts[-1][1]
        if channels <= (LANES - used) * ROWS:
            return rows - ROWS, used, LANES - used
    return rows, 0, LANES


def put_codes(code, line, lane0, per):
    channels = code.shape[1]
    width = up(channels, LANES)
    code = jnp.concatenate([code, jnp.zeros((1, width - channels), jnp.float32)], axis=1)
    lane = lax.broadcasted_iota(jnp.int32, (ROWS, LANES), 1)
    row = lax.broadcasted_iota(jnp.int32, (ROWS, LANES), 0)
    for r in range(-(-channels // per)):
        part = shifted_left(jnp.broadcast_to(code, (ROWS, width)), (r * per - lane0) % width)[:, :LANES]
        line = jnp.where((row == r) & (lane >= lane0) & (lane < lane0 + per), part, line)
    return line


def get_codes(line, channels, lane0, per):
    width = up(channels, LANES)
    lane = lax.broadcasted_iota(jnp.int32, (1, width), 1)
    code = jnp.zeros((1, width), jnp.float32)
    wide = jnp.concatenate([line, jnp.zeros((ROWS, width - LANES), jnp.float32)], axis=1)
    for r in range(-(-channels // per)):
        part = shifted_left(wide, (lane0 - r * per) % width)[r : r + 1]
        code = jnp.where((lane >= r * per) & (lane < (r + 1) * per), part, code)
    return code[:, :channels]


def pack(values, rows):
    channels, columns = values.shape
    whole = columns // LANES
    blocks = channels // ROWS
    out = [values[:, i * LANES : (i + 1) * LANES] for i in range(whole)]
    if columns % LANES:
        rest = values[:, whole * LANES :].astype(jnp.float32)
        rest = jnp.concatenate([rest, jnp.zeros((channels, LANES - rest.shape[1]), jnp.float32)], axis=1)
        lane = lax.broadcasted_iota(jnp.int32, (ROWS, LANES), 1)
        for begin, width in remainders(columns):
            side = LANES // width
            for first in range(0, blocks, side):
                line = jnp.zeros((ROWS, LANES), jnp.float32)
                for i in range(min(side, blocks - first)):
                    part = rest[(first + i) * ROWS : (first + i + 1) * ROWS]
                    part = shifted_left(part, (begin - i * width) % LANES)
                    line = jnp.where((lane >= i * width) & (lane < (i + 1) * width), part, line)
                out.append(line.astype(values.dtype))
    missing = rows - sum(part.shape[0] for part in out)
    if missing:
        out.append(jnp.zeros((missing, LANES), values.dtype))
    return jnp.concatenate(out, axis=0)


def unpack(values, channels, columns):
    whole = columns // LANES
    blocks = channels // ROWS
    out = [values[i * channels : (i + 1) * channels] for i in range(whole)]
    if columns % LANES:
        lane = lax.broadcasted_iota(jnp.int32, (ROWS, LANES), 1)
        lines = [jnp.zeros((ROWS, LANES), jnp.float32)] * blocks
        row = whole * channels
        for begin, width in remainders(columns):
            side = LANES // width
            for first in range(0, blocks, side):
                line = values[row : row + ROWS].astype(jnp.float32)
                row += ROWS
                for i in range(min(side, blocks - first)):
                    part = shifted_left(line, (i * width - begin) % LANES)
                    here = (lane >= begin) & (lane < begin + width)
                    lines[first + i] = jnp.where(here, part, lines[first + i])
        out.append(jnp.concatenate(lines, axis=0).astype(values.dtype))
    return jnp.concatenate(out, axis=1)


def exchange(rims_ref, slots_ref, sems):
    size = lax.axis_size("tm")
    me, col = lax.axis_index("tm"), lax.axis_index("tmpl")
    mate = col + 1 - 2 * (col % 2)
    half = rims_ref.shape[1] // 2

    def there(axis, index):
        return {"device_id": {axis: index}, "device_id_type": pl.DeviceIdType.MESH}

    def copy(src, dst, name, index, where):
        send, recv = sems[name]
        return pltpu.make_async_remote_copy(
            src_ref=src, dst_ref=dst, send_sem=send.at[index], recv_sem=recv.at[index], **where
        )

    piece = pl.ds(pl.multiple_of((col % 2) * half, ROWS), half)
    barrier = pltpu.get_barrier_semaphore()
    peer = [(me + d) % size for d in range(size)]
    rim = copy(rims_ref.at[0, piece], rims_ref.at[1, piece], "rim", 0, there("tm", jnp.maximum(me - 1, 0)))
    rim_on = copy(rims_ref.at[1, piece], rims_ref.at[1, piece], "rim", 1, there("tmpl", mate))
    row = [None] + [
        copy(slots_ref.at[0], slots_ref.at[d], "tmpl", d, there("tm", peer[d])) for d in range(1, size)
    ]

    def greet():
        for d in range(1, size):
            pl.semaphore_signal(barrier, inc=1, **there("tm", peer[d]))
        pl.semaphore_signal(barrier, inc=1, **there("tmpl", mate))

    def start():
        pl.semaphore_wait(barrier, size)

        @pl.when(me > 0)
        def _():
            rim.start()

        for move in row[1:]:
            move.start()

    def land_rim():
        @pl.when(me < size - 1)
        def _():
            rim.wait_recv()
            rim_on.start()
            rim_on.wait_recv()

        @pl.when(me == size - 1)
        def _():
            rims_ref[1] = jnp.zeros(rims_ref.shape[1:], rims_ref.dtype)

    def land_row(d):
        row[d].wait_recv()

    def drain():
        for move in row[1:]:
            move.wait_send()

        @pl.when(me > 0)
        def _():
            rim.wait_send()

        @pl.when(me < size - 1)
        def _():
            rim_on.wait_send()

    return greet, start, land_rim, land_row, drain


def correlate(
    rec_ref,
    tmpl_ref,
    mask_ref,
    lag_ref,
    out_ref,
    own_ref,
    kernel_ref,
    series_ref,
    rims_ref,
    slots_ref,
    wide_ref,
    trace_ref,
    weight_ref,
    spread_ref,
    moved_ref,
    inverse_ref,
    own_sems,
    *sem_refs,
):
    channels, tmpl_len = tmpl_ref.shape
    size = slots_ref.shape[0]
    filled = spread_ref.shape[0]
    rim_len = rim_columns(tmpl_len)
    slab_len = rec_ref.shape[1]
    span = trace_ref.shape[2]
    blocks = -(-tmpl_len // STEP)
    wide = blocks * STEP * GROUP
    deep = STEP * GROUP
    reach = moved_ref.shape[2]
    per_tile = LANES // STEP
    me = lax.axis_index("tm")
    names = ("rim", "tmpl")
    sems = {name: sem_refs[2 * i : 2 * i + 2] for i, name in enumerate(names)}
    greet, start, land_rim, land_row, drain = exchange(
        rims_ref, slots_ref, sems
    )
    greet()
    fetch_row = pltpu.make_async_copy(tmpl_ref, kernel_ref, own_sems.at[0])
    fetch_rec = pltpu.make_async_copy(rec_ref, own_ref, own_sems.at[1])
    fetch_row.start()
    fetch_rec.start()
    line0, lane0, per = code_place(channels, tmpl_len)
    fetch_row.wait()
    packed = pack(kernel_ref[...], packed_rows(channels, tmpl_len, 1))
    slots_ref[0, : packed.shape[0]] = packed
    code = jnp.where(mask_ref[...] != 0, lag_ref[...], -1).astype(jnp.float32)
    line = packed[line0:] if line0 < packed.shape[0] else jnp.zeros((ROWS, LANES), packed.dtype)
    line = put_codes(code, line.astype(jnp.float32), lane0, per)
    slots_ref[0, line0 : line0 + ROWS] = line.astype(packed.dtype)
    fetch_rec.wait()
    rims_ref[0] = pack(own_ref[:, :rim_len], rims_ref.shape[1])
    start()

    lane = lax.broadcasted_iota(jnp.int32, (filled, wide), 1)
    sample = lax.broadcasted_iota(jnp.int32, (filled, wide), 0)
    spread_ref[...] = jnp.where(lane // GROUP == sample, 1.0, 0.0).astype(jnp.bfloat16)
    own = lax.broadcasted_iota(jnp.int32, (channels, wide), 1) % GROUP == (
        lax.broadcasted_iota(jnp.int32, (channels, wide), 0) % GROUP
    )
    lag = (LAGS - 1 - lax.broadcasted_iota(jnp.int32, (LAGS, channels), 0)).astype(jnp.float32)

    def expand(n, slot):
        kernel = unpack(slots_ref[n], channels, tmpl_len)
        widened = jnp.dot(kernel, spread_ref[...], preferred_element_type=jnp.float32)
        as_float = kernel.astype(jnp.float32)
        mean = jnp.sum(as_float * as_float, axis=1, keepdims=True) / tmpl_len
        weight = 1.0 / (jnp.sqrt(mean + 1e-05) * tmpl_len)
        wide_ref[slot] = jnp.where(own, widened, 0.0)
        weight_ref[slot] = jnp.broadcast_to(weight, (channels, LANES))

    def scale():
        tail = unpack(rims_ref[1], channels, rim_len)
        beyond = series_ref.shape[1] - slab_len - tail.shape[1]
        parts = [own_ref[...], tail] + [jnp.zeros((channels, beyond), tail.dtype)] * (beyond > 0)
        series_ref[...] = jnp.concatenate(parts, axis=1)
        series = series_ref[...].astype(jnp.float32)
        squares = series * series
        high = squares.astype(jnp.bfloat16)
        low = (squares - high.astype(jnp.float32)).astype(jnp.bfloat16)
        both = jnp.concatenate([high, low], axis=0)
        row = lax.broadcasted_iota(jnp.int32, (BAND, BAND), 0)
        column = lax.broadcasted_iota(jnp.int32, (BAND, BAND), 1)
        bands = []
        for d in range((tmpl_len + BAND - 2) // BAND + 1):
            off = d * BAND + row - column
            bands.append(jnp.where((off >= 0) & (off < tmpl_len), 1.0, 0.0).astype(jnp.bfloat16))
        for n in range(-(-span // BAND)):
            total = None
            for d, band in enumerate(bands):
                part = both[:, (n + d) * BAND : (n + d + 1) * BAND]
                if part.shape[1] == 0:
                    continue
                part = jnp.dot(part, band[: part.shape[1]], preferred_element_type=jnp.float32)
                total = part if total is None else total + part
            energy = total[:channels] + total[channels:]
            here = slice(n * BAND, min((n + 1) * BAND, span))
            inverse_ref[:, here] = lax.rsqrt(energy / tmpl_len + 1e-05)[:, : here.stop - here.start]

    def spread_out():
        @pl.loop(0, channels // ROWS)
        def _(pair):
            rows = pl.ds(pl.multiple_of(pair * ROWS, ROWS), ROWS)
            series = series_ref[rows, :].astype(jnp.float32)
            for side in range(ROWS // GROUP):
                part = series[side * GROUP : (side + 1) * GROUP]
                moved_ref[pair * (ROWS // GROUP) + side] = jnp.concatenate(
                    [shifted_left(part, b)[:, :reach] for b in range(STEP)], axis=0
                ).astype(jnp.bfloat16)

    def traces(batch):
        @pl.loop(0, channels // GROUP, unroll=unroll_of(channels // GROUP))
        def _(group):
            rows = pl.ds(pl.multiple_of(group * GROUP, GROUP), GROUP)
            left = jnp.concatenate(
                [wide_ref[n, rows, a * deep : (a + 1) * deep] for n in range(batch) for a in range(blocks)],
                axis=0,
            ).astype(jnp.bfloat16)
            partial = jnp.dot(left, moved_ref[group], preferred_element_type=jnp.float32)
            inverse_rms = inverse_ref[rows, :]
            for n in range(batch):
                total = None
                for phase in range(min(per_tile, blocks)):
                    lined = None
                    for a in range(phase, blocks, per_tile):
                        begin = (a - phase) * STEP
                        line = (n * blocks + a) * GROUP
                        piece = partial[line : line + GROUP, begin : begin + span + LANES]
                        if piece.shape[1] < span + LANES:
                            missing = span + LANES - piece.shape[1]
                            piece = jnp.concatenate(
                                [piece, jnp.zeros((GROUP, missing), jnp.float32)], axis=1
                            )
                        lined = piece if lined is None else lined + piece
                    lined = shifted_left(lined, phase * STEP)[:, :span]
                    total = lined if total is None else total + lined
                weight = jnp.concatenate([weight_ref[n, rows, :]] * (span // LANES), axis=1)
                trace_ref[n, rows, :] = total * inverse_rms * weight

    def stack(n, slot):
        line = slots_ref[n, line0 : line0 + ROWS].astype(jnp.float32)
        pick = jnp.where(get_codes(line, channels, lane0, per) == lag, 1.0, 0.0).astype(jnp.bfloat16)
        trace = trace_ref[slot]
        high = trace.astype(jnp.bfloat16)
        low = (trace - high.astype(jnp.float32)).astype(jnp.bfloat16)
        by_lag = jnp.dot(pick, high, preferred_element_type=jnp.float32)
        by_lag += jnp.dot(pick, low, preferred_element_type=jnp.float32)
        lined = pltpu.roll(by_lag, span - LAGS + 1, 1, stride=1, stride_axis=0)
        out_ref[pl.ds((me + size - n) % size, 1), :] = jnp.sum(lined, axis=0, keepdims=True)[:, :slab_len]

    def rows_of(first, batch):
        for n in range(batch):
            expand(first + n, n)
        traces(batch)
        for n in range(batch):
            stack(first + n, n)

    batch = min(BATCH, size)
    if batch == size:
        expand(0, 0)
    land_rim()
    scale()
    spread_out()
    if batch == size:
        for d in range(1, size):
            land_row(d)
            expand(d, d)
        traces(size)
        for d in range(size):
            stack(d, d)
    else:
        for d in range(1, size):
            land_row(d)

        @pl.loop(0, size // batch)
        def _(turn):
            rows_of(turn * batch, batch)

        if size % batch:
            rows_of(size - size % batch, size % batch)
    drain()


def local(records, templates, channel_mask, lag_table):
    channels, slab_len = records.shape
    first, second, tmpl_len = templates.shape[1:]
    assert first == 1 and second == 1
    size = lax.axis_size("tm")
    span = up(slab_len + LAGS - 1, LANES)
    blocks = -(-tmpl_len // STEP)
    wide = blocks * STEP * GROUP
    reach = up(slab_len + LAGS - 1 + (blocks - 1) * STEP, LANES)
    lines = max(packed_rows(channels, tmpl_len, 1), code_place(channels, tmpl_len)[0] + ROWS)
    dma = pltpu.SemaphoreType.DMA
    hbm, vmem = pl.BlockSpec(memory_space=pl.ANY), pl.BlockSpec(memory_space=pltpu.VMEM)
    out = pl.pallas_call(
        correlate,
        out_shape=jax.ShapeDtypeStruct((size, slab_len), jnp.float32),
        in_specs=[hbm, hbm, vmem, vmem],
        out_specs=vmem,
        scratch_shapes=[
            pltpu.VMEM((channels, slab_len), jnp.bfloat16),
            pltpu.VMEM((channels, tmpl_len), jnp.bfloat16),
            pltpu.VMEM((channels, slab_len + up(rim_columns(tmpl_len), LANES)), jnp.bfloat16),
            pltpu.VMEM((2, packed_rows(channels, rim_columns(tmpl_len), 2), LANES), jnp.bfloat16),
            pltpu.VMEM((size, lines, LANES), jnp.bfloat16),
            pltpu.VMEM((BATCH, channels, wide), jnp.float32),
            pltpu.VMEM((BATCH, channels, span), jnp.float32),
            pltpu.VMEM((BATCH, channels, LANES), jnp.float32),
            pltpu.VMEM((up(tmpl_len, LANES), wide), jnp.bfloat16),
            pltpu.VMEM((channels // GROUP, STEP * GROUP, reach), jnp.bfloat16),
            pltpu.VMEM((channels, span), jnp.float32),
            dma((2,)),
            dma((2,)),
            dma((2,)),
            dma((size,)),
            dma((size,)),
        ],
        compiler_params=pltpu.CompilerParams(
            vmem_limit_bytes=62 << 20, collective_id=0, has_side_effects=True
        ),
    )(
        records,
        templates.reshape(channels, tmpl_len),
        channel_mask.reshape(1, channels),
        lag_table.reshape(1, channels),
    )
    return out.reshape(size, 1, slab_len)


def solution(mesh):
    return jax.shard_map(
        local,
        mesh=mesh,
        in_specs=(
            P(None, ("grp", "tm")),
            P(None, "tm", "tmpl", None),
            P(None, "tm", "tmpl"),
            P(None, "tm", "tmpl"),
        ),
        out_specs=P(None, "tmpl", ("grp", "tm")),
        check_vma=False,
    )
```

```python
import jax
import jax.numpy as jnp
from jax import lax
from jax.experimental import pallas as pl
from jax.experimental.pallas import tpu as pltpu
from jax.sharding import PartitionSpec as P

LAGS = 64
LANES = 128
STEP = 32
ROWS = 16
GROUP = 8
BAND = 256
BATCH = 4


def up(value, unit):
    return -(-value // unit) * unit


def shifted_left(values, count):
    width = values.shape[1]
    if count % width == 0:
        return values
    return pltpu.roll(values, width - count % width, 1)


def unroll_of(count, most):
    return max(k for k in range(1, most + 1) if count % k == 0)


def rim_columns(tmpl_len):
    return up(tmpl_len + LAGS - 2, 8)


def remainders(columns):
    parts, begin, left = [], 0, columns % LANES
    width = LANES // 2
    while left:
        if left >= width:
            parts.append((begin, width))
            begin, left = begin + width, left - width
        width //= 2
    return parts


def packed_rows(channels, columns, shares):
    blocks = channels // ROWS
    rows = columns // LANES * channels
    for _, width in remainders(columns):
        rows += -(-blocks // (LANES // width)) * ROWS
    return up(rows, ROWS * shares)


def code_place(channels, columns):
    blocks = channels // ROWS
    rows = packed_rows(channels, columns, 1)
    parts = remainders(columns)
    if parts:
        side = LANES // parts[-1][1]
        used = (blocks % side or side) * parts[-1][1]
        if channels <= (LANES - used) * ROWS:
            return rows - ROWS, used, LANES - used
    return rows, 0, LANES


def put_codes(code, line, lane0, per):
    channels = code.shape[1]
    width = up(channels, LANES)
    code = jnp.concatenate([code, jnp.zeros((1, width - channels), jnp.float32)], axis=1)
    lane = lax.broadcasted_iota(jnp.int32, (ROWS, LANES), 1)
    row = lax.broadcasted_iota(jnp.int32, (ROWS, LANES), 0)
    for r in range(-(-channels // per)):
        part = shifted_left(jnp.broadcast_to(code, (ROWS, width)), (r * per - lane0) % width)[:, :LANES]
        line = jnp.where((row == r) & (lane >= lane0) & (lane < lane0 + per), part, line)
    return line


def get_codes(line, channels, lane0, per):
    width = up(channels, LANES)
    lane = lax.broadcasted_iota(jnp.int32, (1, width), 1)
    code = jnp.zeros((1, width), jnp.float32)
    wide = jnp.concatenate([line, jnp.zeros((ROWS, width - LANES), jnp.float32)], axis=1)
    for r in range(-(-channels // per)):
        part = shifted_left(wide, (lane0 - r * per) % width)[r : r + 1]
        code = jnp.where((lane >= r * per) & (lane < (r + 1) * per), part, code)
    return code[:, :channels]


def pack(values, rows):
    channels, columns = values.shape
    whole = columns // LANES
    blocks = channels // ROWS
    out = [values[:, i * LANES : (i + 1) * LANES] for i in range(whole)]
    if columns % LANES:
        rest = values[:, whole * LANES :].astype(jnp.float32)
        rest = jnp.concatenate([rest, jnp.zeros((channels, LANES - rest.shape[1]), jnp.float32)], axis=1)
        lane = lax.broadcasted_iota(jnp.int32, (ROWS, LANES), 1)
        for begin, width in remainders(columns):
            side = LANES // width
            for first in range(0, blocks, side):
                line = jnp.zeros((ROWS, LANES), jnp.float32)
                for i in range(min(side, blocks - first)):
                    part = rest[(first + i) * ROWS : (first + i + 1) * ROWS]
                    part = shifted_left(part, (begin - i * width) % LANES)
                    line = jnp.where((lane >= i * width) & (lane < (i + 1) * width), part, line)
                out.append(line.astype(values.dtype))
    missing = rows - sum(part.shape[0] for part in out)
    if missing:
        out.append(jnp.zeros((missing, LANES), values.dtype))
    return jnp.concatenate(out, axis=0)


def unpack(values, channels, columns):
    whole = columns // LANES
    blocks = channels // ROWS
    out = [values[i * channels : (i + 1) * channels] for i in range(whole)]
    if columns % LANES:
        lane = lax.broadcasted_iota(jnp.int32, (ROWS, LANES), 1)
        lines = [jnp.zeros((ROWS, LANES), jnp.float32)] * blocks
        row = whole * channels
        for begin, width in remainders(columns):
            side = LANES // width
            for first in range(0, blocks, side):
                line = values[row : row + ROWS].astype(jnp.float32)
                row += ROWS
                for i in range(min(side, blocks - first)):
                    part = shifted_left(line, (i * width - begin) % LANES)
                    here = (lane >= begin) & (lane < begin + width)
                    lines[first + i] = jnp.where(here, part, lines[first + i])
        out.append(jnp.concatenate(lines, axis=0).astype(values.dtype))
    return jnp.concatenate(out, axis=1)


def exchange(rims_ref, slots_ref, sems):
    size = lax.axis_size("tm")
    me, col = lax.axis_index("tm"), lax.axis_index("tmpl")
    mate = col + 1 - 2 * (col % 2)
    half = rims_ref.shape[1] // 2

    def there(axis, index):
        return {"device_id": {axis: index}, "device_id_type": pl.DeviceIdType.MESH}

    def copy(src, dst, name, index, where):
        send, recv = sems[name]
        return pltpu.make_async_remote_copy(
            src_ref=src, dst_ref=dst, send_sem=send.at[index], recv_sem=recv.at[index], **where
        )

    piece = pl.ds(pl.multiple_of((col % 2) * half, ROWS), half)
    barrier = pltpu.get_barrier_semaphore()
    peer = [(me + d) % size for d in range(size)]
    rim = copy(rims_ref.at[0, piece], rims_ref.at[1, piece], "rim", 0, there("tm", jnp.maximum(me - 1, 0)))
    rim_on = copy(rims_ref.at[1, piece], rims_ref.at[1, piece], "rim", 1, there("tmpl", mate))
    row = [None] + [
        copy(slots_ref.at[0], slots_ref.at[d], "tmpl", d, there("tm", peer[d])) for d in range(1, size)
    ]

    def greet():
        for d in range(1, size):
            pl.semaphore_signal(barrier, inc=1, **there("tm", peer[d]))
        pl.semaphore_signal(barrier, inc=1, **there("tmpl", mate))

    def start():
        pl.semaphore_wait(barrier, size)

        @pl.when(me > 0)
        def _():
            rim.start()

        for d in range(1, size):

            @pl.when(me + d < size)
            def _():
                row[d].start()

    def start_back():
        @pl.when(me > 0)
        def _():
            rim.wait_send()

        for d in range(1, size):

            @pl.when(me + d >= size)
            def _():
                row[d].start()

    def land_rim():
        @pl.when(me < size - 1)
        def _():
            rim.wait_recv()
            rim_on.start()
            rim_on.wait_recv()

        @pl.when(me == size - 1)
        def _():
            rims_ref[1] = jnp.zeros(rims_ref.shape[1:], rims_ref.dtype)

    def land_row(d):
        row[d].wait_recv()

    def drain():
        for move in row[1:]:
            move.wait_send()

        @pl.when(me < size - 1)
        def _():
            rim_on.wait_send()

    return greet, start, start_back, land_rim, land_row, drain


def correlate(
    rec_ref,
    tmpl_ref,
    mask_ref,
    lag_ref,
    out_ref,
    kernel_ref,
    masks_ref,
    lags_ref,
    series_ref,
    rims_ref,
    slots_ref,
    wide_ref,
    trace_ref,
    weight_ref,
    spread_ref,
    moved_ref,
    inverse_ref,
    own_sems,
    *sem_refs,
):
    channels, tmpl_len = tmpl_ref.shape
    size = slots_ref.shape[0]
    filled = spread_ref.shape[0]
    rim_len = rim_columns(tmpl_len)
    slab_len = rec_ref.shape[1]
    span = trace_ref.shape[2]
    blocks = -(-tmpl_len // STEP)
    wide = blocks * STEP * GROUP
    deep = STEP * GROUP
    reach = moved_ref.shape[2]
    per_tile = LANES // STEP
    me = lax.axis_index("tm")
    names = ("rim", "tmpl")
    sems = {name: sem_refs[2 * i : 2 * i + 2] for i, name in enumerate(names)}
    greet, start, start_back, land_rim, land_row, drain = exchange(
        rims_ref, slots_ref, sems
    )
    greet()
    pairs = (
        (tmpl_ref, kernel_ref),
        (mask_ref, masks_ref),
        (lag_ref, lags_ref),
        (rec_ref, series_ref.at[:, pl.ds(0, slab_len)]),
    )
    fetched = [pltpu.make_async_copy(src, dst, own_sems.at[i]) for i, (src, dst) in enumerate(pairs)]
    for move in fetched:
        move.start()
    line0, lane0, per = code_place(channels, tmpl_len)
    fetched[0].wait()
    packed = pack(kernel_ref[...], packed_rows(channels, tmpl_len, 1))
    slots_ref[0, : packed.shape[0]] = packed
    for move in fetched[1:3]:
        move.wait()
    code = jnp.where(masks_ref[...] != 0, lags_ref[...], -1).astype(jnp.float32)
    line = packed[line0:] if line0 < packed.shape[0] else jnp.zeros((ROWS, LANES), packed.dtype)
    line = put_codes(code, line.astype(jnp.float32), lane0, per)
    slots_ref[0, line0 : line0 + ROWS] = line.astype(packed.dtype)
    fetched[3].wait()
    rims_ref[0] = pack(series_ref[:, :rim_len], rims_ref.shape[1])
    start()

    lane = lax.broadcasted_iota(jnp.int32, (filled, wide), 1)
    sample = lax.broadcasted_iota(jnp.int32, (filled, wide), 0)
    spread_ref[...] = jnp.where(lane // GROUP == sample, 1.0, 0.0).astype(jnp.bfloat16)
    own = lax.broadcasted_iota(jnp.int32, (channels, wide), 1) % GROUP == (
        lax.broadcasted_iota(jnp.int32, (channels, wide), 0) % GROUP
    )
    lag = (LAGS - 1 - lax.broadcasted_iota(jnp.int32, (LAGS, channels), 0)).astype(jnp.float32)

    def expand(n, slot):
        kernel = unpack(slots_ref[n], channels, tmpl_len)
        widened = jnp.dot(kernel, spread_ref[...], preferred_element_type=jnp.float32)
        as_float = kernel.astype(jnp.float32)
        mean = jnp.sum(as_float * as_float, axis=1, keepdims=True) / tmpl_len
        weight = 1.0 / (jnp.sqrt(mean + 1e-05) * tmpl_len)
        wide_ref[slot] = jnp.where(own, widened, 0.0)
        weight_ref[slot] = jnp.broadcast_to(weight, (channels, LANES))

    def scale():
        series_ref[:, slab_len:] = unpack(rims_ref[1], channels, rim_len)
        series = series_ref[...].astype(jnp.float32)
        squares = series * series
        high = squares.astype(jnp.bfloat16)
        low = (squares - high.astype(jnp.float32)).astype(jnp.bfloat16)
        both = jnp.concatenate([high, low], axis=0)
        row = lax.broadcasted_iota(jnp.int32, (BAND, BAND), 0)
        column = lax.broadcasted_iota(jnp.int32, (BAND, BAND), 1)
        bands = []
        for d in range((tmpl_len + BAND - 2) // BAND + 1):
            off = d * BAND + row - column
            bands.append(jnp.where((off >= 0) & (off < tmpl_len), 1.0, 0.0).astype(jnp.bfloat16))
        for n in range(-(-span // BAND)):
            total = None
            for d, band in enumerate(bands):
                part = both[:, (n + d) * BAND : (n + d + 1) * BAND]
                if part.shape[1] == 0:
                    continue
                part = jnp.dot(part, band[: part.shape[1]], preferred_element_type=jnp.float32)
                total = part if total is None else total + part
            energy = total[:channels] + total[channels:]
            here = slice(n * BAND, min((n + 1) * BAND, span))
            inverse_ref[:, here] = lax.rsqrt(energy / tmpl_len + 1e-05)[:, : here.stop - here.start]

    def spread_out(begin, end):
        reads = min(end + LANES, series_ref.shape[1])
        if end + STEP - 1 <= slab_len:
            reads = min(reads, slab_len)

        @pl.loop(0, channels // ROWS, unroll=unroll_of(channels // ROWS, 5))
        def _(pair):
            rows = pl.ds(pl.multiple_of(pair * ROWS, ROWS), ROWS)
            series = series_ref[rows, begin:reads].astype(jnp.float32)
            for side in range(ROWS // GROUP):
                part = series[side * GROUP : (side + 1) * GROUP]
                moved_ref[pair * (ROWS // GROUP) + side, :, begin:end] = jnp.concatenate(
                    [shifted_left(part, b)[:, : end - begin] for b in range(STEP)], axis=0
                ).astype(jnp.bfloat16)

    def traces(batch):
        @pl.loop(0, channels // GROUP, unroll=unroll_of(channels // GROUP, 20))
        def _(group):
            rows = pl.ds(pl.multiple_of(group * GROUP, GROUP), GROUP)
            left = jnp.concatenate(
                [wide_ref[n, rows, a * deep : (a + 1) * deep] for n in range(batch) for a in range(blocks)],
                axis=0,
            ).astype(jnp.bfloat16)
            partial = jnp.dot(left, moved_ref[group], preferred_element_type=jnp.float32)
            inverse_rms = inverse_ref[rows, :]
            for n in range(batch):
                total = None
                for phase in range(min(per_tile, blocks)):
                    lined = None
                    for a in range(phase, blocks, per_tile):
                        begin = (a - phase) * STEP
                        line = (n * blocks + a) * GROUP
                        piece = partial[line : line + GROUP, begin : begin + span + LANES]
                        if piece.shape[1] < span + LANES:
                            missing = span + LANES - piece.shape[1]
                            piece = jnp.concatenate(
                                [piece, jnp.zeros((GROUP, missing), jnp.float32)], axis=1
                            )
                        lined = piece if lined is None else lined + piece
                    lined = shifted_left(lined, phase * STEP)[:, :span]
                    total = lined if total is None else total + lined
                weight = jnp.concatenate([weight_ref[n, rows, :]] * (span // LANES), axis=1)
                trace_ref[n, rows, :] = total * inverse_rms * weight

    def stack(n, slot):
        line = slots_ref[n, line0 : line0 + ROWS].astype(jnp.float32)
        pick = jnp.where(get_codes(line, channels, lane0, per) == lag, 1.0, 0.0).astype(jnp.bfloat16)
        trace = trace_ref[slot]
        high = trace.astype(jnp.bfloat16)
        low = (trace - high.astype(jnp.float32)).astype(jnp.bfloat16)
        by_lag = jnp.dot(pick, high, preferred_element_type=jnp.float32)
        by_lag += jnp.dot(pick, low, preferred_element_type=jnp.float32)
        lined = pltpu.roll(by_lag, span - LAGS + 1, 1, stride=1, stride_axis=0)
        out_ref[(me + size - n) % size] = jnp.sum(lined, axis=0, keepdims=True)[:, :slab_len]

    def rows_of(first, batch):
        for n in range(batch):
            expand(first + n, n)
        traces(batch)
        for n in range(batch):
            stack(first + n, n)

    batch = min(BATCH, size)
    if batch == size:
        expand(0, 0)
    start_back()
    ready = (slab_len - STEP + 1) // LANES * LANES
    if ready:
        spread_out(0, ready)
    land_rim()
    scale()
    spread_out(ready, reach)
    if batch == size:
        for d in range(1, size):
            land_row(d)
            expand(d, d)
        traces(size)
        for d in range(size):
            stack(d, d)
    else:
        for d in range(1, size):
            land_row(d)

        @pl.loop(0, size // batch)
        def _(turn):
            rows_of(turn * batch, batch)

        if size % batch:
            rows_of(size - size % batch, size % batch)
    drain()


def local(records, templates, channel_mask, lag_table):
    channels, slab_len = records.shape
    first, second, tmpl_len = templates.shape[1:]
    assert first == 1 and second == 1
    size = lax.axis_size("tm")
    span = up(slab_len + LAGS - 1, LANES)
    blocks = -(-tmpl_len // STEP)
    wide = blocks * STEP * GROUP
    reach = up(slab_len + LAGS - 1 + (blocks - 1) * STEP, LANES)
    lines = max(packed_rows(channels, tmpl_len, 1), code_place(channels, tmpl_len)[0] + ROWS)
    dma = pltpu.SemaphoreType.DMA
    hbm, vmem = pl.BlockSpec(memory_space=pltpu.HBM), pl.BlockSpec(memory_space=pltpu.VMEM)
    out = pl.pallas_call(
        correlate,
        out_shape=jax.ShapeDtypeStruct((size, 1, slab_len), jnp.float32),
        in_specs=[hbm] * 4,
        out_specs=vmem,
        scratch_shapes=[
            pltpu.VMEM((channels, tmpl_len), jnp.bfloat16),
            pltpu.VMEM((1, channels), jnp.int32),
            pltpu.VMEM((1, channels), jnp.int32),
            pltpu.VMEM((channels, slab_len + up(rim_columns(tmpl_len), LANES)), jnp.bfloat16),
            pltpu.VMEM((2, packed_rows(channels, rim_columns(tmpl_len), 2), LANES), jnp.bfloat16),
            pltpu.VMEM((size, lines, LANES), jnp.bfloat16),
            pltpu.VMEM((BATCH, channels, wide), jnp.float32),
            pltpu.VMEM((BATCH, channels, span), jnp.float32),
            pltpu.VMEM((BATCH, channels, LANES), jnp.float32),
            pltpu.VMEM((up(tmpl_len, LANES), wide), jnp.bfloat16),
            pltpu.VMEM((channels // GROUP, STEP * GROUP, reach), jnp.bfloat16),
            pltpu.VMEM((channels, span), jnp.float32),
            dma((4,)),
            dma((2,)),
            dma((2,)),
            dma((size,)),
            dma((size,)),
        ],
        compiler_params=pltpu.CompilerParams(
            vmem_limit_bytes=62 << 20, collective_id=0, has_side_effects=True
        ),
    )(
        records,
        templates.reshape(channels, tmpl_len),
        channel_mask.reshape(1, channels),
        lag_table.reshape(1, channels),
    )
    return out


def solution(mesh):
    return jax.shard_map(
        local,
        mesh=mesh,
        in_specs=(
            P(None, ("grp", "tm")),
            P(None, "tm", "tmpl", None),
            P(None, "tm", "tmpl"),
            P(None, "tm", "tmpl"),
        ),
        out_specs=P(None, "tmpl", ("grp", "tm")),
        check_vma=False,
    )
```

```python
import jax
import jax.numpy as jnp
from jax import lax
from jax.experimental import pallas as pl
from jax.experimental.pallas import tpu as pltpu
from jax.sharding import PartitionSpec as P

LAGS = 64
LANES = 128
STEP = 32
ROWS = 16
GROUP = 8
BAND = 256
BATCH = 4


def up(value, unit):
    return -(-value // unit) * unit


def shifted_left(values, count):
    width = values.shape[1]
    if count % width == 0:
        return values
    return pltpu.roll(values, width - count % width, 1)


def unroll_of(count, most):
    return max(k for k in range(1, most + 1) if count % k == 0)


def rim_columns(tmpl_len):
    return up(tmpl_len + LAGS - 2, 8)


def remainders(columns):
    parts, begin, left = [], 0, columns % LANES
    width = LANES // 2
    while left:
        if left >= width:
            parts.append((begin, width))
            begin, left = begin + width, left - width
        width //= 2
    return parts


def packed_rows(channels, columns, shares):
    blocks = channels // ROWS
    rows = columns // LANES * channels
    for _, width in remainders(columns):
        rows += -(-blocks // (LANES // width)) * ROWS
    return up(rows, ROWS * shares)


def code_place(channels, columns):
    blocks = channels // ROWS
    rows = packed_rows(channels, columns, 1)
    parts = remainders(columns)
    if parts:
        side = LANES // parts[-1][1]
        used = (blocks % side or side) * parts[-1][1]
        if channels <= (LANES - used) * ROWS:
            return rows - ROWS, used, LANES - used
    return rows, 0, LANES


def put_codes(code, line, lane0, per):
    channels = code.shape[1]
    width = up(channels, LANES)
    code = jnp.concatenate([code, jnp.zeros((1, width - channels), jnp.float32)], axis=1)
    lane = lax.broadcasted_iota(jnp.int32, (ROWS, LANES), 1)
    row = lax.broadcasted_iota(jnp.int32, (ROWS, LANES), 0)
    for r in range(-(-channels // per)):
        part = shifted_left(jnp.broadcast_to(code, (ROWS, width)), (r * per - lane0) % width)[:, :LANES]
        line = jnp.where((row == r) & (lane >= lane0) & (lane < lane0 + per), part, line)
    return line


def get_codes(line, channels, lane0, per):
    width = up(channels, LANES)
    lane = lax.broadcasted_iota(jnp.int32, (1, width), 1)
    code = jnp.zeros((1, width), jnp.float32)
    wide = jnp.concatenate([line, jnp.zeros((ROWS, width - LANES), jnp.float32)], axis=1)
    for r in range(-(-channels // per)):
        part = shifted_left(wide, (lane0 - r * per) % width)[r : r + 1]
        code = jnp.where((lane >= r * per) & (lane < (r + 1) * per), part, code)
    return code[:, :channels]


def pack(values, rows):
    channels, columns = values.shape
    whole = columns // LANES
    blocks = channels // ROWS
    out = [values[:, i * LANES : (i + 1) * LANES] for i in range(whole)]
    if columns % LANES:
        rest = values[:, whole * LANES :].astype(jnp.float32)
        rest = jnp.concatenate([rest, jnp.zeros((channels, LANES - rest.shape[1]), jnp.float32)], axis=1)
        lane = lax.broadcasted_iota(jnp.int32, (ROWS, LANES), 1)
        for begin, width in remainders(columns):
            side = LANES // width
            for first in range(0, blocks, side):
                line = jnp.zeros((ROWS, LANES), jnp.float32)
                for i in range(min(side, blocks - first)):
                    part = rest[(first + i) * ROWS : (first + i + 1) * ROWS]
                    part = shifted_left(part, (begin - i * width) % LANES)
                    line = jnp.where((lane >= i * width) & (lane < (i + 1) * width), part, line)
                out.append(line.astype(values.dtype))
    missing = rows - sum(part.shape[0] for part in out)
    if missing:
        out.append(jnp.zeros((missing, LANES), values.dtype))
    return jnp.concatenate(out, axis=0)


def unpack(values, channels, columns):
    whole = columns // LANES
    blocks = channels // ROWS
    out = [values[i * channels : (i + 1) * channels] for i in range(whole)]
    if columns % LANES:
        lane = lax.broadcasted_iota(jnp.int32, (ROWS, LANES), 1)
        lines = [jnp.zeros((ROWS, LANES), jnp.float32)] * blocks
        row = whole * channels
        for begin, width in remainders(columns):
            side = LANES // width
            for first in range(0, blocks, side):
                line = values[row : row + ROWS].astype(jnp.float32)
                row += ROWS
                for i in range(min(side, blocks - first)):
                    part = shifted_left(line, (i * width - begin) % LANES)
                    here = (lane >= begin) & (lane < begin + width)
                    lines[first + i] = jnp.where(here, part, lines[first + i])
        out.append(jnp.concatenate(lines, axis=0).astype(values.dtype))
    return jnp.concatenate(out, axis=1)


def exchange(rims_ref, slots_ref, sems):
    size = lax.axis_size("tm")
    me, col = lax.axis_index("tm"), lax.axis_index("tmpl")
    mate = col + 1 - 2 * (col % 2)
    half = rims_ref.shape[1] // 2

    def there(axis, index):
        return {"device_id": {axis: index}, "device_id_type": pl.DeviceIdType.MESH}

    def copy(src, dst, name, index, where):
        send, recv = sems[name]
        return pltpu.make_async_remote_copy(
            src_ref=src, dst_ref=dst, send_sem=send.at[index], recv_sem=recv.at[index], **where
        )

    piece = pl.ds(pl.multiple_of((col % 2) * half, ROWS), half)
    barrier = pltpu.get_barrier_semaphore()
    peer = [(me + d) % size for d in range(size)]
    rim = copy(rims_ref.at[0, piece], rims_ref.at[1, piece], "rim", 0, there("tm", jnp.maximum(me - 1, 0)))
    rim_on = copy(rims_ref.at[1, piece], rims_ref.at[1, piece], "rim", 1, there("tmpl", mate))
    row = [None] + [
        copy(slots_ref.at[0], slots_ref.at[d], "tmpl", d, there("tm", peer[d])) for d in range(1, size)
    ]

    def greet():
        for d in range(1, size):
            pl.semaphore_signal(barrier, inc=1, **there("tm", peer[d]))
        pl.semaphore_signal(barrier, inc=1, **there("tmpl", mate))

    def start():
        pl.semaphore_wait(barrier, size)

        @pl.when(me > 0)
        def _():
            rim.start()

        for d in range(1, size):

            @pl.when(me + d < size)
            def _():
                row[d].start()

    def start_back():
        @pl.when(me > 0)
        def _():
            rim.wait_send()

        for d in range(1, size):

            @pl.when(me + d == size)
            def _():
                row[d].start()

    def start_rest():
        for d in range(1, size):

            @pl.when(me + d == size)
            def _():
                row[d].wait_send()

        for d in range(1, size):

            @pl.when(me + d > size)
            def _():
                row[d].start()

    def land_rim():
        @pl.when(me < size - 1)
        def _():
            rim.wait_recv()
            rim_on.start()
            rim_on.wait_recv()

        @pl.when(me == size - 1)
        def _():
            rims_ref[1] = jnp.zeros(rims_ref.shape[1:], rims_ref.dtype)

    def land_row(d):
        row[d].wait_recv()

    def drain():
        for d in range(1, size):

            @pl.when(me + d != size)
            def _():
                row[d].wait_send()

        @pl.when(me < size - 1)
        def _():
            rim_on.wait_send()

    return greet, start, start_back, start_rest, land_rim, land_row, drain


def correlate(
    rec_ref,
    tmpl_ref,
    mask_ref,
    lag_ref,
    out_ref,
    kernel_ref,
    masks_ref,
    lags_ref,
    series_ref,
    rims_ref,
    slots_ref,
    wide_ref,
    trace_ref,
    weight_ref,
    spread_ref,
    moved_ref,
    inverse_ref,
    own_sems,
    *sem_refs,
):
    channels, tmpl_len = tmpl_ref.shape
    size = slots_ref.shape[0]
    filled = spread_ref.shape[0]
    rim_len = rim_columns(tmpl_len)
    slab_len = rec_ref.shape[1]
    span = trace_ref.shape[2]
    blocks = -(-tmpl_len // STEP)
    wide = blocks * STEP * GROUP
    deep = STEP * GROUP
    reach = moved_ref.shape[2]
    per_tile = LANES // STEP
    me = lax.axis_index("tm")
    names = ("rim", "tmpl")
    sems = {name: sem_refs[2 * i : 2 * i + 2] for i, name in enumerate(names)}
    greet, start, start_back, start_rest, land_rim, land_row, drain = exchange(
        rims_ref, slots_ref, sems
    )
    greet()
    pairs = (
        (tmpl_ref, kernel_ref),
        (mask_ref, masks_ref),
        (lag_ref, lags_ref),
        (rec_ref, series_ref.at[:, pl.ds(0, slab_len)]),
    )
    fetched = [pltpu.make_async_copy(src, dst, own_sems.at[i]) for i, (src, dst) in enumerate(pairs)]
    for move in fetched:
        move.start()
    line0, lane0, per = code_place(channels, tmpl_len)
    fetched[0].wait()
    packed = pack(kernel_ref[...], packed_rows(channels, tmpl_len, 1))
    slots_ref[0, : packed.shape[0]] = packed
    for move in fetched[1:3]:
        move.wait()
    code = jnp.where(masks_ref[...] != 0, lags_ref[...], -1).astype(jnp.float32)
    line = packed[line0:] if line0 < packed.shape[0] else jnp.zeros((ROWS, LANES), packed.dtype)
    line = put_codes(code, line.astype(jnp.float32), lane0, per)
    slots_ref[0, line0 : line0 + ROWS] = line.astype(packed.dtype)
    fetched[3].wait()
    rims_ref[0] = pack(series_ref[:, :rim_len], rims_ref.shape[1])
    start()

    lane = lax.broadcasted_iota(jnp.int32, (filled, wide), 1)
    sample = lax.broadcasted_iota(jnp.int32, (filled, wide), 0)
    spread_ref[...] = jnp.where(lane // GROUP == sample, 1.0, 0.0).astype(jnp.bfloat16)
    own = lax.broadcasted_iota(jnp.int32, (channels, wide), 1) % GROUP == (
        lax.broadcasted_iota(jnp.int32, (channels, wide), 0) % GROUP
    )
    lag = (LAGS - 1 - lax.broadcasted_iota(jnp.int32, (LAGS, channels), 0)).astype(jnp.float32)

    def expand(n, slot):
        kernel = unpack(slots_ref[n], channels, tmpl_len)
        widened = jnp.dot(kernel, spread_ref[...], preferred_element_type=jnp.float32)
        as_float = kernel.astype(jnp.float32)
        mean = jnp.sum(as_float * as_float, axis=1, keepdims=True) / tmpl_len
        weight = 1.0 / (jnp.sqrt(mean + 1e-05) * tmpl_len)
        wide_ref[slot] = jnp.where(own, widened, 0.0)
        weight_ref[slot] = jnp.broadcast_to(weight, (channels, LANES))

    def scale():
        series_ref[:, slab_len:] = unpack(rims_ref[1], channels, rim_len)
        series = series_ref[...].astype(jnp.float32)
        squares = series * series
        high = squares.astype(jnp.bfloat16)
        low = (squares - high.astype(jnp.float32)).astype(jnp.bfloat16)
        both = jnp.concatenate([high, low], axis=0)
        row = lax.broadcasted_iota(jnp.int32, (BAND, BAND), 0)
        column = lax.broadcasted_iota(jnp.int32, (BAND, BAND), 1)
        bands = []
        for d in range((tmpl_len + BAND - 2) // BAND + 1):
            off = d * BAND + row - column
            bands.append(jnp.where((off >= 0) & (off < tmpl_len), 1.0, 0.0).astype(jnp.bfloat16))
        for n in range(-(-span // BAND)):
            total = None
            for d, band in enumerate(bands):
                part = both[:, (n + d) * BAND : (n + d + 1) * BAND]
                if part.shape[1] == 0:
                    continue
                part = jnp.dot(part, band[: part.shape[1]], preferred_element_type=jnp.float32)
                total = part if total is None else total + part
            energy = total[:channels] + total[channels:]
            here = slice(n * BAND, min((n + 1) * BAND, span))
            inverse_ref[:, here] = lax.rsqrt(energy / tmpl_len + 1e-05)[:, : here.stop - here.start]

    def spread_out(begin, end):
        reads = min(end + LANES, series_ref.shape[1])
        if end + STEP - 1 <= slab_len:
            reads = min(reads, slab_len)

        @pl.loop(0, channels // ROWS, unroll=unroll_of(channels // ROWS, 5))
        def _(pair):
            rows = pl.ds(pl.multiple_of(pair * ROWS, ROWS), ROWS)
            series = series_ref[rows, begin:reads].astype(jnp.float32)
            for side in range(ROWS // GROUP):
                part = series[side * GROUP : (side + 1) * GROUP]
                moved_ref[pair * (ROWS // GROUP) + side, :, begin:end] = jnp.concatenate(
                    [shifted_left(part, b)[:, : end - begin] for b in range(STEP)], axis=0
                ).astype(jnp.bfloat16)

    def traces(batch):
        @pl.loop(0, channels // GROUP, unroll=unroll_of(channels // GROUP, 20))
        def _(group):
            rows = pl.ds(pl.multiple_of(group * GROUP, GROUP), GROUP)
            left = jnp.concatenate(
                [wide_ref[n, rows, a * deep : (a + 1) * deep] for n in range(batch) for a in range(blocks)],
                axis=0,
            ).astype(jnp.bfloat16)
            partial = jnp.dot(left, moved_ref[group], preferred_element_type=jnp.float32)
            inverse_rms = inverse_ref[rows, :]
            for n in range(batch):
                total = None
                for phase in range(min(per_tile, blocks)):
                    lined = None
                    for a in range(phase, blocks, per_tile):
                        begin = (a - phase) * STEP
                        line = (n * blocks + a) * GROUP
                        piece = partial[line : line + GROUP, begin : begin + span + LANES]
                        if piece.shape[1] < span + LANES:
                            missing = span + LANES - piece.shape[1]
                            piece = jnp.concatenate(
                                [piece, jnp.zeros((GROUP, missing), jnp.float32)], axis=1
                            )
                        lined = piece if lined is None else lined + piece
                    lined = shifted_left(lined, phase * STEP)[:, :span]
                    total = lined if total is None else total + lined
                weight = jnp.concatenate([weight_ref[n, rows, :]] * (span // LANES), axis=1)
                trace_ref[n, rows, :] = total * inverse_rms * weight

    def stack(n, slot):
        line = slots_ref[n, line0 : line0 + ROWS].astype(jnp.float32)
        pick = jnp.where(get_codes(line, channels, lane0, per) == lag, 1.0, 0.0).astype(jnp.bfloat16)
        trace = trace_ref[slot]
        high = trace.astype(jnp.bfloat16)
        low = (trace - high.astype(jnp.float32)).astype(jnp.bfloat16)
        by_lag = jnp.dot(pick, high, preferred_element_type=jnp.float32)
        by_lag += jnp.dot(pick, low, preferred_element_type=jnp.float32)
        lined = pltpu.roll(by_lag, span - LAGS + 1, 1, stride=1, stride_axis=0)
        out_ref[(me + size - n) % size] = jnp.sum(lined, axis=0, keepdims=True)[:, :slab_len]

    def rows_of(first, batch):
        for n in range(batch):
            expand(first + n, n)
        traces(batch)
        for n in range(batch):
            stack(first + n, n)

    batch = min(BATCH, size)
    if batch == size:
        expand(0, 0)
    start_back()
    ready = (slab_len - STEP + 1) // LANES * LANES
    if ready:
        spread_out(0, ready)
    start_rest()
    land_rim()
    scale()
    spread_out(ready, reach)
    if batch == size:
        for d in range(size - 1, 0, -1):
            land_row(d)
            expand(d, d)
        traces(size)
        for d in range(size):
            stack(d, d)
    else:
        for d in range(1, size):
            land_row(d)

        @pl.loop(0, size // batch)
        def _(turn):
            rows_of(turn * batch, batch)

        if size % batch:
            rows_of(size - size % batch, size % batch)
    drain()


def local(records, templates, channel_mask, lag_table):
    channels, slab_len = records.shape
    first, second, tmpl_len = templates.shape[1:]
    assert first == 1 and second == 1
    size = lax.axis_size("tm")
    span = up(slab_len + LAGS - 1, LANES)
    blocks = -(-tmpl_len // STEP)
    wide = blocks * STEP * GROUP
    reach = up(slab_len + LAGS - 1 + (blocks - 1) * STEP, LANES)
    lines = max(packed_rows(channels, tmpl_len, 1), code_place(channels, tmpl_len)[0] + ROWS)
    dma = pltpu.SemaphoreType.DMA
    hbm, vmem = pl.BlockSpec(memory_space=pltpu.HBM), pl.BlockSpec(memory_space=pltpu.VMEM)
    out = pl.pallas_call(
        correlate,
        out_shape=jax.ShapeDtypeStruct((size, 1, slab_len), jnp.float32),
        in_specs=[hbm] * 4,
        out_specs=vmem,
        scratch_shapes=[
            pltpu.VMEM((channels, tmpl_len), jnp.bfloat16),
            pltpu.VMEM((1, channels), jnp.int32),
            pltpu.VMEM((1, channels), jnp.int32),
            pltpu.VMEM((channels, slab_len + up(rim_columns(tmpl_len), LANES)), jnp.bfloat16),
            pltpu.VMEM((2, packed_rows(channels, rim_columns(tmpl_len), 2), LANES), jnp.bfloat16),
            pltpu.VMEM((size, lines, LANES), jnp.bfloat16),
            pltpu.VMEM((BATCH, channels, wide), jnp.float32),
            pltpu.VMEM((BATCH, channels, span), jnp.float32),
            pltpu.VMEM((BATCH, channels, LANES), jnp.float32),
            pltpu.VMEM((up(tmpl_len, LANES), wide), jnp.bfloat16),
            pltpu.VMEM((channels // GROUP, STEP * GROUP, reach), jnp.bfloat16),
            pltpu.VMEM((channels, span), jnp.float32),
            dma((4,)),
            dma((2,)),
            dma((2,)),
            dma((size,)),
            dma((size,)),
        ],
        compiler_params=pltpu.CompilerParams(
            vmem_limit_bytes=62 << 20, collective_id=0, has_side_effects=True
        ),
    )(
        records,
        templates.reshape(channels, tmpl_len),
        channel_mask.reshape(1, channels),
        lag_table.reshape(1, channels),
    )
    return out


def solution(mesh):
    return jax.shard_map(
        local,
        mesh=mesh,
        in_specs=(
            P(None, ("grp", "tm")),
            P(None, "tm", "tmpl", None),
            P(None, "tm", "tmpl"),
            P(None, "tm", "tmpl"),
        ),
        out_specs=P(None, "tmpl", ("grp", "tm")),
        check_vma=False,
    )
```

```python
import jax
import jax.numpy as jnp
from jax import lax
from jax.experimental import pallas as pl
from jax.experimental.pallas import tpu as pltpu
from jax.sharding import PartitionSpec as P

LAGS = 64
LANES = 128
STEP = 32
ROWS = 16
GROUP = 8
BAND = 256
BATCH = 4


def up(value, unit):
    return -(-value // unit) * unit


def shifted_left(values, count):
    width = values.shape[1]
    if count % width == 0:
        return values
    return pltpu.roll(values, width - count % width, 1)


def unroll_of(count, most):
    return max(k for k in range(1, most + 1) if count % k == 0)


def rim_columns(tmpl_len):
    return up(tmpl_len + LAGS - 2, 8)


def remainders(columns):
    parts, begin, left = [], 0, columns % LANES
    width = LANES // 2
    while left:
        if left >= width:
            parts.append((begin, width))
            begin, left = begin + width, left - width
        width //= 2
    return parts


def packed_rows(channels, columns, shares):
    blocks = channels // ROWS
    rows = columns // LANES * channels
    for _, width in remainders(columns):
        rows += -(-blocks // (LANES // width)) * ROWS
    return up(rows, ROWS * shares)


def code_place(channels, columns):
    blocks = channels // ROWS
    rows = packed_rows(channels, columns, 1)
    parts = remainders(columns)
    if parts:
        side = LANES // parts[-1][1]
        used = (blocks % side or side) * parts[-1][1]
        if channels <= (LANES - used) * ROWS:
            return rows - ROWS, used, LANES - used
    return rows, 0, LANES


def put_codes(code, line, lane0, per):
    channels = code.shape[1]
    width = up(channels, LANES)
    code = jnp.concatenate([code, jnp.zeros((1, width - channels), jnp.float32)], axis=1)
    lane = lax.broadcasted_iota(jnp.int32, (ROWS, LANES), 1)
    row = lax.broadcasted_iota(jnp.int32, (ROWS, LANES), 0)
    for r in range(-(-channels // per)):
        part = shifted_left(jnp.broadcast_to(code, (ROWS, width)), (r * per - lane0) % width)[:, :LANES]
        line = jnp.where((row == r) & (lane >= lane0) & (lane < lane0 + per), part, line)
    return line


def get_codes(line, channels, lane0, per):
    width = up(channels, LANES)
    lane = lax.broadcasted_iota(jnp.int32, (1, width), 1)
    code = jnp.zeros((1, width), jnp.float32)
    wide = jnp.concatenate([line, jnp.zeros((ROWS, width - LANES), jnp.float32)], axis=1)
    for r in range(-(-channels // per)):
        part = shifted_left(wide, (lane0 - r * per) % width)[r : r + 1]
        code = jnp.where((lane >= r * per) & (lane < (r + 1) * per), part, code)
    return code[:, :channels]


def pack(values, rows):
    channels, columns = values.shape
    whole = columns // LANES
    blocks = channels // ROWS
    out = [values[:, i * LANES : (i + 1) * LANES] for i in range(whole)]
    if columns % LANES:
        rest = values[:, whole * LANES :].astype(jnp.float32)
        rest = jnp.concatenate([rest, jnp.zeros((channels, LANES - rest.shape[1]), jnp.float32)], axis=1)
        lane = lax.broadcasted_iota(jnp.int32, (ROWS, LANES), 1)
        for begin, width in remainders(columns):
            side = LANES // width
            for first in range(0, blocks, side):
                line = jnp.zeros((ROWS, LANES), jnp.float32)
                for i in range(min(side, blocks - first)):
                    part = rest[(first + i) * ROWS : (first + i + 1) * ROWS]
                    part = shifted_left(part, (begin - i * width) % LANES)
                    line = jnp.where((lane >= i * width) & (lane < (i + 1) * width), part, line)
                out.append(line.astype(values.dtype))
    missing = rows - sum(part.shape[0] for part in out)
    if missing:
        out.append(jnp.zeros((missing, LANES), values.dtype))
    return jnp.concatenate(out, axis=0)


def unpack(values, channels, columns):
    whole = columns // LANES
    blocks = channels // ROWS
    out = [values[i * channels : (i + 1) * channels] for i in range(whole)]
    if columns % LANES:
        lane = lax.broadcasted_iota(jnp.int32, (ROWS, LANES), 1)
        lines = [jnp.zeros((ROWS, LANES), jnp.float32)] * blocks
        row = whole * channels
        for begin, width in remainders(columns):
            side = LANES // width
            for first in range(0, blocks, side):
                line = values[row : row + ROWS].astype(jnp.float32)
                row += ROWS
                for i in range(min(side, blocks - first)):
                    part = shifted_left(line, (i * width - begin) % LANES)
                    here = (lane >= begin) & (lane < begin + width)
                    lines[first + i] = jnp.where(here, part, lines[first + i])
        out.append(jnp.concatenate(lines, axis=0).astype(values.dtype))
    return jnp.concatenate(out, axis=1)


def exchange(rims_ref, slots_ref, sems):
    size = lax.axis_size("tm")
    me, col = lax.axis_index("tm"), lax.axis_index("tmpl")
    mate = col + 1 - 2 * (col % 2)
    half = rims_ref.shape[1] // 2

    def there(axis, index):
        return {"device_id": {axis: index}, "device_id_type": pl.DeviceIdType.MESH}

    def copy(src, dst, name, index, where):
        send, recv = sems[name]
        return pltpu.make_async_remote_copy(
            src_ref=src, dst_ref=dst, send_sem=send.at[index], recv_sem=recv.at[index], **where
        )

    piece = pl.ds(pl.multiple_of((col % 2) * half, ROWS), half)
    barrier = pltpu.get_barrier_semaphore()
    peer = [(me + d) % size for d in range(size)]
    rim = copy(rims_ref.at[0, piece], rims_ref.at[1, piece], "rim", 0, there("tm", jnp.maximum(me - 1, 0)))
    rim_on = copy(rims_ref.at[1, piece], rims_ref.at[1, piece], "rim", 1, there("tmpl", mate))
    row = [None] + [
        copy(slots_ref.at[0], slots_ref.at[d], "tmpl", d, there("tm", peer[d])) for d in range(1, size)
    ]

    def above(d):
        return me + d < size

    def greet_if(side, d):
        @pl.when(side)
        def _():
            pl.semaphore_signal(barrier, inc=1, **there("tm", peer[d]))

    def greet():
        if size > 1:
            pl.semaphore_signal(barrier, inc=1, **there("tmpl", mate))
        for d in range(1, size):
            greet_if(me == 0, d)

    def start_down():
        @pl.when(me > 0)
        def _():
            pl.semaphore_wait(barrier, me + 1)
            rim.start()
            for d in range(1, size):
                greet_if(above(d), d)
            for d in range(1, size):
                greet_if(jnp.logical_not(above(d)), d)

    def start_up():
        @pl.when(me == 0)
        def _():
            if size > 1:
                pl.semaphore_wait(barrier, size)

        @pl.when((me > 0) & (me < size - 1))
        def _():
            pl.semaphore_wait(barrier, size - 1 - me)

        for d in range(1, size):

            @pl.when(above(d))
            def _():
                row[d].start()

    def start_back():
        @pl.when(me > 0)
        def _():
            rim.wait_send()

        for d in range(1, size):

            @pl.when(me + d >= size)
            def _():
                row[d].start()

    def land_rim():
        @pl.when(me < size - 1)
        def _():
            rim.wait_recv()
            rim_on.start()
            rim_on.wait_recv()

        @pl.when(me == size - 1)
        def _():
            rims_ref[1] = jnp.zeros(rims_ref.shape[1:], rims_ref.dtype)

    def land_row(d):
        row[d].wait_recv()

    def drain():
        for move in row[1:]:
            move.wait_send()

        @pl.when(me < size - 1)
        def _():
            rim_on.wait_send()

    return greet, start_down, start_back, start_up, land_rim, land_row, drain


def correlate(
    rec_ref,
    tmpl_ref,
    mask_ref,
    lag_ref,
    out_ref,
    kernel_ref,
    masks_ref,
    lags_ref,
    series_ref,
    rims_ref,
    slots_ref,
    wide_ref,
    trace_ref,
    weight_ref,
    spread_ref,
    moved_ref,
    inverse_ref,
    own_sems,
    *sem_refs,
):
    channels, tmpl_len = tmpl_ref.shape
    size = slots_ref.shape[0]
    filled = spread_ref.shape[0]
    rim_len = rim_columns(tmpl_len)
    slab_len = rec_ref.shape[1]
    span = trace_ref.shape[2]
    blocks = -(-tmpl_len // STEP)
    wide = blocks * STEP * GROUP
    deep = STEP * GROUP
    reach = moved_ref.shape[2]
    per_tile = LANES // STEP
    me = lax.axis_index("tm")
    names = ("rim", "tmpl")
    sems = {name: sem_refs[2 * i : 2 * i + 2] for i, name in enumerate(names)}
    greet, start_down, start_back, start_up, land_rim, land_row, drain = exchange(
        rims_ref, slots_ref, sems
    )
    greet()
    pairs = (
        (tmpl_ref, kernel_ref),
        (mask_ref, masks_ref),
        (lag_ref, lags_ref),
        (rec_ref, series_ref.at[:, pl.ds(0, slab_len)]),
    )
    fetched = [pltpu.make_async_copy(src, dst, own_sems.at[i]) for i, (src, dst) in enumerate(pairs)]
    for move in fetched:
        move.start()
    line0, lane0, per = code_place(channels, tmpl_len)
    fetched[0].wait()
    packed = pack(kernel_ref[...], packed_rows(channels, tmpl_len, 1))
    slots_ref[0, : packed.shape[0]] = packed
    for move in fetched[1:3]:
        move.wait()
    code = jnp.where(masks_ref[...] != 0, lags_ref[...], -1).astype(jnp.float32)
    line = packed[line0:] if line0 < packed.shape[0] else jnp.zeros((ROWS, LANES), packed.dtype)
    line = put_codes(code, line.astype(jnp.float32), lane0, per)
    slots_ref[0, line0 : line0 + ROWS] = line.astype(packed.dtype)
    fetched[3].wait()
    rims_ref[0] = pack(series_ref[:, :rim_len], rims_ref.shape[1])
    start_down()

    lane = lax.broadcasted_iota(jnp.int32, (filled, wide), 1)
    sample = lax.broadcasted_iota(jnp.int32, (filled, wide), 0)
    spread_ref[...] = jnp.where(lane // GROUP == sample, 1.0, 0.0).astype(jnp.bfloat16)
    own = lax.broadcasted_iota(jnp.int32, (channels, wide), 1) % GROUP == (
        lax.broadcasted_iota(jnp.int32, (channels, wide), 0) % GROUP
    )
    lag = (LAGS - 1 - lax.broadcasted_iota(jnp.int32, (LAGS, channels), 0)).astype(jnp.float32)

    def expand(n, slot):
        kernel = unpack(slots_ref[n], channels, tmpl_len)
        widened = jnp.dot(kernel, spread_ref[...], preferred_element_type=jnp.float32)
        as_float = kernel.astype(jnp.float32)
        mean = jnp.sum(as_float * as_float, axis=1, keepdims=True) / tmpl_len
        weight = 1.0 / (jnp.sqrt(mean + 1e-05) * tmpl_len)
        wide_ref[slot] = jnp.where(own, widened, 0.0)
        weight_ref[slot] = jnp.broadcast_to(weight, (channels, LANES))

    def scale():
        series_ref[:, slab_len:] = unpack(rims_ref[1], channels, rim_len)
        series = series_ref[...].astype(jnp.float32)
        squares = series * series
        high = squares.astype(jnp.bfloat16)
        low = (squares - high.astype(jnp.float32)).astype(jnp.bfloat16)
        both = jnp.concatenate([high, low], axis=0)
        row = lax.broadcasted_iota(jnp.int32, (BAND, BAND), 0)
        column = lax.broadcasted_iota(jnp.int32, (BAND, BAND), 1)
        bands = []
        for d in range((tmpl_len + BAND - 2) // BAND + 1):
            off = d * BAND + row - column
            bands.append(jnp.where((off >= 0) & (off < tmpl_len), 1.0, 0.0).astype(jnp.bfloat16))
        for n in range(-(-span // BAND)):
            total = None
            for d, band in enumerate(bands):
                part = both[:, (n + d) * BAND : (n + d + 1) * BAND]
                if part.shape[1] == 0:
                    continue
                part = jnp.dot(part, band[: part.shape[1]], preferred_element_type=jnp.float32)
                total = part if total is None else total + part
            energy = total[:channels] + total[channels:]
            here = slice(n * BAND, min((n + 1) * BAND, span))
            inverse_ref[:, here] = lax.rsqrt(energy / tmpl_len + 1e-05)[:, : here.stop - here.start]

    def spread_out(begin, end):
        reads = min(end + LANES, series_ref.shape[1])
        if end + STEP - 1 <= slab_len:
            reads = min(reads, slab_len)

        @pl.loop(0, channels // ROWS, unroll=unroll_of(channels // ROWS, 5))
        def _(pair):
            rows = pl.ds(pl.multiple_of(pair * ROWS, ROWS), ROWS)
            series = series_ref[rows, begin:reads].astype(jnp.float32)
            for side in range(ROWS // GROUP):
                part = series[side * GROUP : (side + 1) * GROUP]
                moved_ref[pair * (ROWS // GROUP) + side, :, begin:end] = jnp.concatenate(
                    [shifted_left(part, b)[:, : end - begin] for b in range(STEP)], axis=0
                ).astype(jnp.bfloat16)

    def traces(batch):
        @pl.loop(0, channels // GROUP, unroll=unroll_of(channels // GROUP, 20))
        def _(group):
            rows = pl.ds(pl.multiple_of(group * GROUP, GROUP), GROUP)
            left = jnp.concatenate(
                [wide_ref[n, rows, a * deep : (a + 1) * deep] for n in range(batch) for a in range(blocks)],
                axis=0,
            ).astype(jnp.bfloat16)
            partial = jnp.dot(left, moved_ref[group], preferred_element_type=jnp.float32)
            inverse_rms = inverse_ref[rows, :]
            for n in range(batch):
                total = None
                for phase in range(min(per_tile, blocks)):
                    lined = None
                    for a in range(phase, blocks, per_tile):
                        begin = (a - phase) * STEP
                        line = (n * blocks + a) * GROUP
                        piece = partial[line : line + GROUP, begin : begin + span + LANES]
                        if piece.shape[1] < span + LANES:
                            missing = span + LANES - piece.shape[1]
                            piece = jnp.concatenate(
                                [piece, jnp.zeros((GROUP, missing), jnp.float32)], axis=1
                            )
                        lined = piece if lined is None else lined + piece
                    lined = shifted_left(lined, phase * STEP)[:, :span]
                    total = lined if total is None else total + lined
                weight = jnp.concatenate([weight_ref[n, rows, :]] * (span // LANES), axis=1)
                trace_ref[n, rows, :] = total * inverse_rms * weight

    def stack(n, slot):
        line = slots_ref[n, line0 : line0 + ROWS].astype(jnp.float32)
        pick = jnp.where(get_codes(line, channels, lane0, per) == lag, 1.0, 0.0).astype(jnp.bfloat16)
        trace = trace_ref[slot]
        high = trace.astype(jnp.bfloat16)
        low = (trace - high.astype(jnp.float32)).astype(jnp.bfloat16)
        by_lag = jnp.dot(pick, high, preferred_element_type=jnp.float32)
        by_lag += jnp.dot(pick, low, preferred_element_type=jnp.float32)
        lined = pltpu.roll(by_lag, span - LAGS + 1, 1, stride=1, stride_axis=0)
        out_ref[(me + size - n) % size] = jnp.sum(lined, axis=0, keepdims=True)[:, :slab_len]

    def rows_of(first, batch):
        for n in range(batch):
            expand(first + n, n)
        traces(batch)
        for n in range(batch):
            stack(first + n, n)

    batch = min(BATCH, size)
    if batch == size:
        expand(0, 0)
    start_back()
    ready = (slab_len - STEP + 1) // LANES * LANES
    if ready:
        spread_out(0, ready)
    start_up()
    land_rim()
    scale()
    spread_out(ready, reach)
    if batch == size:
        for d in range(1, size):
            land_row(d)
            expand(d, d)
        traces(size)
        for d in range(size):
            stack(d, d)
    else:
        for d in range(1, size):
            land_row(d)

        @pl.loop(0, size // batch)
        def _(turn):
            rows_of(turn * batch, batch)

        if size % batch:
            rows_of(size - size % batch, size % batch)
    drain()


def local(records, templates, channel_mask, lag_table):
    channels, slab_len = records.shape
    first, second, tmpl_len = templates.shape[1:]
    assert first == 1 and second == 1
    size = lax.axis_size("tm")
    span = up(slab_len + LAGS - 1, LANES)
    blocks = -(-tmpl_len // STEP)
    wide = blocks * STEP * GROUP
    reach = up(slab_len + LAGS - 1 + (blocks - 1) * STEP, LANES)
    lines = max(packed_rows(channels, tmpl_len, 1), code_place(channels, tmpl_len)[0] + ROWS)
    dma = pltpu.SemaphoreType.DMA
    hbm, vmem = pl.BlockSpec(memory_space=pltpu.HBM), pl.BlockSpec(memory_space=pltpu.VMEM)
    out = pl.pallas_call(
        correlate,
        out_shape=jax.ShapeDtypeStruct((size, 1, slab_len), jnp.float32),
        in_specs=[hbm] * 4,
        out_specs=vmem,
        scratch_shapes=[
            pltpu.VMEM((channels, tmpl_len), jnp.bfloat16),
            pltpu.VMEM((1, channels), jnp.int32),
            pltpu.VMEM((1, channels), jnp.int32),
            pltpu.VMEM((channels, slab_len + up(rim_columns(tmpl_len), LANES)), jnp.bfloat16),
            pltpu.VMEM((2, packed_rows(channels, rim_columns(tmpl_len), 2), LANES), jnp.bfloat16),
            pltpu.VMEM((size, lines, LANES), jnp.bfloat16),
            pltpu.VMEM((BATCH, channels, wide), jnp.float32),
            pltpu.VMEM((BATCH, channels, span), jnp.float32),
            pltpu.VMEM((BATCH, channels, LANES), jnp.float32),
            pltpu.VMEM((up(tmpl_len, LANES), wide), jnp.bfloat16),
            pltpu.VMEM((channels // GROUP, STEP * GROUP, reach), jnp.bfloat16),
            pltpu.VMEM((channels, span), jnp.float32),
            dma((4,)),
            dma((2,)),
            dma((2,)),
            dma((size,)),
            dma((size,)),
        ],
        compiler_params=pltpu.CompilerParams(
            vmem_limit_bytes=62 << 20, collective_id=0, has_side_effects=True
        ),
    )(
        records,
        templates.reshape(channels, tmpl_len),
        channel_mask.reshape(1, channels),
        lag_table.reshape(1, channels),
    )
    return out


def solution(mesh):
    return jax.shard_map(
        local,
        mesh=mesh,
        in_specs=(
            P(None, ("grp", "tm")),
            P(None, "tm", "tmpl", None),
            P(None, "tm", "tmpl"),
            P(None, "tm", "tmpl"),
        ),
        out_specs=P(None, "tmpl", ("grp", "tm")),
        check_vma=False,
    )
```

```python
import jax
import jax.numpy as jnp
from jax import lax
from jax.experimental import pallas as pl
from jax.experimental.pallas import tpu as pltpu
from jax.sharding import PartitionSpec as P

LAGS = 64
LANES = 128
STEP = 32
ROWS = 16
GROUP = 8
BAND = 256
BATCH = 4


def up(value, unit):
    return -(-value // unit) * unit


def shifted_left(values, count):
    width = values.shape[1]
    if count % width == 0:
        return values
    return pltpu.roll(values, width - count % width, 1)


def unroll_of(count, most):
    return max(k for k in range(1, most + 1) if count % k == 0)


def rim_columns(tmpl_len):
    return up(tmpl_len + LAGS - 2, 8)


def remainders(columns):
    parts, begin, left = [], 0, columns % LANES
    width = LANES // 2
    while left:
        if left >= width:
            parts.append((begin, width))
            begin, left = begin + width, left - width
        width //= 2
    return parts


def packed_rows(channels, columns, shares):
    blocks = channels // ROWS
    rows = columns // LANES * channels
    for _, width in remainders(columns):
        rows += -(-blocks // (LANES // width)) * ROWS
    return up(rows, ROWS * shares)


def code_place(channels, columns):
    blocks = channels // ROWS
    rows = packed_rows(channels, columns, 1)
    parts = remainders(columns)
    if parts:
        side = LANES // parts[-1][1]
        used = (blocks % side or side) * parts[-1][1]
        if channels <= (LANES - used) * ROWS:
            return rows - ROWS, used, LANES - used
    return rows, 0, LANES


def put_codes(code, line, lane0, per):
    channels = code.shape[1]
    width = up(channels, LANES)
    code = jnp.concatenate([code, jnp.zeros((1, width - channels), jnp.float32)], axis=1)
    lane = lax.broadcasted_iota(jnp.int32, (ROWS, LANES), 1)
    row = lax.broadcasted_iota(jnp.int32, (ROWS, LANES), 0)
    for r in range(-(-channels // per)):
        part = shifted_left(jnp.broadcast_to(code, (ROWS, width)), (r * per - lane0) % width)[:, :LANES]
        line = jnp.where((row == r) & (lane >= lane0) & (lane < lane0 + per), part, line)
    return line


def get_codes(line, channels, lane0, per):
    width = up(channels, LANES)
    lane = lax.broadcasted_iota(jnp.int32, (1, width), 1)
    code = jnp.zeros((1, width), jnp.float32)
    wide = jnp.concatenate([line, jnp.zeros((ROWS, width - LANES), jnp.float32)], axis=1)
    for r in range(-(-channels // per)):
        part = shifted_left(wide, (lane0 - r * per) % width)[r : r + 1]
        code = jnp.where((lane >= r * per) & (lane < (r + 1) * per), part, code)
    return code[:, :channels]


def pack(values, rows):
    channels, columns = values.shape
    whole = columns // LANES
    blocks = channels // ROWS
    out = [values[:, i * LANES : (i + 1) * LANES] for i in range(whole)]
    if columns % LANES:
        rest = values[:, whole * LANES :].astype(jnp.float32)
        rest = jnp.concatenate([rest, jnp.zeros((channels, LANES - rest.shape[1]), jnp.float32)], axis=1)
        lane = lax.broadcasted_iota(jnp.int32, (ROWS, LANES), 1)
        for begin, width in remainders(columns):
            side = LANES // width
            for first in range(0, blocks, side):
                line = jnp.zeros((ROWS, LANES), jnp.float32)
                for i in range(min(side, blocks - first)):
                    part = rest[(first + i) * ROWS : (first + i + 1) * ROWS]
                    part = shifted_left(part, (begin - i * width) % LANES)
                    line = jnp.where((lane >= i * width) & (lane < (i + 1) * width), part, line)
                out.append(line.astype(values.dtype))
    missing = rows - sum(part.shape[0] for part in out)
    if missing:
        out.append(jnp.zeros((missing, LANES), values.dtype))
    return jnp.concatenate(out, axis=0)


def unpack(values, channels, columns):
    whole = columns // LANES
    blocks = channels // ROWS
    out = [values[i * channels : (i + 1) * channels] for i in range(whole)]
    if columns % LANES:
        lane = lax.broadcasted_iota(jnp.int32, (ROWS, LANES), 1)
        lines = [jnp.zeros((ROWS, LANES), jnp.float32)] * blocks
        row = whole * channels
        for begin, width in remainders(columns):
            side = LANES // width
            for first in range(0, blocks, side):
                line = values[row : row + ROWS].astype(jnp.float32)
                row += ROWS
                for i in range(min(side, blocks - first)):
                    part = shifted_left(line, (i * width - begin) % LANES)
                    here = (lane >= begin) & (lane < begin + width)
                    lines[first + i] = jnp.where(here, part, lines[first + i])
        out.append(jnp.concatenate(lines, axis=0).astype(values.dtype))
    return jnp.concatenate(out, axis=1)


def exchange(rims_ref, slots_ref, sems):
    size = lax.axis_size("tm")
    me, col = lax.axis_index("tm"), lax.axis_index("tmpl")
    mate = col + 1 - 2 * (col % 2)
    half = rims_ref.shape[1] // 2

    def there(axis, index):
        return {"device_id": {axis: index}, "device_id_type": pl.DeviceIdType.MESH}

    def copy(src, dst, name, index, where):
        send, recv = sems[name]
        return pltpu.make_async_remote_copy(
            src_ref=src, dst_ref=dst, send_sem=send.at[index], recv_sem=recv.at[index], **where
        )

    piece = pl.ds(pl.multiple_of((col % 2) * half, ROWS), half)
    barrier = pltpu.get_barrier_semaphore()
    peer = [(me + d) % size for d in range(size)]
    rim = copy(rims_ref.at[0, piece], rims_ref.at[1, piece], "rim", 0, there("tm", jnp.maximum(me - 1, 0)))
    rim_on = copy(rims_ref.at[1, piece], rims_ref.at[1, piece], "rim", 1, there("tmpl", mate))
    row = [None] + [
        copy(slots_ref.at[0], slots_ref.at[d], "tmpl", d, there("tm", peer[d])) for d in range(1, size)
    ]

    def above(d):
        return me + d < size

    def greet_if(side, d):
        @pl.when(side)
        def _():
            pl.semaphore_signal(barrier, inc=1, **there("tm", peer[d]))

    def greet():
        if size > 1:
            pl.semaphore_signal(barrier, inc=1, **there("tmpl", mate))
        for d in range(1, size):
            greet_if(me == 0, d)

    def start_down():
        @pl.when(me > 0)
        def _():
            pl.semaphore_wait(barrier, me + 1)
            rim.start()
            for d in range(1, size):
                greet_if(above(d), d)
            for d in range(1, size):
                greet_if(jnp.logical_not(above(d)), d)

    def start_up():
        @pl.when(me == 0)
        def _():
            if size > 1:
                pl.semaphore_wait(barrier, size)

        @pl.when((me > 0) & (me < size - 1))
        def _():
            pl.semaphore_wait(barrier, size - 1 - me)

        for d in range(1, size):

            @pl.when(above(d))
            def _():
                row[d].start()

    def start_back():
        @pl.when(me > 0)
        def _():
            rim.wait_send()

        for d in range(1, size):

            @pl.when(me + d >= size)
            def _():
                row[d].start()

    def land_rim():
        @pl.when(me < size - 1)
        def _():
            rim.wait_recv()
            rim_on.start()
            rim_on.wait_recv()

        @pl.when(me == size - 1)
        def _():
            rims_ref[1] = jnp.zeros(rims_ref.shape[1:], rims_ref.dtype)

    def land_row(d):
        copy(slots_ref.at[0], slots_ref.at[d], "tmpl", d, there("tm", peer[1])).wait_recv()

    def drain():
        for move in row[1:]:
            move.wait_send()

        @pl.when(me < size - 1)
        def _():
            rim_on.wait_send()

    return greet, start_down, start_back, start_up, land_rim, land_row, drain


def correlate(
    rec_ref,
    tmpl_ref,
    mask_ref,
    lag_ref,
    out_ref,
    kernel_ref,
    masks_ref,
    lags_ref,
    series_ref,
    rims_ref,
    slots_ref,
    wide_ref,
    trace_ref,
    weight_ref,
    spread_ref,
    moved_ref,
    inverse_ref,
    own_sems,
    *sem_refs,
):
    channels, tmpl_len = tmpl_ref.shape
    size = slots_ref.shape[0]
    filled = spread_ref.shape[0]
    rim_len = rim_columns(tmpl_len)
    slab_len = rec_ref.shape[1]
    span = trace_ref.shape[2]
    blocks = -(-tmpl_len // STEP)
    wide = blocks * STEP * GROUP
    deep = STEP * GROUP
    reach = moved_ref.shape[2]
    per_tile = LANES // STEP
    me = lax.axis_index("tm")
    names = ("rim", "tmpl")
    sems = {name: sem_refs[2 * i : 2 * i + 2] for i, name in enumerate(names)}
    greet, start_down, start_back, start_up, land_rim, land_row, drain = exchange(
        rims_ref, slots_ref, sems
    )
    greet()
    pairs = (
        (tmpl_ref, kernel_ref),
        (mask_ref, masks_ref),
        (lag_ref, lags_ref),
        (rec_ref, series_ref.at[:, pl.ds(0, slab_len)]),
    )
    fetched = [pltpu.make_async_copy(src, dst, own_sems.at[i]) for i, (src, dst) in enumerate(pairs)]
    for move in fetched:
        move.start()
    line0, lane0, per = code_place(channels, tmpl_len)
    fetched[0].wait()
    packed = pack(kernel_ref[...], packed_rows(channels, tmpl_len, 1))
    slots_ref[0, : packed.shape[0]] = packed
    for move in fetched[1:3]:
        move.wait()
    code = jnp.where(masks_ref[...] != 0, lags_ref[...], -1).astype(jnp.float32)
    line = packed[line0:] if line0 < packed.shape[0] else jnp.zeros((ROWS, LANES), packed.dtype)
    line = put_codes(code, line.astype(jnp.float32), lane0, per)
    slots_ref[0, line0 : line0 + ROWS] = line.astype(packed.dtype)
    fetched[3].wait()
    rims_ref[0] = pack(series_ref[:, :rim_len], rims_ref.shape[1])
    start_down()

    lane = lax.broadcasted_iota(jnp.int32, (filled, wide), 1)
    sample = lax.broadcasted_iota(jnp.int32, (filled, wide), 0)
    spread_ref[...] = jnp.where(lane // GROUP == sample, 1.0, 0.0).astype(jnp.bfloat16)
    own = lax.broadcasted_iota(jnp.int32, (channels, wide), 1) % GROUP == (
        lax.broadcasted_iota(jnp.int32, (channels, wide), 0) % GROUP
    )
    lag = (LAGS - 1 - lax.broadcasted_iota(jnp.int32, (LAGS, channels), 0)).astype(jnp.float32)

    def expand(n, slot):
        kernel = unpack(slots_ref[n], channels, tmpl_len)
        widened = jnp.dot(kernel, spread_ref[...], preferred_element_type=jnp.float32)
        as_float = kernel.astype(jnp.float32)
        mean = jnp.sum(as_float * as_float, axis=1, keepdims=True) / tmpl_len
        weight = 1.0 / (jnp.sqrt(mean + 1e-05) * tmpl_len)
        wide_ref[slot] = jnp.where(own, widened, 0.0)
        weight_ref[slot] = jnp.broadcast_to(weight, (channels, LANES))

    def scale():
        series_ref[:, slab_len:] = unpack(rims_ref[1], channels, rim_len)
        series = series_ref[...].astype(jnp.float32)
        squares = series * series
        high = squares.astype(jnp.bfloat16)
        low = (squares - high.astype(jnp.float32)).astype(jnp.bfloat16)
        both = jnp.concatenate([high, low], axis=0)
        row = lax.broadcasted_iota(jnp.int32, (BAND, BAND), 0)
        column = lax.broadcasted_iota(jnp.int32, (BAND, BAND), 1)
        bands = []
        for d in range((tmpl_len + BAND - 2) // BAND + 1):
            off = d * BAND + row - column
            bands.append(jnp.where((off >= 0) & (off < tmpl_len), 1.0, 0.0).astype(jnp.bfloat16))
        for n in range(-(-span // BAND)):
            total = None
            for d, band in enumerate(bands):
                part = both[:, (n + d) * BAND : (n + d + 1) * BAND]
                if part.shape[1] == 0:
                    continue
                part = jnp.dot(part, band[: part.shape[1]], preferred_element_type=jnp.float32)
                total = part if total is None else total + part
            energy = total[:channels] + total[channels:]
            here = slice(n * BAND, min((n + 1) * BAND, span))
            inverse_ref[:, here] = lax.rsqrt(energy / tmpl_len + 1e-05)[:, : here.stop - here.start]

    def spread_out(begin, end):
        reads = min(end + LANES, series_ref.shape[1])
        if end + STEP - 1 <= slab_len:
            reads = min(reads, slab_len)

        @pl.loop(0, channels // ROWS, unroll=unroll_of(channels // ROWS, 5))
        def _(pair):
            rows = pl.ds(pl.multiple_of(pair * ROWS, ROWS), ROWS)
            series = series_ref[rows, begin:reads].astype(jnp.float32)
            for side in range(ROWS // GROUP):
                part = series[side * GROUP : (side + 1) * GROUP]
                moved_ref[pair * (ROWS // GROUP) + side, :, begin:end] = jnp.concatenate(
                    [shifted_left(part, b)[:, : end - begin] for b in range(STEP)], axis=0
                ).astype(jnp.bfloat16)

    def traces(batch):
        @pl.loop(0, channels // GROUP, unroll=unroll_of(channels // GROUP, 20))
        def _(group):
            rows = pl.ds(pl.multiple_of(group * GROUP, GROUP), GROUP)
            left = jnp.concatenate(
                [wide_ref[n, rows, a * deep : (a + 1) * deep] for n in range(batch) for a in range(blocks)],
                axis=0,
            ).astype(jnp.bfloat16)
            partial = jnp.dot(left, moved_ref[group], preferred_element_type=jnp.float32)
            inverse_rms = inverse_ref[rows, :]
            for n in range(batch):
                total = None
                for phase in range(min(per_tile, blocks)):
                    lined = None
                    for a in range(phase, blocks, per_tile):
                        begin = (a - phase) * STEP
                        line = (n * blocks + a) * GROUP
                        piece = partial[line : line + GROUP, begin : begin + span + LANES]
                        if piece.shape[1] < span + LANES:
                            missing = span + LANES - piece.shape[1]
                            piece = jnp.concatenate(
                                [piece, jnp.zeros((GROUP, missing), jnp.float32)], axis=1
                            )
                        lined = piece if lined is None else lined + piece
                    lined = shifted_left(lined, phase * STEP)[:, :span]
                    total = lined if total is None else total + lined
                weight = jnp.concatenate([weight_ref[n, rows, :]] * (span // LANES), axis=1)
                trace_ref[n, rows, :] = total * inverse_rms * weight

    def stack(n, slot):
        line = slots_ref[n, line0 : line0 + ROWS].astype(jnp.float32)
        pick = jnp.where(get_codes(line, channels, lane0, per) == lag, 1.0, 0.0).astype(jnp.bfloat16)
        trace = trace_ref[slot]
        high = trace.astype(jnp.bfloat16)
        low = (trace - high.astype(jnp.float32)).astype(jnp.bfloat16)
        by_lag = jnp.dot(pick, high, preferred_element_type=jnp.float32)
        by_lag += jnp.dot(pick, low, preferred_element_type=jnp.float32)
        lined = pltpu.roll(by_lag, span - LAGS + 1, 1, stride=1, stride_axis=0)
        out_ref[(me + size - n) % size] = jnp.sum(lined, axis=0, keepdims=True)[:, :slab_len]

    def rows_of(first, batch):
        for n in range(batch):
            expand(first + n, n)
        traces(batch)
        for n in range(batch):
            stack(first + n, n)

    batch = min(BATCH, size)
    if batch == size:
        expand(0, 0)
    start_back()
    ready = (slab_len - STEP + 1) // LANES * LANES
    if ready:
        spread_out(0, ready)
    start_up()
    land_rim()
    scale()
    spread_out(ready, reach)
    if batch == size:
        turned = jnp.where(me == 0, size - 2, 0)
        order = [0] + [lax.rem(turned + d - 1, size - 1) + 1 for d in range(1, size)]
        cuts = [0, 2, size] if size > 2 else [0, size]
        for begin, end in zip(cuts[:-1], cuts[1:]):
            for i in range(max(begin, 1), end):
                land_row(order[i])
                expand(order[i], i - begin)
            traces(end - begin)
            for i in range(begin, end):
                stack(order[i], i - begin)
    else:
        for d in range(1, size):
            land_row(d)

        @pl.loop(0, size // batch)
        def _(turn):
            rows_of(turn * batch, batch)

        if size % batch:
            rows_of(size - size % batch, size % batch)
    drain()


def local(records, templates, channel_mask, lag_table):
    channels, slab_len = records.shape
    first, second, tmpl_len = templates.shape[1:]
    assert first == 1 and second == 1
    size = lax.axis_size("tm")
    span = up(slab_len + LAGS - 1, LANES)
    blocks = -(-tmpl_len // STEP)
    wide = blocks * STEP * GROUP
    reach = up(slab_len + LAGS - 1 + (blocks - 1) * STEP, LANES)
    lines = max(packed_rows(channels, tmpl_len, 1), code_place(channels, tmpl_len)[0] + ROWS)
    dma = pltpu.SemaphoreType.DMA
    hbm, vmem = pl.BlockSpec(memory_space=pltpu.HBM), pl.BlockSpec(memory_space=pltpu.VMEM)
    out = pl.pallas_call(
        correlate,
        out_shape=jax.ShapeDtypeStruct((size, 1, slab_len), jnp.float32),
        in_specs=[hbm] * 4,
        out_specs=vmem,
        scratch_shapes=[
            pltpu.VMEM((channels, tmpl_len), jnp.bfloat16),
            pltpu.VMEM((1, channels), jnp.int32),
            pltpu.VMEM((1, channels), jnp.int32),
            pltpu.VMEM((channels, slab_len + up(rim_columns(tmpl_len), LANES)), jnp.bfloat16),
            pltpu.VMEM((2, packed_rows(channels, rim_columns(tmpl_len), 2), LANES), jnp.bfloat16),
            pltpu.VMEM((size, lines, LANES), jnp.bfloat16),
            pltpu.VMEM((BATCH, channels, wide), jnp.float32),
            pltpu.VMEM((BATCH, channels, span), jnp.float32),
            pltpu.VMEM((BATCH, channels, LANES), jnp.float32),
            pltpu.VMEM((up(tmpl_len, LANES), wide), jnp.bfloat16),
            pltpu.VMEM((channels // GROUP, STEP * GROUP, reach), jnp.bfloat16),
            pltpu.VMEM((channels, span), jnp.float32),
            dma((4,)),
            dma((2,)),
            dma((2,)),
            dma((size,)),
            dma((size,)),
        ],
        compiler_params=pltpu.CompilerParams(
            vmem_limit_bytes=62 << 20, collective_id=0, has_side_effects=True
        ),
    )(
        records,
        templates.reshape(channels, tmpl_len),
        channel_mask.reshape(1, channels),
        lag_table.reshape(1, channels),
    )
    return out


def solution(mesh):
    return jax.shard_map(
        local,
        mesh=mesh,
        in_specs=(
            P(None, ("grp", "tm")),
            P(None, "tm", "tmpl", None),
            P(None, "tm", "tmpl"),
            P(None, "tm", "tmpl"),
        ),
        out_specs=P(None, "tmpl", ("grp", "tm")),
        check_vma=False,
    )
```

```python
import jax
import jax.numpy as jnp
from jax import lax
from jax.experimental import pallas as pl
from jax.experimental.pallas import tpu as pltpu
from jax.sharding import PartitionSpec as P

LAGS = 64
LANES = 128
STEP = 32
ROWS = 16
GROUP = 8
BAND = 256
BATCH = 4


def up(value, unit):
    return -(-value // unit) * unit


def shifted_left(values, count):
    width = values.shape[1]
    if count % width == 0:
        return values
    return pltpu.roll(values, width - count % width, 1)


def unroll_of(count, most):
    return max(k for k in range(1, most + 1) if count % k == 0)


def rim_columns(tmpl_len):
    return up(tmpl_len + LAGS - 2, 8)


def remainders(columns):
    parts, begin, left = [], 0, columns % LANES
    width = LANES // 2
    while left:
        if left >= width:
            parts.append((begin, width))
            begin, left = begin + width, left - width
        width //= 2
    return parts


def packed_rows(channels, columns, shares):
    blocks = channels // ROWS
    rows = columns // LANES * channels
    for _, width in remainders(columns):
        rows += -(-blocks // (LANES // width)) * ROWS
    return up(rows, ROWS * shares)


def code_place(channels, columns):
    blocks = channels // ROWS
    rows = packed_rows(channels, columns, 1)
    parts = remainders(columns)
    if parts:
        side = LANES // parts[-1][1]
        used = (blocks % side or side) * parts[-1][1]
        if channels <= (LANES - used) * ROWS:
            return rows - ROWS, used, LANES - used
    return rows, 0, LANES


def put_codes(code, line, lane0, per):
    channels = code.shape[1]
    width = up(channels, LANES)
    code = jnp.concatenate([code, jnp.zeros((1, width - channels), jnp.float32)], axis=1)
    lane = lax.broadcasted_iota(jnp.int32, (ROWS, LANES), 1)
    row = lax.broadcasted_iota(jnp.int32, (ROWS, LANES), 0)
    for r in range(-(-channels // per)):
        part = shifted_left(jnp.broadcast_to(code, (ROWS, width)), (r * per - lane0) % width)[:, :LANES]
        line = jnp.where((row == r) & (lane >= lane0) & (lane < lane0 + per), part, line)
    return line


def get_codes(line, channels, lane0, per):
    width = up(channels, LANES)
    lane = lax.broadcasted_iota(jnp.int32, (1, width), 1)
    code = jnp.zeros((1, width), jnp.float32)
    wide = jnp.concatenate([line, jnp.zeros((ROWS, width - LANES), jnp.float32)], axis=1)
    for r in range(-(-channels // per)):
        part = shifted_left(wide, (lane0 - r * per) % width)[r : r + 1]
        code = jnp.where((lane >= r * per) & (lane < (r + 1) * per), part, code)
    return code[:, :channels]


def pack(values, rows):
    channels, columns = values.shape
    whole = columns // LANES
    blocks = channels // ROWS
    out = [values[:, i * LANES : (i + 1) * LANES] for i in range(whole)]
    if columns % LANES:
        rest = values[:, whole * LANES :].astype(jnp.float32)
        rest = jnp.concatenate([rest, jnp.zeros((channels, LANES - rest.shape[1]), jnp.float32)], axis=1)
        lane = lax.broadcasted_iota(jnp.int32, (ROWS, LANES), 1)
        for begin, width in remainders(columns):
            side = LANES // width
            for first in range(0, blocks, side):
                line = jnp.zeros((ROWS, LANES), jnp.float32)
                for i in range(min(side, blocks - first)):
                    part = rest[(first + i) * ROWS : (first + i + 1) * ROWS]
                    part = shifted_left(part, (begin - i * width) % LANES)
                    line = jnp.where((lane >= i * width) & (lane < (i + 1) * width), part, line)
                out.append(line.astype(values.dtype))
    missing = rows - sum(part.shape[0] for part in out)
    if missing:
        out.append(jnp.zeros((missing, LANES), values.dtype))
    return jnp.concatenate(out, axis=0)


def unpack(values, channels, columns):
    whole = columns // LANES
    blocks = channels // ROWS
    out = [values[i * channels : (i + 1) * channels] for i in range(whole)]
    if columns % LANES:
        lane = lax.broadcasted_iota(jnp.int32, (ROWS, LANES), 1)
        lines = [jnp.zeros((ROWS, LANES), jnp.float32)] * blocks
        row = whole * channels
        for begin, width in remainders(columns):
            side = LANES // width
            for first in range(0, blocks, side):
                line = values[row : row + ROWS].astype(jnp.float32)
                row += ROWS
                for i in range(min(side, blocks - first)):
                    part = shifted_left(line, (i * width - begin) % LANES)
                    here = (lane >= begin) & (lane < begin + width)
                    lines[first + i] = jnp.where(here, part, lines[first + i])
        out.append(jnp.concatenate(lines, axis=0).astype(values.dtype))
    return jnp.concatenate(out, axis=1)


def exchange(rims_ref, slots_ref, sems):
    size = lax.axis_size("tm")
    me, col = lax.axis_index("tm"), lax.axis_index("tmpl")
    mate = col + 1 - 2 * (col % 2)
    half = rims_ref.shape[1] // 2

    def there(axis, index):
        return {"device_id": {axis: index}, "device_id_type": pl.DeviceIdType.MESH}

    def copy(src, dst, name, index, where):
        send, recv = sems[name]
        return pltpu.make_async_remote_copy(
            src_ref=src, dst_ref=dst, send_sem=send.at[index], recv_sem=recv.at[index], **where
        )

    piece = pl.ds(pl.multiple_of((col % 2) * half, ROWS), half)
    barrier = pltpu.get_barrier_semaphore()
    peer = [(me + d) % size for d in range(size)]
    rim = copy(rims_ref.at[0, piece], rims_ref.at[1, piece], "rim", 0, there("tm", jnp.maximum(me - 1, 0)))
    rim_on = copy(rims_ref.at[1, piece], rims_ref.at[1, piece], "rim", 1, there("tmpl", mate))
    row = [None] + [
        copy(slots_ref.at[0], slots_ref.at[d], "tmpl", d, there("tm", peer[d])) for d in range(1, size)
    ]

    def above(d):
        return me + d < size

    def greet_if(side, d):
        @pl.when(side)
        def _():
            pl.semaphore_signal(barrier, inc=1, **there("tm", peer[d]))

    def greet():
        if size > 1:
            pl.semaphore_signal(barrier, inc=1, **there("tmpl", mate))
        for d in range(1, size):
            greet_if(me == 0, d)

    def start_down():
        @pl.when(me > 0)
        def _():
            pl.semaphore_wait(barrier, me + 1)
            rim.start()
            for d in range(1, size):
                greet_if(above(d), d)
            for d in range(1, size):
                greet_if(jnp.logical_not(above(d)), d)

    def start_up():
        @pl.when(me == 0)
        def _():
            if size > 1:
                pl.semaphore_wait(barrier, size)

        @pl.when((me > 0) & (me < size - 1))
        def _():
            pl.semaphore_wait(barrier, size - 1 - me)

        for d in range(1, size):

            @pl.when(above(d))
            def _():
                row[d].start()

    def start_back():
        @pl.when(me > 0)
        def _():
            rim.wait_send()

        for d in range(1, size):

            @pl.when(me + d >= size)
            def _():
                row[d].start()

    def land_rim():
        @pl.when(me < size - 1)
        def _():
            rim.wait_recv()
            rim_on.start()
            rim_on.wait_recv()

        @pl.when(me == size - 1)
        def _():
            rims_ref[1] = jnp.zeros(rims_ref.shape[1:], rims_ref.dtype)

    def land_row(d):
        copy(slots_ref.at[0], slots_ref.at[d], "tmpl", d, there("tm", peer[1])).wait_recv()

    def drain():
        for move in row[1:]:
            move.wait_send()

        @pl.when(me < size - 1)
        def _():
            rim_on.wait_send()

    return greet, start_down, start_back, start_up, land_rim, land_row, drain


def correlate(
    rec_ref,
    tmpl_ref,
    mask_ref,
    lag_ref,
    out_ref,
    kernel_ref,
    masks_ref,
    lags_ref,
    series_ref,
    rims_ref,
    slots_ref,
    wide_ref,
    trace_ref,
    weight_ref,
    spread_ref,
    moved_ref,
    inverse_ref,
    own_sems,
    *sem_refs,
):
    channels, tmpl_len = tmpl_ref.shape
    size = slots_ref.shape[0]
    filled = spread_ref.shape[0]
    rim_len = rim_columns(tmpl_len)
    slab_len = rec_ref.shape[1]
    span = trace_ref.shape[2]
    blocks = -(-tmpl_len // STEP)
    wide = blocks * STEP * GROUP
    deep = STEP * GROUP
    reach = moved_ref.shape[2]
    per_tile = LANES // STEP
    me = lax.axis_index("tm")
    names = ("rim", "tmpl")
    sems = {name: sem_refs[2 * i : 2 * i + 2] for i, name in enumerate(names)}
    greet, start_down, start_back, start_up, land_rim, land_row, drain = exchange(
        rims_ref, slots_ref, sems
    )
    greet()
    pairs = (
        (tmpl_ref, kernel_ref),
        (mask_ref, masks_ref),
        (lag_ref, lags_ref),
        (rec_ref, series_ref.at[:, pl.ds(0, slab_len)]),
    )
    fetched = [pltpu.make_async_copy(src, dst, own_sems.at[i]) for i, (src, dst) in enumerate(pairs)]
    for move in fetched:
        move.start()
    line0, lane0, per = code_place(channels, tmpl_len)
    fetched[0].wait()
    packed = pack(kernel_ref[...], packed_rows(channels, tmpl_len, 1))
    slots_ref[0, : packed.shape[0]] = packed
    for move in fetched[1:3]:
        move.wait()
    code = jnp.where(masks_ref[...] != 0, lags_ref[...], -1).astype(jnp.float32)
    line = packed[line0:] if line0 < packed.shape[0] else jnp.zeros((ROWS, LANES), packed.dtype)
    line = put_codes(code, line.astype(jnp.float32), lane0, per)
    slots_ref[0, line0 : line0 + ROWS] = line.astype(packed.dtype)
    fetched[3].wait()
    rims_ref[0] = pack(series_ref[:, :rim_len], rims_ref.shape[1])
    start_down()

    lane = lax.broadcasted_iota(jnp.int32, (filled, wide), 1)
    sample = lax.broadcasted_iota(jnp.int32, (filled, wide), 0)
    spread_ref[...] = jnp.where(lane // GROUP == sample, 1.0, 0.0).astype(jnp.bfloat16)
    own = lax.broadcasted_iota(jnp.int32, (channels, wide), 1) % GROUP == (
        lax.broadcasted_iota(jnp.int32, (channels, wide), 0) % GROUP
    )
    lag = (LAGS - 1 - lax.broadcasted_iota(jnp.int32, (LAGS, channels), 0)).astype(jnp.float32)

    def expand(n, slot):
        kernel = unpack(slots_ref[n], channels, tmpl_len)
        widened = jnp.dot(kernel, spread_ref[...], preferred_element_type=jnp.float32)
        as_float = kernel.astype(jnp.float32)
        mean = jnp.sum(as_float * as_float, axis=1, keepdims=True) / tmpl_len
        weight = 1.0 / (jnp.sqrt(mean + 1e-05) * tmpl_len)
        wide_ref[slot] = jnp.where(own, widened, 0.0)
        weight_ref[slot] = jnp.broadcast_to(weight, (channels, LANES))

    def scale():
        series_ref[:, slab_len:] = unpack(rims_ref[1], channels, rim_len)
        series = series_ref[...].astype(jnp.float32)
        squares = series * series
        high = squares.astype(jnp.bfloat16)
        low = (squares - high.astype(jnp.float32)).astype(jnp.bfloat16)
        both = jnp.concatenate([high, low], axis=0)
        row = lax.broadcasted_iota(jnp.int32, (BAND, BAND), 0)
        column = lax.broadcasted_iota(jnp.int32, (BAND, BAND), 1)
        bands = []
        for d in range((tmpl_len + BAND - 2) // BAND + 1):
            off = d * BAND + row - column
            bands.append(jnp.where((off >= 0) & (off < tmpl_len), 1.0, 0.0).astype(jnp.bfloat16))
        for n in range(-(-span // BAND)):
            total = None
            for d, band in enumerate(bands):
                part = both[:, (n + d) * BAND : (n + d + 1) * BAND]
                if part.shape[1] == 0:
                    continue
                part = jnp.dot(part, band[: part.shape[1]], preferred_element_type=jnp.float32)
                total = part if total is None else total + part
            energy = total[:channels] + total[channels:]
            here = slice(n * BAND, min((n + 1) * BAND, span))
            inverse_ref[:, here] = lax.rsqrt(energy / tmpl_len + 1e-05)[:, : here.stop - here.start]

    def spread_out(begin, end):
        reads = min(end + LANES, series_ref.shape[1])
        if end + STEP - 1 <= slab_len:
            reads = min(reads, slab_len)

        @pl.loop(0, channels // ROWS, unroll=unroll_of(channels // ROWS, 5))
        def _(pair):
            rows = pl.ds(pl.multiple_of(pair * ROWS, ROWS), ROWS)
            series = series_ref[rows, begin:reads].astype(jnp.float32)
            for side in range(ROWS // GROUP):
                part = series[side * GROUP : (side + 1) * GROUP]
                moved_ref[pair * (ROWS // GROUP) + side, :, begin:end] = jnp.concatenate(
                    [shifted_left(part, b)[:, : end - begin] for b in range(STEP)], axis=0
                ).astype(jnp.bfloat16)

    def traces(batch):
        @pl.loop(0, channels // GROUP, unroll=unroll_of(channels // GROUP, 20))
        def _(group):
            rows = pl.ds(pl.multiple_of(group * GROUP, GROUP), GROUP)
            left = jnp.concatenate(
                [wide_ref[n, rows, a * deep : (a + 1) * deep] for n in range(batch) for a in range(blocks)],
                axis=0,
            ).astype(jnp.bfloat16)
            partial = jnp.dot(left, moved_ref[group], preferred_element_type=jnp.float32)
            inverse_rms = inverse_ref[rows, :]
            for n in range(batch):
                total = None
                for phase in range(min(per_tile, blocks)):
                    lined = None
                    for a in range(phase, blocks, per_tile):
                        begin = (a - phase) * STEP
                        line = (n * blocks + a) * GROUP
                        piece = partial[line : line + GROUP, begin : begin + span + LANES]
                        if piece.shape[1] < span + LANES:
                            missing = span + LANES - piece.shape[1]
                            piece = jnp.concatenate(
                                [piece, jnp.zeros((GROUP, missing), jnp.float32)], axis=1
                            )
                        lined = piece if lined is None else lined + piece
                    lined = shifted_left(lined, phase * STEP)[:, :span]
                    total = lined if total is None else total + lined
                weight = jnp.concatenate([weight_ref[n, rows, :]] * (span // LANES), axis=1)
                trace_ref[n, rows, :] = total * inverse_rms * weight

    def stack(n, slot):
        line = slots_ref[n, line0 : line0 + ROWS].astype(jnp.float32)
        pick = jnp.where(get_codes(line, channels, lane0, per) == lag, 1.0, 0.0).astype(jnp.bfloat16)
        trace = trace_ref[slot]
        high = trace.astype(jnp.bfloat16)
        low = (trace - high.astype(jnp.float32)).astype(jnp.bfloat16)
        by_lag = jnp.dot(pick, high, preferred_element_type=jnp.float32)
        by_lag += jnp.dot(pick, low, preferred_element_type=jnp.float32)
        lined = pltpu.roll(by_lag, span - LAGS + 1, 1, stride=1, stride_axis=0)
        out_ref[(me + size - n) % size] = jnp.sum(lined, axis=0, keepdims=True)[:, :slab_len]

    def rows_of(first, batch):
        for n in range(batch):
            expand(first + n, n)
        traces(batch)
        for n in range(batch):
            stack(first + n, n)

    batch = min(BATCH, size)
    if batch == size:
        expand(0, 0)
    start_back()
    ready = (slab_len - STEP + 1) // LANES * LANES
    if ready:
        spread_out(0, ready)
    start_up()
    land_rim()
    scale()
    spread_out(ready, reach)
    if batch == size:
        turned = jnp.where(me == 0, size - 2, 0)
        order = [0] + [lax.rem(turned + d - 1, size - 1) + 1 for d in range(1, size)]
        cuts = [0, 2, size] if size > 2 else [0, size]
        for begin, end in zip(cuts[:-1], cuts[1:]):
            for i in range(max(begin, 1), end):
                land_row(order[i])
                expand(order[i], i - begin)
            traces(end - begin)
            for i in range(begin, end):
                stack(order[i], i - begin)
    else:
        for d in range(1, size):
            land_row(d)

        @pl.loop(0, size // batch)
        def _(turn):
            rows_of(turn * batch, batch)

        if size % batch:
            rows_of(size - size % batch, size % batch)
    drain()


def local(records, templates, channel_mask, lag_table):
    channels, slab_len = records.shape
    first, second, tmpl_len = templates.shape[1:]
    assert first == 1 and second == 1
    size = lax.axis_size("tm")
    span = up(slab_len + LAGS - 1, LANES)
    blocks = -(-tmpl_len // STEP)
    wide = blocks * STEP * GROUP
    reach = up(slab_len + LAGS - 1 + (blocks - 1) * STEP, LANES)
    lines = max(packed_rows(channels, tmpl_len, 1), code_place(channels, tmpl_len)[0] + ROWS)
    dma = pltpu.SemaphoreType.DMA
    hbm, vmem = pl.BlockSpec(memory_space=pltpu.HBM), pl.BlockSpec(memory_space=pltpu.VMEM)
    out = pl.pallas_call(
        correlate,
        out_shape=pltpu.VMEM((size, 1, slab_len), jnp.float32),
        in_specs=[hbm] * 4,
        out_specs=vmem,
        scratch_shapes=[
            pltpu.VMEM((channels, tmpl_len), jnp.bfloat16),
            pltpu.VMEM((1, channels), jnp.int32),
            pltpu.VMEM((1, channels), jnp.int32),
            pltpu.VMEM((channels, slab_len + up(rim_columns(tmpl_len), LANES)), jnp.bfloat16),
            pltpu.VMEM((2, packed_rows(channels, rim_columns(tmpl_len), 2), LANES), jnp.bfloat16),
            pltpu.VMEM((size, lines, LANES), jnp.bfloat16),
            pltpu.VMEM((BATCH, channels, wide), jnp.float32),
            pltpu.VMEM((BATCH, channels, span), jnp.float32),
            pltpu.VMEM((BATCH, channels, LANES), jnp.float32),
            pltpu.VMEM((up(tmpl_len, LANES), wide), jnp.bfloat16),
            pltpu.VMEM((channels // GROUP, STEP * GROUP, reach), jnp.bfloat16),
            pltpu.VMEM((channels, span), jnp.float32),
            dma((4,)),
            dma((2,)),
            dma((2,)),
            dma((size,)),
            dma((size,)),
        ],
        compiler_params=pltpu.CompilerParams(
            vmem_limit_bytes=62 << 20, collective_id=0, has_side_effects=True
        ),
    )(
        records,
        templates.reshape(channels, tmpl_len),
        channel_mask.reshape(1, channels),
        lag_table.reshape(1, channels),
    )
    return out


def solution(mesh):
    return jax.shard_map(
        local,
        mesh=mesh,
        in_specs=(
            P(None, ("grp", "tm")),
            P(None, "tm", "tmpl", None),
            P(None, "tm", "tmpl"),
            P(None, "tm", "tmpl"),
        ),
        out_specs=P(None, "tmpl", ("grp", "tm")),
        check_vma=False,
    )
```

```python
import jax
import jax.numpy as jnp
from jax import lax
from jax.experimental import pallas as pl
from jax.experimental.pallas import tpu as pltpu
from jax.sharding import PartitionSpec as P

LAGS = 64
LANES = 128
STEP = 32
ROWS = 16
GROUP = 8
BAND = 256
BATCH = 4


def up(value, unit):
    return -(-value // unit) * unit


def shifted_left(values, count):
    width = values.shape[1]
    if count % width == 0:
        return values
    return pltpu.roll(values, width - count % width, 1)


def unroll_of(count, most):
    return max(k for k in range(1, most + 1) if count % k == 0)


def rim_columns(tmpl_len):
    return up(tmpl_len + LAGS - 2, 8)


def remainders(columns):
    parts, begin, left = [], 0, columns % LANES
    width = LANES // 2
    while left:
        if left >= width:
            parts.append((begin, width))
            begin, left = begin + width, left - width
        width //= 2
    return parts


def packed_rows(channels, columns, shares):
    blocks = channels // ROWS
    rows = columns // LANES * channels
    for _, width in remainders(columns):
        rows += -(-blocks // (LANES // width)) * ROWS
    return up(rows, ROWS * shares)


def code_place(channels, columns):
    blocks = channels // ROWS
    rows = packed_rows(channels, columns, 1)
    parts = remainders(columns)
    if parts:
        side = LANES // parts[-1][1]
        used = (blocks % side or side) * parts[-1][1]
        if channels <= (LANES - used) * ROWS:
            return rows - ROWS, used, LANES - used
    return rows, 0, LANES


def put_codes(code, line, lane0, per):
    channels = code.shape[1]
    width = up(channels, LANES)
    code = jnp.concatenate([code, jnp.zeros((1, width - channels), jnp.float32)], axis=1)
    lane = lax.broadcasted_iota(jnp.int32, (ROWS, LANES), 1)
    row = lax.broadcasted_iota(jnp.int32, (ROWS, LANES), 0)
    for r in range(-(-channels // per)):
        part = shifted_left(jnp.broadcast_to(code, (ROWS, width)), (r * per - lane0) % width)[:, :LANES]
        line = jnp.where((row == r) & (lane >= lane0) & (lane < lane0 + per), part, line)
    return line


def get_codes(line, channels, lane0, per):
    width = up(channels, LANES)
    lane = lax.broadcasted_iota(jnp.int32, (1, width), 1)
    code = jnp.zeros((1, width), jnp.float32)
    wide = jnp.concatenate([line, jnp.zeros((ROWS, width - LANES), jnp.float32)], axis=1)
    for r in range(-(-channels // per)):
        part = shifted_left(wide, (lane0 - r * per) % width)[r : r + 1]
        code = jnp.where((lane >= r * per) & (lane < (r + 1) * per), part, code)
    return code[:, :channels]


def pack(values, rows):
    channels, columns = values.shape
    whole = columns // LANES
    blocks = channels // ROWS
    out = [values[:, i * LANES : (i + 1) * LANES] for i in range(whole)]
    if columns % LANES:
        rest = values[:, whole * LANES :].astype(jnp.float32)
        rest = jnp.concatenate([rest, jnp.zeros((channels, LANES - rest.shape[1]), jnp.float32)], axis=1)
        lane = lax.broadcasted_iota(jnp.int32, (ROWS, LANES), 1)
        for begin, width in remainders(columns):
            side = LANES // width
            for first in range(0, blocks, side):
                line = jnp.zeros((ROWS, LANES), jnp.float32)
                for i in range(min(side, blocks - first)):
                    part = rest[(first + i) * ROWS : (first + i + 1) * ROWS]
                    part = shifted_left(part, (begin - i * width) % LANES)
                    line = jnp.where((lane >= i * width) & (lane < (i + 1) * width), part, line)
                out.append(line.astype(values.dtype))
    missing = rows - sum(part.shape[0] for part in out)
    if missing:
        out.append(jnp.zeros((missing, LANES), values.dtype))
    return jnp.concatenate(out, axis=0)


def unpack(values, channels, columns):
    whole = columns // LANES
    blocks = channels // ROWS
    out = [values[i * channels : (i + 1) * channels] for i in range(whole)]
    if columns % LANES:
        lane = lax.broadcasted_iota(jnp.int32, (ROWS, LANES), 1)
        lines = [jnp.zeros((ROWS, LANES), jnp.float32)] * blocks
        row = whole * channels
        for begin, width in remainders(columns):
            side = LANES // width
            for first in range(0, blocks, side):
                line = values[row : row + ROWS].astype(jnp.float32)
                row += ROWS
                for i in range(min(side, blocks - first)):
                    part = shifted_left(line, (i * width - begin) % LANES)
                    here = (lane >= begin) & (lane < begin + width)
                    lines[first + i] = jnp.where(here, part, lines[first + i])
        out.append(jnp.concatenate(lines, axis=0).astype(values.dtype))
    return jnp.concatenate(out, axis=1)


def exchange(rims_ref, slots_ref, sems):
    size = lax.axis_size("tm")
    me, col = lax.axis_index("tm"), lax.axis_index("tmpl")
    mate = col + 1 - 2 * (col % 2)
    half = rims_ref.shape[1] // 2

    def there(axis, index):
        return {"device_id": {axis: index}, "device_id_type": pl.DeviceIdType.MESH}

    def copy(src, dst, name, index, where):
        send, recv = sems[name]
        return pltpu.make_async_remote_copy(
            src_ref=src, dst_ref=dst, send_sem=send.at[index], recv_sem=recv.at[index], **where
        )

    piece = pl.ds(pl.multiple_of((col % 2) * half, ROWS), half)
    barrier = pltpu.get_barrier_semaphore()
    peer = [(me + d) % size for d in range(size)]
    rim = copy(rims_ref.at[0, piece], rims_ref.at[1, piece], "rim", 0, there("tm", jnp.maximum(me - 1, 0)))
    rim_on = copy(rims_ref.at[1, piece], rims_ref.at[1, piece], "rim", 1, there("tmpl", mate))
    row = [None] + [
        copy(slots_ref.at[0], slots_ref.at[d], "tmpl", d, there("tm", peer[d])) for d in range(1, size)
    ]

    def above(d):
        return me + d < size

    def greet_if(side, d):
        @pl.when(side)
        def _():
            pl.semaphore_signal(barrier, inc=1, **there("tm", peer[d]))

    def greet():
        if size > 1:
            pl.semaphore_signal(barrier, inc=1, **there("tmpl", mate))
        for d in range(1, size):
            greet_if(me == 0, d)

    def start_down():
        @pl.when(me > 0)
        def _():
            pl.semaphore_wait(barrier, me + 1)
            rim.start()
            for d in range(1, size):
                greet_if(above(d), d)
            for d in range(1, size):
                greet_if(jnp.logical_not(above(d)), d)

    def start_up():
        @pl.when(me == 0)
        def _():
            if size > 1:
                pl.semaphore_wait(barrier, size)

        @pl.when((me > 0) & (me < size - 1))
        def _():
            pl.semaphore_wait(barrier, size - 1 - me)

        for d in range(1, size):

            @pl.when(above(d))
            def _():
                row[d].start()

    def start_back():
        for d in range(1, size):

            @pl.when(me + d >= size)
            def _():
                row[d].start()

    def land_rim():
        @pl.when(me < size - 1)
        def _():
            rim.wait_recv()
            rim_on.start()
            rim_on.wait_recv()

        @pl.when(me == size - 1)
        def _():
            rims_ref[1] = jnp.zeros(rims_ref.shape[1:], rims_ref.dtype)

    def land_row(d):
        copy(slots_ref.at[0], slots_ref.at[d], "tmpl", d, there("tm", peer[1])).wait_recv()

    def drain():
        for move in row[1:]:
            move.wait_send()

        @pl.when(me > 0)
        def _():
            rim.wait_send()

        @pl.when(me < size - 1)
        def _():
            rim_on.wait_send()

    return greet, start_down, start_back, start_up, land_rim, land_row, drain


def correlate(
    rec_ref,
    tmpl_ref,
    mask_ref,
    lag_ref,
    out_ref,
    kernel_ref,
    masks_ref,
    lags_ref,
    series_ref,
    rims_ref,
    slots_ref,
    wide_ref,
    trace_ref,
    weight_ref,
    spread_ref,
    moved_ref,
    inverse_ref,
    own_sems,
    *sem_refs,
):
    channels, tmpl_len = tmpl_ref.shape
    size = slots_ref.shape[0]
    filled = spread_ref.shape[0]
    rim_len = rim_columns(tmpl_len)
    slab_len = rec_ref.shape[1]
    span = trace_ref.shape[2]
    blocks = -(-tmpl_len // STEP)
    wide = blocks * STEP * GROUP
    deep = STEP * GROUP
    reach = moved_ref.shape[2]
    per_tile = LANES // STEP
    me, col = lax.axis_index("tm"), lax.axis_index("tmpl")
    names = ("rim", "tmpl")
    sems = {name: sem_refs[2 * i : 2 * i + 2] for i, name in enumerate(names)}
    greet, start_down, start_back, start_up, land_rim, land_row, drain = exchange(
        rims_ref, slots_ref, sems
    )
    greet()
    pairs = (
        (rec_ref, series_ref.at[:, pl.ds(0, slab_len)]),
        (tmpl_ref, kernel_ref),
        (mask_ref, masks_ref),
        (lag_ref, lags_ref),
    )
    fetched = [pltpu.make_async_copy(src, dst, own_sems.at[i]) for i, (src, dst) in enumerate(pairs)]
    for move in fetched:
        move.start()
    lane = lax.broadcasted_iota(jnp.int32, (filled, wide), 1)
    sample = lax.broadcasted_iota(jnp.int32, (filled, wide), 0)
    spread_ref[...] = jnp.where(lane // GROUP == sample, 1.0, 0.0).astype(jnp.bfloat16)
    own = lax.broadcasted_iota(jnp.int32, (channels, wide), 1) % GROUP == (
        lax.broadcasted_iota(jnp.int32, (channels, wide), 0) % GROUP
    )
    lag = (LAGS - 1 - lax.broadcasted_iota(jnp.int32, (LAGS, channels), 0)).astype(jnp.float32)

    fetched[0].wait()
    rims_ref[0] = pack(series_ref[:, :rim_len], rims_ref.shape[1])
    start_down()
    line0, lane0, per = code_place(channels, tmpl_len)
    for move in fetched[1:]:
        move.wait()
    packed = pack(kernel_ref[...], packed_rows(channels, tmpl_len, 1))
    slots_ref[0, : packed.shape[0]] = packed
    code = jnp.where(masks_ref[...] != 0, lags_ref[...], -1).astype(jnp.float32)
    line = packed[line0:] if line0 < packed.shape[0] else jnp.zeros((ROWS, LANES), packed.dtype)
    line = put_codes(code, line.astype(jnp.float32), lane0, per)
    slots_ref[0, line0 : line0 + ROWS] = line.astype(packed.dtype)

    def expand(n, slot):
        kernel = unpack(slots_ref[n], channels, tmpl_len)
        widened = jnp.dot(kernel, spread_ref[...], preferred_element_type=jnp.float32)
        as_float = kernel.astype(jnp.float32)
        mean = jnp.sum(as_float * as_float, axis=1, keepdims=True) / tmpl_len
        weight = 1.0 / (jnp.sqrt(mean + 1e-05) * tmpl_len)
        wide_ref[slot] = jnp.where(own, widened, 0.0)
        weight_ref[slot] = jnp.broadcast_to(weight, (channels, LANES))

    def scale():
        series_ref[:, slab_len:] = unpack(rims_ref[1], channels, rim_len)
        series = series_ref[...].astype(jnp.float32)
        squares = series * series
        high = squares.astype(jnp.bfloat16)
        low = (squares - high.astype(jnp.float32)).astype(jnp.bfloat16)
        both = jnp.concatenate([high, low], axis=0)
        row = lax.broadcasted_iota(jnp.int32, (BAND, BAND), 0)
        column = lax.broadcasted_iota(jnp.int32, (BAND, BAND), 1)
        bands = []
        for d in range((tmpl_len + BAND - 2) // BAND + 1):
            off = d * BAND + row - column
            bands.append(jnp.where((off >= 0) & (off < tmpl_len), 1.0, 0.0).astype(jnp.bfloat16))
        for n in range(-(-span // BAND)):
            total = None
            for d, band in enumerate(bands):
                part = both[:, (n + d) * BAND : (n + d + 1) * BAND]
                if part.shape[1] == 0:
                    continue
                part = jnp.dot(part, band[: part.shape[1]], preferred_element_type=jnp.float32)
                total = part if total is None else total + part
            energy = total[:channels] + total[channels:]
            here = slice(n * BAND, min((n + 1) * BAND, span))
            inverse_ref[:, here] = lax.rsqrt(energy / tmpl_len + 1e-05)[:, : here.stop - here.start]

    def spread_out(begin, end):
        reads = min(end + LANES, series_ref.shape[1])
        if end + STEP - 1 <= slab_len:
            reads = min(reads, slab_len)

        @pl.loop(0, channels // ROWS, unroll=unroll_of(channels // ROWS, 5))
        def _(pair):
            rows = pl.ds(pl.multiple_of(pair * ROWS, ROWS), ROWS)
            series = series_ref[rows, begin:reads].astype(jnp.float32)
            for side in range(ROWS // GROUP):
                part = series[side * GROUP : (side + 1) * GROUP]
                moved_ref[pair * (ROWS // GROUP) + side, :, begin:end] = jnp.concatenate(
                    [shifted_left(part, b)[:, : end - begin] for b in range(STEP)], axis=0
                ).astype(jnp.bfloat16)

    def traces(batch):
        @pl.loop(0, channels // GROUP, unroll=unroll_of(channels // GROUP, 20))
        def _(group):
            rows = pl.ds(pl.multiple_of(group * GROUP, GROUP), GROUP)
            left = jnp.concatenate(
                [wide_ref[n, rows, a * deep : (a + 1) * deep] for n in range(batch) for a in range(blocks)],
                axis=0,
            ).astype(jnp.bfloat16)
            partial = jnp.dot(left, moved_ref[group], preferred_element_type=jnp.float32)
            inverse_rms = inverse_ref[rows, :]
            for n in range(batch):
                total = None
                for phase in range(min(per_tile, blocks)):
                    lined = None
                    for a in range(phase, blocks, per_tile):
                        begin = (a - phase) * STEP
                        line = (n * blocks + a) * GROUP
                        piece = partial[line : line + GROUP, begin : begin + span + LANES]
                        if piece.shape[1] < span + LANES:
                            missing = span + LANES - piece.shape[1]
                            piece = jnp.concatenate(
                                [piece, jnp.zeros((GROUP, missing), jnp.float32)], axis=1
                            )
                        lined = piece if lined is None else lined + piece
                    lined = shifted_left(lined, phase * STEP)[:, :span]
                    total = lined if total is None else total + lined
                weight = jnp.concatenate([weight_ref[n, rows, :]] * (span // LANES), axis=1)
                trace_ref[n, rows, :] = total * inverse_rms * weight

    def stack(n, slot):
        line = slots_ref[n, line0 : line0 + ROWS].astype(jnp.float32)
        pick = jnp.where(get_codes(line, channels, lane0, per) == lag, 1.0, 0.0).astype(jnp.bfloat16)
        trace = trace_ref[slot]
        high = trace.astype(jnp.bfloat16)
        low = (trace - high.astype(jnp.float32)).astype(jnp.bfloat16)
        by_lag = jnp.dot(pick, high, preferred_element_type=jnp.float32)
        by_lag += jnp.dot(pick, low, preferred_element_type=jnp.float32)
        lined = pltpu.roll(by_lag, span - LAGS + 1, 1, stride=1, stride_axis=0)
        out_ref[(me + size - n) % size] = jnp.sum(lined, axis=0, keepdims=True)[:, :slab_len]

    def rows_of(first, batch):
        for n in range(batch):
            expand(first + n, n)
        traces(batch)
        for n in range(batch):
            stack(first + n, n)

    batch = min(BATCH, size)
    if batch == size:
        expand(0, 0)
    pl.when(col % 2 == 0)(start_back)
    ready = (slab_len - STEP + 1) // LANES * LANES
    if ready:
        spread_out(0, ready)
    pl.when(col % 2 == 1)(start_back)
    start_up()
    land_rim()
    scale()
    spread_out(ready, reach)
    if batch == size:
        turned = jnp.where(me == 0, size - 2, 0)
        order = [0] + [lax.rem(turned + d - 1, size - 1) + 1 for d in range(1, size)]

        def in_turn(cuts):
            for begin, end in zip(cuts[:-1], cuts[1:]):
                for i in range(max(begin, 1), end):
                    land_row(order[i])
                    expand(order[i], i - begin)
                traces(end - begin)
                for i in range(begin, end):
                    stack(order[i], i - begin)

        if size > 2:
            pl.when(col % 2 == 0)(lambda: in_turn([0, 2, size]))
            pl.when(col % 2 == 1)(lambda: in_turn([0, size]))
        else:
            in_turn([0, size])
    else:
        for d in range(1, size):
            land_row(d)

        @pl.loop(0, size // batch)
        def _(turn):
            rows_of(turn * batch, batch)

        if size % batch:
            rows_of(size - size % batch, size % batch)
    drain()


def local(records, templates, channel_mask, lag_table):
    channels, slab_len = records.shape
    first, second, tmpl_len = templates.shape[1:]
    assert first == 1 and second == 1
    size = lax.axis_size("tm")
    span = up(slab_len + LAGS - 1, LANES)
    blocks = -(-tmpl_len // STEP)
    wide = blocks * STEP * GROUP
    reach = up(slab_len + LAGS - 1 + (blocks - 1) * STEP, LANES)
    lines = max(packed_rows(channels, tmpl_len, 1), code_place(channels, tmpl_len)[0] + ROWS)
    dma = pltpu.SemaphoreType.DMA
    hbm, vmem = pl.BlockSpec(memory_space=pltpu.HBM), pl.BlockSpec(memory_space=pltpu.VMEM)
    out = pl.pallas_call(
        correlate,
        out_shape=pltpu.VMEM((size, 1, slab_len), jnp.float32),
        in_specs=[hbm] * 4,
        out_specs=vmem,
        scratch_shapes=[
            pltpu.VMEM((channels, tmpl_len), jnp.bfloat16),
            pltpu.VMEM((1, channels), jnp.int32),
            pltpu.VMEM((1, channels), jnp.int32),
            pltpu.VMEM((channels, slab_len + up(rim_columns(tmpl_len), LANES)), jnp.bfloat16),
            pltpu.VMEM((2, packed_rows(channels, rim_columns(tmpl_len), 2), LANES), jnp.bfloat16),
            pltpu.VMEM((size, lines, LANES), jnp.bfloat16),
            pltpu.VMEM((BATCH, channels, wide), jnp.float32),
            pltpu.VMEM((BATCH, channels, span), jnp.float32),
            pltpu.VMEM((BATCH, channels, LANES), jnp.float32),
            pltpu.VMEM((up(tmpl_len, LANES), wide), jnp.bfloat16),
            pltpu.VMEM((channels // GROUP, STEP * GROUP, reach), jnp.bfloat16),
            pltpu.VMEM((channels, span), jnp.float32),
            dma((4,)),
            dma((2,)),
            dma((2,)),
            dma((size,)),
            dma((size,)),
        ],
        compiler_params=pltpu.CompilerParams(
            vmem_limit_bytes=62 << 20, collective_id=0, has_side_effects=True
        ),
    )(
        records,
        templates.reshape(channels, tmpl_len),
        channel_mask.reshape(1, channels),
        lag_table.reshape(1, channels),
    )
    return out


def solution(mesh):
    return jax.shard_map(
        local,
        mesh=mesh,
        in_specs=(
            P(None, ("grp", "tm")),
            P(None, "tm", "tmpl", None),
            P(None, "tm", "tmpl"),
            P(None, "tm", "tmpl"),
        ),
        out_specs=P(None, "tmpl", ("grp", "tm")),
        check_vma=False,
    )
```

```python
import jax
import jax.numpy as jnp
from jax import lax
from jax.experimental import pallas as pl
from jax.experimental.pallas import tpu as pltpu
from jax.sharding import PartitionSpec as P

LAGS = 64
LANES = 128
STEP = 32
ROWS = 16
GROUP = 8
BAND = 256
BATCH = 4


def up(value, unit):
    return -(-value // unit) * unit


def shifted_left(values, count):
    width = values.shape[1]
    if count % width == 0:
        return values
    return pltpu.roll(values, width - count % width, 1)


def unroll_of(count, most):
    return max(k for k in range(1, most + 1) if count % k == 0)


def rim_columns(tmpl_len):
    return up(tmpl_len + LAGS - 2, 8)


def remainders(columns):
    parts, begin, left = [], 0, columns % LANES
    width = LANES // 2
    while left:
        if left >= width:
            parts.append((begin, width))
            begin, left = begin + width, left - width
        width //= 2
    return parts


def packed_rows(channels, columns, shares):
    blocks = channels // ROWS
    rows = columns // LANES * channels
    for _, width in remainders(columns):
        rows += -(-blocks // (LANES // width)) * ROWS
    return up(rows, ROWS * shares)


def code_place(channels, columns):
    blocks = channels // ROWS
    rows = packed_rows(channels, columns, 1)
    parts = remainders(columns)
    if parts:
        side = LANES // parts[-1][1]
        used = (blocks % side or side) * parts[-1][1]
        if channels <= (LANES - used) * ROWS:
            return rows - ROWS, used, LANES - used
    return rows, 0, LANES


def put_codes(code, line, lane0, per):
    channels = code.shape[1]
    width = up(channels, LANES)
    code = jnp.concatenate([code, jnp.zeros((1, width - channels), jnp.float32)], axis=1)
    lane = lax.broadcasted_iota(jnp.int32, (ROWS, LANES), 1)
    row = lax.broadcasted_iota(jnp.int32, (ROWS, LANES), 0)
    for r in range(-(-channels // per)):
        part = shifted_left(jnp.broadcast_to(code, (ROWS, width)), (r * per - lane0) % width)[:, :LANES]
        line = jnp.where((row == r) & (lane >= lane0) & (lane < lane0 + per), part, line)
    return line


def get_codes(line, channels, lane0, per):
    width = up(channels, LANES)
    lane = lax.broadcasted_iota(jnp.int32, (1, width), 1)
    code = jnp.zeros((1, width), jnp.float32)
    wide = jnp.concatenate([line, jnp.zeros((ROWS, width - LANES), jnp.float32)], axis=1)
    for r in range(-(-channels // per)):
        part = shifted_left(wide, (lane0 - r * per) % width)[r : r + 1]
        code = jnp.where((lane >= r * per) & (lane < (r + 1) * per), part, code)
    return code[:, :channels]


def pack(values, rows):
    channels, columns = values.shape
    whole = columns // LANES
    blocks = channels // ROWS
    out = [values[:, i * LANES : (i + 1) * LANES] for i in range(whole)]
    if columns % LANES:
        rest = values[:, whole * LANES :].astype(jnp.float32)
        rest = jnp.concatenate([rest, jnp.zeros((channels, LANES - rest.shape[1]), jnp.float32)], axis=1)
        lane = lax.broadcasted_iota(jnp.int32, (ROWS, LANES), 1)
        for begin, width in remainders(columns):
            side = LANES // width
            for first in range(0, blocks, side):
                line = jnp.zeros((ROWS, LANES), jnp.float32)
                for i in range(min(side, blocks - first)):
                    part = rest[(first + i) * ROWS : (first + i + 1) * ROWS]
                    part = shifted_left(part, (begin - i * width) % LANES)
                    line = jnp.where((lane >= i * width) & (lane < (i + 1) * width), part, line)
                out.append(line.astype(values.dtype))
    missing = rows - sum(part.shape[0] for part in out)
    if missing:
        out.append(jnp.zeros((missing, LANES), values.dtype))
    return jnp.concatenate(out, axis=0)


def unpack(values, channels, columns):
    whole = columns // LANES
    blocks = channels // ROWS
    out = [values[i * channels : (i + 1) * channels] for i in range(whole)]
    if columns % LANES:
        lane = lax.broadcasted_iota(jnp.int32, (ROWS, LANES), 1)
        lines = [jnp.zeros((ROWS, LANES), jnp.float32)] * blocks
        row = whole * channels
        for begin, width in remainders(columns):
            side = LANES // width
            for first in range(0, blocks, side):
                line = values[row : row + ROWS].astype(jnp.float32)
                row += ROWS
                for i in range(min(side, blocks - first)):
                    part = shifted_left(line, (i * width - begin) % LANES)
                    here = (lane >= begin) & (lane < begin + width)
                    lines[first + i] = jnp.where(here, part, lines[first + i])
        out.append(jnp.concatenate(lines, axis=0).astype(values.dtype))
    return jnp.concatenate(out, axis=1)


def exchange(rims_ref, slots_ref, sems):
    size = lax.axis_size("tm")
    me, col = lax.axis_index("tm"), lax.axis_index("tmpl")
    mate = col + 1 - 2 * (col % 2)
    half = rims_ref.shape[1] // 2

    def there(axis, index):
        return {"device_id": {axis: index}, "device_id_type": pl.DeviceIdType.MESH}

    def copy(src, dst, name, index, where):
        send, recv = sems[name]
        return pltpu.make_async_remote_copy(
            src_ref=src, dst_ref=dst, send_sem=send.at[index], recv_sem=recv.at[index], **where
        )

    piece = pl.ds(pl.multiple_of((col % 2) * half, ROWS), half)
    barrier = pltpu.get_barrier_semaphore()
    peer = [(me + d) % size for d in range(size)]
    rim = copy(rims_ref.at[0, piece], rims_ref.at[1, piece], "rim", 0, there("tm", jnp.maximum(me - 1, 0)))
    rim_on = copy(rims_ref.at[1, piece], rims_ref.at[1, piece], "rim", 1, there("tmpl", mate))
    row = [None] + [
        copy(slots_ref.at[0], slots_ref.at[d], "tmpl", d, there("tm", peer[d])) for d in range(1, size)
    ]

    def above(d):
        return me + d < size

    def greet_if(side, d):
        @pl.when(side)
        def _():
            pl.semaphore_signal(barrier, inc=1, **there("tm", peer[d]))

    def greet():
        if size > 1:
            pl.semaphore_signal(barrier, inc=1, **there("tmpl", mate))
        for d in range(1, size):
            greet_if(me == 0, d)

    def start_down():
        @pl.when(me > 0)
        def _():
            pl.semaphore_wait(barrier, me + 1)
            rim.start()
            for d in range(1, size):
                greet_if(above(d), d)
            for d in range(1, size):
                greet_if(jnp.logical_not(above(d)), d)

    def start_up():
        @pl.when(me == 0)
        def _():
            if size > 1:
                pl.semaphore_wait(barrier, size)

        @pl.when((me > 0) & (me < size - 1))
        def _():
            pl.semaphore_wait(barrier, size - 1 - me)

        for d in range(1, size):

            @pl.when(above(d))
            def _():
                row[d].start()

    def start_back():
        for d in range(1, size):

            @pl.when(me + d >= size)
            def _():
                row[d].start()

    def land_rim():
        @pl.when(me < size - 1)
        def _():
            rim.wait_recv()
            rim_on.start()
            rim_on.wait_recv()

        @pl.when(me == size - 1)
        def _():
            rims_ref[1] = jnp.zeros(rims_ref.shape[1:], rims_ref.dtype)

    def land_row(d):
        copy(slots_ref.at[0], slots_ref.at[d], "tmpl", d, there("tm", peer[1])).wait_recv()

    def drain():
        for move in row[1:]:
            move.wait_send()

        @pl.when(me > 0)
        def _():
            rim.wait_send()

        @pl.when(me < size - 1)
        def _():
            rim_on.wait_send()

    return greet, start_down, start_back, start_up, land_rim, land_row, drain


def correlate(
    rec_ref,
    tmpl_ref,
    mask_ref,
    lag_ref,
    out_ref,
    kernel_ref,
    masks_ref,
    lags_ref,
    series_ref,
    rims_ref,
    slots_ref,
    wide_ref,
    trace_ref,
    weight_ref,
    spread_ref,
    moved_ref,
    inverse_ref,
    own_sems,
    *sem_refs,
):
    channels, tmpl_len = tmpl_ref.shape
    size = slots_ref.shape[0]
    filled = spread_ref.shape[0]
    rim_len = rim_columns(tmpl_len)
    slab_len = rec_ref.shape[1]
    span = trace_ref.shape[2]
    blocks = -(-tmpl_len // STEP)
    wide = blocks * STEP * GROUP
    deep = STEP * GROUP
    reach = moved_ref.shape[2]
    per_tile = LANES // STEP
    me, col = lax.axis_index("tm"), lax.axis_index("tmpl")
    names = ("rim", "tmpl")
    sems = {name: sem_refs[2 * i : 2 * i + 2] for i, name in enumerate(names)}
    greet, start_down, start_back, start_up, land_rim, land_row, drain = exchange(
        rims_ref, slots_ref, sems
    )
    greet()
    pairs = (
        (rec_ref, series_ref.at[:, pl.ds(0, slab_len)]),
        (tmpl_ref, kernel_ref),
        (mask_ref, masks_ref),
        (lag_ref, lags_ref),
    )
    fetched = [pltpu.make_async_copy(src, dst, own_sems.at[i]) for i, (src, dst) in enumerate(pairs)]
    for move in fetched:
        move.start()
    lane = lax.broadcasted_iota(jnp.int32, (filled, wide), 1)
    sample = lax.broadcasted_iota(jnp.int32, (filled, wide), 0)
    spread_ref[...] = jnp.where(lane // GROUP == sample, 1.0, 0.0).astype(jnp.bfloat16)
    own = lax.broadcasted_iota(jnp.int32, (channels, wide), 1) % GROUP == (
        lax.broadcasted_iota(jnp.int32, (channels, wide), 0) % GROUP
    )
    lag = (LAGS - 1 - lax.broadcasted_iota(jnp.int32, (LAGS, channels), 0)).astype(jnp.float32)

    fetched[0].wait()
    rims_ref[0] = pack(series_ref[:, :rim_len], rims_ref.shape[1])
    start_down()
    line0, lane0, per = code_place(channels, tmpl_len)
    for move in fetched[1:]:
        move.wait()
    packed = pack(kernel_ref[...], packed_rows(channels, tmpl_len, 1))
    slots_ref[0, : packed.shape[0]] = packed
    code = jnp.where(masks_ref[...] != 0, lags_ref[...], -1).astype(jnp.float32)
    line = packed[line0:] if line0 < packed.shape[0] else jnp.zeros((ROWS, LANES), packed.dtype)
    line = put_codes(code, line.astype(jnp.float32), lane0, per)
    slots_ref[0, line0 : line0 + ROWS] = line.astype(packed.dtype)

    def expand(n, slot):
        kernel = unpack(slots_ref[n], channels, tmpl_len)
        widened = jnp.dot(kernel, spread_ref[...], preferred_element_type=jnp.float32)
        as_float = kernel.astype(jnp.float32)
        mean = jnp.sum(as_float * as_float, axis=1, keepdims=True) / tmpl_len
        weight = 1.0 / (jnp.sqrt(mean + 1e-05) * tmpl_len)
        wide_ref[slot] = jnp.where(own, widened, 0.0)
        weight_ref[slot] = jnp.broadcast_to(weight, (channels, LANES))

    def scale():
        series_ref[:, slab_len:] = unpack(rims_ref[1], channels, rim_len)
        series = series_ref[...].astype(jnp.float32)
        squares = series * series
        high = squares.astype(jnp.bfloat16)
        low = (squares - high.astype(jnp.float32)).astype(jnp.bfloat16)
        both = jnp.concatenate([high, low], axis=0)
        row = lax.broadcasted_iota(jnp.int32, (BAND, BAND), 0)
        column = lax.broadcasted_iota(jnp.int32, (BAND, BAND), 1)
        bands = []
        for d in range((tmpl_len + BAND - 2) // BAND + 1):
            off = d * BAND + row - column
            bands.append(jnp.where((off >= 0) & (off < tmpl_len), 1.0, 0.0).astype(jnp.bfloat16))
        for n in range(-(-span // BAND)):
            total = None
            for d, band in enumerate(bands):
                part = both[:, (n + d) * BAND : (n + d + 1) * BAND]
                if part.shape[1] == 0:
                    continue
                part = jnp.dot(part, band[: part.shape[1]], preferred_element_type=jnp.float32)
                total = part if total is None else total + part
            energy = total[:channels] + total[channels:]
            here = slice(n * BAND, min((n + 1) * BAND, span))
            inverse_ref[:, here] = lax.rsqrt(energy / tmpl_len + 1e-05)[:, : here.stop - here.start]

    def spread_out(begin, end):
        reads = min(end + LANES, series_ref.shape[1])
        if end + STEP - 1 <= slab_len:
            reads = min(reads, slab_len)

        @pl.loop(0, channels // ROWS, unroll=unroll_of(channels // ROWS, 5))
        def _(pair):
            rows = pl.ds(pl.multiple_of(pair * ROWS, ROWS), ROWS)
            series = series_ref[rows, begin:reads].astype(jnp.float32)
            for side in range(ROWS // GROUP):
                part = series[side * GROUP : (side + 1) * GROUP]
                moved_ref[pair * (ROWS // GROUP) + side, :, begin:end] = jnp.concatenate(
                    [shifted_left(part, b)[:, : end - begin] for b in range(STEP)], axis=0
                ).astype(jnp.bfloat16)

    def traces(batch):
        @pl.loop(0, channels // GROUP, unroll=unroll_of(channels // GROUP, 20))
        def _(group):
            rows = pl.ds(pl.multiple_of(group * GROUP, GROUP), GROUP)
            left = jnp.concatenate(
                [wide_ref[n, rows, a * deep : (a + 1) * deep] for n in range(batch) for a in range(blocks)],
                axis=0,
            ).astype(jnp.bfloat16)
            partial = jnp.dot(left, moved_ref[group], preferred_element_type=jnp.float32)
            inverse_rms = inverse_ref[rows, :]
            for n in range(batch):
                total = None
                for phase in range(min(per_tile, blocks)):
                    lined = None
                    for a in range(phase, blocks, per_tile):
                        begin = (a - phase) * STEP
                        line = (n * blocks + a) * GROUP
                        piece = partial[line : line + GROUP, begin : begin + span + LANES]
                        if piece.shape[1] < span + LANES:
                            missing = span + LANES - piece.shape[1]
                            piece = jnp.concatenate(
                                [piece, jnp.zeros((GROUP, missing), jnp.float32)], axis=1
                            )
                        lined = piece if lined is None else lined + piece
                    lined = shifted_left(lined, phase * STEP)[:, :span]
                    total = lined if total is None else total + lined
                weight = jnp.concatenate([weight_ref[n, rows, :]] * (span // LANES), axis=1)
                trace_ref[n, rows, :] = total * inverse_rms * weight

    def stack(n, slot):
        line = slots_ref[n, line0 : line0 + ROWS].astype(jnp.float32)
        pick = jnp.where(get_codes(line, channels, lane0, per) == lag, 1.0, 0.0).astype(jnp.bfloat16)
        trace = trace_ref[slot]
        high = trace.astype(jnp.bfloat16)
        low = (trace - high.astype(jnp.float32)).astype(jnp.bfloat16)
        by_lag = jnp.dot(pick, high, preferred_element_type=jnp.float32)
        by_lag += jnp.dot(pick, low, preferred_element_type=jnp.float32)
        lined = pltpu.roll(by_lag, span - LAGS + 1, 1, stride=1, stride_axis=0)
        out_ref[(me + size - n) % size] = jnp.sum(lined, axis=0, keepdims=True)[:, :slab_len]

    def rows_of(first, batch):
        for n in range(batch):
            expand(first + n, n)
        traces(batch)
        for n in range(batch):
            stack(first + n, n)

    batch = min(BATCH, size)
    if batch == size:
        expand(0, 0)
    pl.when((col % 2 == 0) | (me == size - 2))(start_back)
    ready = (slab_len - STEP + 1) // LANES * LANES
    if ready:
        spread_out(0, ready)
    pl.when((col % 2 == 1) & (me != size - 2))(start_back)
    start_up()
    land_rim()
    scale()
    spread_out(ready, reach)
    if batch == size:
        turned = jnp.where(me == 0, size - 2, 0)
        order = [0] + [lax.rem(turned + d - 1, size - 1) + 1 for d in range(1, size)]

        def in_turn(cuts):
            for begin, end in zip(cuts[:-1], cuts[1:]):
                for i in range(max(begin, 1), end):
                    land_row(order[i])
                    expand(order[i], i - begin)
                traces(end - begin)
                for i in range(begin, end):
                    stack(order[i], i - begin)

        if size > 2:
            pl.when(col % 2 == 0)(lambda: in_turn([0, 2, size]))
            pl.when(col % 2 == 1)(lambda: in_turn([0, size]))
        else:
            in_turn([0, size])
    else:
        for d in range(1, size):
            land_row(d)

        @pl.loop(0, size // batch)
        def _(turn):
            rows_of(turn * batch, batch)

        if size % batch:
            rows_of(size - size % batch, size % batch)
    drain()


def local(records, templates, channel_mask, lag_table):
    channels, slab_len = records.shape
    first, second, tmpl_len = templates.shape[1:]
    assert first == 1 and second == 1
    size = lax.axis_size("tm")
    span = up(slab_len + LAGS - 1, LANES)
    blocks = -(-tmpl_len // STEP)
    wide = blocks * STEP * GROUP
    reach = up(slab_len + LAGS - 1 + (blocks - 1) * STEP, LANES)
    lines = max(packed_rows(channels, tmpl_len, 1), code_place(channels, tmpl_len)[0] + ROWS)
    dma = pltpu.SemaphoreType.DMA
    hbm, vmem = pl.BlockSpec(memory_space=pltpu.HBM), pl.BlockSpec(memory_space=pltpu.VMEM)
    out = pl.pallas_call(
        correlate,
        out_shape=pltpu.VMEM((size, 1, slab_len), jnp.float32),
        in_specs=[hbm] * 4,
        out_specs=vmem,
        scratch_shapes=[
            pltpu.VMEM((channels, tmpl_len), jnp.bfloat16),
            pltpu.VMEM((1, channels), jnp.int32),
            pltpu.VMEM((1, channels), jnp.int32),
            pltpu.VMEM((channels, slab_len + up(rim_columns(tmpl_len), LANES)), jnp.bfloat16),
            pltpu.VMEM((2, packed_rows(channels, rim_columns(tmpl_len), 2), LANES), jnp.bfloat16),
            pltpu.VMEM((size, lines, LANES), jnp.bfloat16),
            pltpu.VMEM((BATCH, channels, wide), jnp.float32),
            pltpu.VMEM((BATCH, channels, span), jnp.float32),
            pltpu.VMEM((BATCH, channels, LANES), jnp.float32),
            pltpu.VMEM((up(tmpl_len, LANES), wide), jnp.bfloat16),
            pltpu.VMEM((channels // GROUP, STEP * GROUP, reach), jnp.bfloat16),
            pltpu.VMEM((channels, span), jnp.float32),
            dma((4,)),
            dma((2,)),
            dma((2,)),
            dma((size,)),
            dma((size,)),
        ],
        compiler_params=pltpu.CompilerParams(
            vmem_limit_bytes=62 << 20, collective_id=0, has_side_effects=True
        ),
    )(
        records,
        templates.reshape(channels, tmpl_len),
        channel_mask.reshape(1, channels),
        lag_table.reshape(1, channels),
    )
    return out


def solution(mesh):
    return jax.shard_map(
        local,
        mesh=mesh,
        in_specs=(
            P(None, ("grp", "tm")),
            P(None, "tm", "tmpl", None),
            P(None, "tm", "tmpl"),
            P(None, "tm", "tmpl"),
        ),
        out_specs=P(None, "tmpl", ("grp", "tm")),
        check_vma=False,
    )
```
